32 devices in a mesh: groups: 2 (over y), dp: 4 (over z), mp: 4 (over x, core).
Axes of the slice: x: 2, y: 2, z: 4, core: 2. Of those that a mesh axis runs over, the one named last changes fastest.
Arguments:
- qkv_home: bfloat16 [8, 764, 3, 3072], P(('groups', 'dp'), None, None, 'mp'), parts along dimension 0, may hold values from -6 to 6
- resid_home: bfloat16 [8, 764, 6144], P(('groups', 'dp'), None, 'mp'), parts along dimension 0, may hold values from -6 to 6
- out_weight: bfloat16 [3072, 6144], P('dp', 'mp'), may hold values from -0.109375 to 0.109375
- label_weight: bfloat16 [6144, 12288], P('mp', 'dp'), may hold values from -0.21875 to 0.21875
- label_bias: float32 [12288], P('dp'), may hold values from -5 to 5
- query_gain: float32 [128], replicated, may hold values from 0.25 to 1.75
- key_gain: float32 [128], replicated, may hold values from 0.25 to 1.75
- patch_counts: int32 [8, 4], P('groups'), parts along dimension 0, may hold values from 1 to 191, as said below
- move_plan: int32 [8, 4], P('groups'), parts along dimension 0, may hold values from 0 to 3, as said below
- segment_ids: int32 [8, 764], P(('groups', 'dp')), parts along dimension 0, may hold values from 0 to 4, as said below
Outputs:
- mixed: bfloat16 [8, 384, 6144], P(('groups', 'dp'), None, 'mp'), parts along dimension 0
- labels: float32 [8, 4, 12288], P(('groups', 'dp'), 'mp'), parts along dimension 0
The draws below stay inside these ranges and needn't reach their ends.
There are 2 independent parts, one for each index of `groups`. The reference program is written for one: setup_inputs(seed, part) draws one part's arguments, and reference() takes and returns one part's arrays. A program takes and returns all parts, laid end to end along the dimension named above; an argument that names none is the same for every part. Nothing has to cross between parts.
Inputs may be any that keep to these rules, and one draw needn't show every extreme that they name: `patch_counts`: home row r holds its 4 images packed in the order j; every destination row receives exactly one image from every home row, 384 patches in all; every draw holds an image of 191 patches. Every row of move_plan is a permutation, and every destination row appears once in every column, so each destination receives one image from each home row. `segment_ids`: image j of home row r has id j on its patch_counts[r, j] slots, which follow those of image j - 1; slots after the last image have id 4.
All inputs are finite; a program needn't handle non-finite values.
Results may differ from the reference program's by a relative error of at most 0.0065.
Values may be sent and summed in bfloat16 or wider, within the bound.
A program may use at most 64 MiB of HBM per device.

```python
import math
import jax
import jax.numpy as jnp
from jax import lax

D = 6144
HD = 128
HEADS = 24
CLASSES = 12288
TOK = 384
ROWS = 4
MEAN = 96
HOME = 764


def draw_layout(key):
    base_key = jax.random.fold_in(key, 7)
    sub_keys = jax.random.split(base_key, 6)
    row_ids = jnp.arange(ROWS, dtype=jnp.int32)
    col_shift = jax.random.permutation(sub_keys[0], ROWS).astype(jnp.int32)
    row_shift = jax.random.permutation(sub_keys[1], ROWS).astype(jnp.int32)
    move_plan = (col_shift[None, :] + row_shift[:, None]) % ROWS
    pairing = jax.random.permutation(sub_keys[2], ROWS).astype(jnp.int32)
    centers = jax.random.randint(sub_keys[3], (ROWS // 2, 1), 1, 2 * MEAN)
    jitter = jax.random.randint(sub_keys[4], (ROWS // 2, ROWS), -(MEAN // 2), MEAN // 2 + 1)
    heavy = jnp.clip(centers + jitter, 1, 2 * MEAN - 1)
    full_dest = jax.random.randint(sub_keys[5], (ROWS // 2, 1), 0, ROWS)
    heavy = jnp.where(row_ids[None, :] == full_dest, 2 * MEAN - 1, heavy).astype(jnp.int32)
    loads = jnp.zeros((ROWS, ROWS), jnp.int32)
    loads = loads.at[pairing[0::2]].set(heavy)
    loads = loads.at[pairing[1::2]].set(2 * MEAN - heavy)
    counts = jnp.take_along_axis(loads, move_plan, axis=1)
    image_ends = jnp.cumsum(counts, axis=1)
    slot_ids = jnp.arange(HOME, dtype=jnp.int32)
    segments = jnp.sum((slot_ids[None, :, None] >= image_ends[:, None, :]).astype(jnp.int32), axis=2)
    return (counts.astype(jnp.int32), move_plan.astype(jnp.int32), segments.astype(jnp.int32))


def draw_patch_counts(key, part):
    return draw_layout(key)[0]


def draw_move_plan(key, part):
    return draw_layout(key)[1]


def draw_segment_ids(key, part):
    return draw_layout(key)[2]


def steps_of(own_key, dims, cuts, low, largest):
    factor_of, own = 1.0, jax.random.fold_in(own_key, 6)
    for axis_at, parts in cuts:
        heights = jnp.exp(jax.random.uniform(jax.random.fold_in(own, axis_at), (parts,), jnp.float32, low / len(cuts), largest / len(cuts)))
        factor_of = factor_of * jnp.repeat(heights, dims[axis_at] // parts).reshape([-1 if axis == axis_at else 1 for axis in range(len(dims))])
    return factor_of


def centred(rng, shape, width, bound, cuts=(), held_as=jnp.bfloat16):
    factor_of = steps_of(rng, shape, cuts, -0.22, 0.18) if cuts else 1.0
    result = jax.random.normal(rng, shape, jnp.float32) * width * factor_of
    return jnp.minimum(jnp.maximum(result, -bound), bound).astype(held_as)


def setup_inputs(seed: int = 0, part: int = 0) -> dict:
    key_of = jax.random.split(jax.random.key(seed), 11)
    part_keys = jax.random.split(jax.random.fold_in(key_of[10], part), 11)
    return {
        "qkv_home": centred(part_keys[0], (ROWS, HOME, 3, HEADS * HD), 1.0, 6.0, ((0, 4), (3, 4))),
        "resid_home": centred(part_keys[1], (ROWS, HOME, D), 1.0, 6.0, ((0, 4), (2, 4))),
        "out_weight": centred(key_of[2], (HEADS * HD, D), (HEADS * HD) ** -0.5, 0.109375, ((0, 4), (1, 4))),
        "label_weight": centred(key_of[3], (D, CLASSES), (D // 8) ** -0.5, 0.21875, ((0, 4), (1, 4))),
        "label_bias": centred(key_of[4], (CLASSES,), 1.0, 5.0, ((0, 4),), jnp.float32),
        "query_gain": jnp.clip(1.0 + 0.15 * jax.random.normal(key_of[5], (HD,), jnp.float32), 0.25, 1.75),
        "key_gain": jnp.clip(1.0 + 0.15 * jax.random.normal(key_of[6], (HD,), jnp.float32), 0.25, 1.75),
        "patch_counts": draw_patch_counts(jax.random.fold_in(jax.random.fold_in(key_of[10], part), 71), part),
        "move_plan": draw_move_plan(jax.random.fold_in(jax.random.fold_in(key_of[10], part), 71), part),
        "segment_ids": draw_segment_ids(jax.random.fold_in(jax.random.fold_in(key_of[10], part), 71), part),
    }


EPSILON = 1e-06

def head_norm(values, norm_gain):
    center = values - lax.optimization_barrier(jnp.mean(values, axis=-1, keepdims=True))
    spread = lax.optimization_barrier(jnp.mean(center * center, axis=-1, keepdims=True))
    return center * lax.rsqrt(spread + EPSILON) * norm_gain

def rounded(values):
    return lax.optimization_barrier(values.astype(jnp.bfloat16)).astype(jnp.float32)

def attend(qkv_rows, seg_rows, query_gain, key_gain):
    length = qkv_rows.shape[0]
    head_count = qkv_rows.shape[2] // HD
    split_parts = qkv_rows.astype(jnp.float32).reshape(length, 3, head_count, HD)
    queries = rounded(head_norm(split_parts[:, 0], query_gain))
    key_rows = rounded(head_norm(split_parts[:, 1], key_gain))
    scores = jnp.einsum('qhd,khd->hqk', queries, key_rows) / math.sqrt(HD)
    same_image = (seg_rows[:, None] == seg_rows[None, :]).astype(jnp.float32)
    raised = jnp.exp(scores) * same_image[None]
    weights = rounded(raised / lax.optimization_barrier(jnp.sum(raised, axis=-1, keepdims=True)))
    head_out = jnp.einsum('hqk,khd->qhd', weights, split_parts[:, 2])
    return head_out.reshape(length, head_count * HD).astype(jnp.bfloat16)

def reference(qkv_home, resid_home, out_weight, label_weight, label_bias, query_gain, key_gain, patch_counts, move_plan, segment_ids):
    row_count = patch_counts.shape[0]
    home_slots = qkv_home.shape[1]
    image_ids = jnp.arange(row_count, dtype=jnp.int32)

    def one_row(entry):
        qkv_rows, resid_rows, seg_rows, count_row = entry
        heads_done = attend(qkv_rows, seg_rows, query_gain, key_gain)
        projected = jnp.dot(heads_done, out_weight, preferred_element_type=jnp.float32)
        row_mixed = (resid_rows.astype(jnp.float32) + projected).astype(jnp.bfloat16)
        member = (image_ids[:, None] == seg_rows[None, :]).astype(jnp.bfloat16)
        image_sums = jnp.dot(member, row_mixed, preferred_element_type=jnp.float32)
        row_pooled = (image_sums / count_row[:, None].astype(jnp.float32)).astype(jnp.bfloat16)
        return (row_mixed, row_pooled)
    home_mixed, pooled = lax.map(one_row, (qkv_home, resid_home, segment_ids, patch_counts))
    logits = jnp.dot(pooled.reshape(row_count * row_count, -1), label_weight, preferred_element_type=jnp.float32)
    logits = logits + label_bias.astype(jnp.float32)[None, :]
    labels = jax.nn.sigmoid(logits).reshape(row_count, row_count, -1)
    image_ends = jnp.cumsum(patch_counts, axis=1)
    starts = image_ends - patch_counts
    matches = (move_plan[:, :, None] == image_ids[None, None, :]).astype(jnp.int32)
    image_sizes = lax.optimization_barrier(jnp.sum(patch_counts[:, :, None] * matches, axis=1))
    firsts = lax.optimization_barrier(jnp.sum(starts[:, :, None] * matches, axis=1))
    column_ends = jnp.cumsum(image_sizes, axis=0)
    column_starts = column_ends - image_sizes
    slot_ids = jnp.arange(TOK, dtype=jnp.int32)
    source = lax.optimization_barrier(jnp.sum((slot_ids[None, :, None] >= column_ends.T[:, None, :]).astype(jnp.int32), axis=2))
    chosen = (source[:, :, None] == image_ids[None, None, :]).astype(jnp.int32)
    shift_by = lax.optimization_barrier(jnp.sum(chosen * (firsts.T[:, None, :] - column_starts.T[:, None, :]), axis=2))
    flat_index = (source * home_slots + shift_by + slot_ids[None, :]).astype(jnp.int32)
    mixed = jnp.take(home_mixed.reshape(row_count * home_slots, -1), flat_index.reshape(-1), axis=0)
    mixed = mixed.reshape(row_count, TOK, -1)
    return (mixed, labels)
```

```python
import functools
import math

import jax
import jax.numpy as jnp
from jax import lax
from jax.experimental import pallas as pl
from jax.experimental.pallas import tpu as pltpu
from jax.sharding import PartitionSpec as P

TOK = 384


EPSILON = 1e-06


def head_norm(values, norm_gain):
    center = values - jnp.mean(values, axis=-1, keepdims=True)
    spread = jnp.mean(center * center, axis=-1, keepdims=True)
    return center * lax.rsqrt(spread + EPSILON) * norm_gain


def attend(qkv_rows, seg_rows, query_gain, key_gain):
    length = qkv_rows.shape[0]
    head_width = query_gain.shape[0]
    head_count = qkv_rows.shape[2] // head_width
    split_parts = qkv_rows.reshape(length, 3, head_count, head_width)
    queries = head_norm(split_parts[:, 0].astype(jnp.float32), query_gain).astype(jnp.bfloat16)
    key_rows = head_norm(split_parts[:, 1].astype(jnp.float32), key_gain).astype(jnp.bfloat16)
    scores = jnp.einsum(
        "qhd,khd->hqk", queries, key_rows, preferred_element_type=jnp.float32
    ) / math.sqrt(head_width)
    same_image = seg_rows[:, None] == seg_rows[None, :]
    raised = jnp.where(same_image[None], jnp.exp(scores), 0.0)
    weights = (raised / jnp.sum(raised, axis=-1, keepdims=True)).astype(jnp.bfloat16)
    head_out = jnp.einsum(
        "hqk,khd->qhd", weights, split_parts[:, 2], preferred_element_type=jnp.float32
    )
    return head_out.reshape(length, head_count * head_width).astype(jnp.bfloat16)


def project(heads_local, resid_rows, out_weight):
    gathered = lax.all_gather(heads_local, "mp", axis=1, tiled=True)
    running = resid_rows.astype(jnp.float32) + jnp.dot(
        gathered,
        lax.all_gather(out_weight, "dp", axis=0, tiled=True),
        preferred_element_type=jnp.float32,
    )
    return running.astype(jnp.bfloat16)


def pool(row_mixed, seg_rows, count_row):
    images = count_row.shape[0]
    member_ids = lax.broadcasted_iota(jnp.int32, (images, seg_rows.shape[0]), 0)
    member = (member_ids == seg_rows[None, :]).astype(jnp.bfloat16)
    image_sums = jnp.dot(member, row_mixed, preferred_element_type=jnp.float32)
    return (image_sums / count_row[:, None].astype(jnp.float32)).astype(jnp.bfloat16)


def label_terms(pooled, label_weight):
    return jnp.einsum(
        "abd,dc->abc",
        lax.all_gather(pooled[None], "dp", axis=0, tiled=True),
        label_weight,
        preferred_element_type=jnp.float32,
    )


def pick(values, row_index, is_valid):
    taken = jnp.take(values, row_index, axis=0)
    taken = taken.reshape(is_valid.shape + values.shape[1:])
    keep_mask = is_valid.reshape(is_valid.shape + (1,) * (values.ndim - 1))
    return jnp.where(keep_mask, taken, jnp.zeros_like(taken))


MESH = pl.DeviceIdType.MESH
LANES = 128
TILE = 256
WINDOW = 256
EXTRA = 16


def remote(src, dst, send_sem, recv_sem, where):
    return pltpu.make_async_remote_copy(
        src_ref=src,
        dst_ref=dst,
        send_sem=send_sem,
        recv_sem=recv_sem,
        device_id=where,
        device_id_type=MESH,
    )


def normed(values, gain):
    values = values.astype(jnp.float32)
    center = values - jnp.mean(values, axis=-1, keepdims=True)
    spread = jnp.mean(center * center, axis=-1, keepdims=True)
    return (center * lax.rsqrt(spread + EPSILON) * gain).astype(jnp.bfloat16)


def block_kernel(
    sizes,
    counts,
    plan,
    bias_ref,
    qg_ref,
    kg_ref,
    qkv_hbm,
    resid_hbm,
    w_hbm,
    lw_hbm,
    out_ref,
    lab_ref,
    raw,
    blk,
    hx,
    gath,
    relay,
    wall,
    resv,
    end_qkv,
    end_resid,
    zall,
    places,
    ssend,
    srecv,
    tbuf,
    fsend,
    ppall,
    poo,
    poorecv,
    lwv,
    lgs,
    lrecv,
    pbuf,
    precv,
    load_sem,
    os,
    orr,
    cs,
    rr,
    ins,
    cr,
    wzs,
    wzr,
    wys,
    wyr,
    xs,
    xr,
    ss,
    sr,
    fs,
    fr,
    pps,
    ppr,
    pos,
    por,
    ls,
    lr,
    bs,
    br,
):
    rows, slots, pair = sizes
    z = lax.axis_index("dp")
    mp = lax.axis_index("mp")
    group = lax.axis_index("groups")
    other = 1 - group
    core = lax.rem(mp, 2)
    xpos = mp // 2
    near = mp + 1 - 2 * core
    side = lax.rem(mp + 2, 4)
    half_id = z // 2
    member_id = z - 2 * half_id
    zo = 3 * half_id
    zp = 1 + half_id
    zq = 2 - half_id
    zo2 = 3 - 3 * half_id
    inner = z == zp
    outer = z == zo
    partner = zo + zp - z
    keeps = xpos == half_id
    crosses = xpos != half_id
    order_a = [zo2, zq, zo, zp]
    order_c = [zo, zp, zo2, zq]
    homes = [z, zq, zo2]
    width = raw.shape[2]
    split = width // 2
    depth, cols = w_hbm.shape
    tiles = cols // TILE
    images = rows
    two = 2 * pair
    tokens = out_ref.shape[0]
    bf16, f32 = jnp.bfloat16, jnp.float32

    loads = [
        pltpu.make_async_copy(qkv_hbm, raw, load_sem.at[0]),
        pltpu.make_async_copy(w_hbm, wall.at[member_id], load_sem.at[1]),
        pltpu.make_async_copy(resid_hbm, resv, load_sem.at[2]),
        pltpu.make_async_copy(lw_hbm, lwv, load_sem.at[3]),
    ]
    for load in loads:
        load.start()

    barrier = pltpu.get_barrier_semaphore()
    for k in range(1, 4):
        pl.semaphore_signal(
            barrier, inc=1, device_id={"mp": lax.rem(mp + k, 4)}, device_id_type=MESH
        )
    for k in range(1, rows):
        pl.semaphore_signal(
            barrier, inc=1, device_id={"dp": lax.rem(z + k, rows)}, device_id_type=MESH
        )
    pl.semaphore_signal(barrier, inc=1, device_id={"groups": other}, device_id_type=MESH)
    pl.semaphore_wait(barrier, 3 + rows - 1 + 1)

    def tile_at(t):
        return pl.ds(pl.multiple_of(t * TILE, TILE), TILE)

    def block_at(index):
        return pl.ds(pl.multiple_of(index * pair, pair), pair)

    def repeat(count, body):
        def step(t, carry):
            body(t)
            return carry

        lax.fori_loop(0, count, step, 0)

    def weight_part(which, part, t):
        size = depth // 2
        return wall.at[which, pl.ds(pl.multiple_of(part * size, size), size), tile_at(t)]

    def wzcopy(t):
        size = depth // 2
        own = w_hbm.at[pl.ds(pl.multiple_of(group * size, size), size), tile_at(t)]
        return remote(
            own, weight_part(member_id, group, t), wzs.at[t], wzr.at[t], {"dp": partner}
        )

    def wycopy(t):
        part = weight_part(1 - member_id, group, t)
        return remote(part, part, wys.at[t], wyr.at[t], {"groups": other})

    def forward_weight(t):
        part = weight_part(1 - member_id, group, t)
        remote(part, part, wys.at[t], wzr.at[t], {"groups": other}).wait_recv()
        wycopy(t).start()

    def wait_weight(t):
        part = weight_part(1 - member_id, other, t)
        remote(part, part, wys.at[t], wyr.at[t], {"groups": other}).wait_recv()

    repeat(tiles, lambda t: wzcopy(t).start())

    def gathered(which, home, dest):
        first = home * two + lax.rem(dest, 2) * pair
        return which, dest // 2, pl.ds(pl.multiple_of(first, pair), pair)

    def own_piece(which, k):
        kb, e, at = gathered(which, 0, order_a[k])
        return gath.at[kb, e, at, :]

    def own_near(k):
        part = own_piece(core, k)
        return remote(part, part, os.at[k, 0], orr.at[k, 0], {"mp": near})

    def own_side(k):
        part = own_piece(core, k)
        return remote(part, part, os.at[k, 1], orr.at[k, 1], {"mp": side})

    def own_wait(kind, k):
        part = own_piece(core if kind else 1 - core, k)
        remote(part, part, os.at[k, kind], orr.at[k, kind], {"mp": near}).wait_recv()

    def half_at(which):
        return pl.ds(pl.multiple_of(which * split, LANES), split)

    there = jnp.where(outer, 2, 1)

    def cross_low(k):
        dest = order_c[k]
        kb, e, at = gathered(core, there, dest)
        return remote(
            hx.at[block_at(dest), pl.ds(0, split)],
            gath.at[kb, e, at, pl.ds(0, split)],
            cs.at[k, 0],
            cr.at[there - 1, k, 0],
            {"dp": zq},
        )

    def cross_side(k):
        dest = order_c[k]
        return remote(
            hx.at[block_at(dest), pl.ds(split, split)],
            relay.at[k],
            cs.at[k, 1],
            rr.at[k],
            {"mp": side},
        )

    def cross_high(k):
        kb, e, at = gathered(core, there, order_c[k])
        return remote(
            relay.at[k],
            gath.at[kb, e, at, pl.ds(split, split)],
            cs.at[k, 0],
            cr.at[there - 1, k, 0],
            {"dp": zq},
        )

    mine = jnp.where(keeps, 0, 1)

    def cross_piece(h, k, which, part):
        kb, e, at = gathered(which, h + 1, order_a[k])
        return gath.at[kb, e, at, half_at(part)]

    def cross_copy(h, k, kind):
        part = cross_piece(h, k, core, 1 - mine if kind == 2 else mine)
        target = side if kind == 1 else near
        return remote(part, part, ins.at[h, k, kind], cr.at[h, k, kind + 1], {"mp": target})

    def cross_wait(h, k, kind):
        which = core if kind in (0, 2) else 1 - core
        part = cross_piece(h, k, which, mine if kind < 2 else 1 - mine)
        remote(part, part, ins.at[h, k, 0], cr.at[h, k, kind], {"mp": near}).wait_recv()

    def serve_home(k):
        @pl.when(keeps)
        def _():
            remote(
                relay.at[k], relay.at[k], cs.at[k, 1], rr.at[k], {"mp": side}
            ).wait_recv()
            cross_high(k).start()

        @pl.when(crosses)
        def _():
            own_wait(1, k)
            own_near(k).start()

    own_counts = [counts[z, j] for j in range(images)]
    own_plan = [plan[z, j] for j in range(images)]
    own_starts, running = [], 0
    for j in range(images):
        own_starts.append(running)
        running = running + own_counts[j]

    def span_of(dest):
        first, count = 0, 0
        for j in range(images):
            hit = (own_plan[j] == dest).astype(jnp.int32)
            first = first + hit * own_starts[j]
            count = count + hit * own_counts[j]
        return first, count

    pick_row = lax.broadcasted_iota(jnp.int32, (pair, 1), 0)
    pick_col = lax.broadcasted_iota(jnp.int32, (1, WINDOW), 1)
    base = slots // 16 * 16
    rest = slots - base

    def picker(dest):
        first, count = span_of(dest)
        low = lax.min(lax.div(first, 16), (base - WINDOW) // 16) * 16
        valid = pick_row < count
        chosen = jnp.logical_and(pick_col == pick_row + (first - low), valid).astype(bf16)
        ends = jnp.logical_and(pick_col[:, :16] == pick_row + (first - base), valid).astype(bf16)
        return pl.ds(low, WINDOW), chosen, ends, count

    def moved_rows(chosen, ends, body, end):
        part = jnp.dot(chosen, body, preferred_element_type=f32)
        return part + jnp.dot(ends, end, preferred_element_type=f32)

    heads = width // LANES
    q_gain = qg_ref[...]
    k_gain = kg_ref[...]
    scale = math.log2(math.e) / math.sqrt(LANES)
    key_at = lax.broadcasted_iota(jnp.int32, (1, pair), 1)

    loads[0].wait()
    end_qkv[...] = jnp.zeros(end_qkv.shape, bf16)
    if rest:
        end_qkv[:, pl.ds(0, rest), :] = raw[:, pl.ds(base, rest), :]

    def attend_block(dest):
        at_rows, chosen, ends, count = picker(dest)
        for part in range(3):
            blk[part] = moved_rows(
                chosen, ends, raw[part, at_rows, :], end_qkv[part]
            ).astype(bf16)
        seen = key_at < count

        def one_head(h):
            at = pl.ds(pl.multiple_of(h * LANES, LANES), LANES)
            scores = lax.dot_general(
                normed(blk[0, :, at], q_gain),
                normed(blk[1, :, at], k_gain),
                (((1,), (1,)), ((), ())),
                preferred_element_type=f32,
            )
            raised = jnp.where(seen, jnp.exp2(scores * scale), 0.0)
            total = jnp.sum(raised, axis=-1, keepdims=True)
            weights = (raised * (1.0 / total)).astype(bf16)
            result = jnp.dot(weights, blk[2, :, at], preferred_element_type=f32)
            hx[block_at(dest), at] = result.astype(bf16)

        repeat(heads, one_head)

    for k in range(rows):
        dest = jnp.where(keeps, order_a[k], order_c[k])
        attend_block(dest)

        @pl.when(keeps)
        def _(k=k):
            kb, e, at = gathered(core, 0, order_a[k])
            gath[kb, e, at, :] = hx[block_at(order_a[k]), :]
            own_side(k).start()
            own_near(k).start()

        @pl.when(crosses)
        def _(k=k):
            cross_side(k).start()
            cross_low(k).start()

        if k:
            serve_home(k - 1)
    serve_home(rows - 1)

    loads[2].wait()
    end_resid[...] = jnp.zeros(end_resid.shape, bf16)
    if rest:
        end_resid[pl.ds(0, rest), :] = resv[pl.ds(base, rest), :]

    place_row = lax.broadcasted_iota(jnp.int32, (tokens + EXTRA, 1), 0)
    place_col = lax.broadcasted_iota(jnp.int32, (1, rows * pair), 1)

    def build_place(k):
        dest = order_a[k]
        begin = 0
        target = jnp.zeros(place_col.shape, jnp.int32)
        marker = jnp.zeros(place_col.shape, jnp.int32)
        limit = jnp.zeros(place_col.shape, jnp.int32)
        for r in range(rows):
            count = 0
            for j in range(images):
                count = count + (plan[r, j] == dest).astype(jnp.int32) * counts[r, j]
            here = place_col >= r * pair
            target = jnp.where(here, place_col + (begin - r * pair), target)
            marker = jnp.where(here, tokens + r, marker)
            limit = jnp.where(here, r * pair + count, limit)
            begin = begin + count
        target = jnp.where(place_col < limit, target, -1)
        marker = jnp.where(place_col < limit, marker, -1)
        hit = jnp.logical_or(place_row == target, place_row == marker)
        places[k] = hit.astype(bf16)

    zero_block = jnp.zeros((pair, cols), bf16)

    @pl.when(inner)
    def _():
        zall[zo, block_at(zo), :] = zero_block
        for k in range(rows):
            build_place(k)

    @pl.when(outer)
    def _():
        for r in range(1, rows):
            zall[zo, block_at(lax.rem(z + r, rows)), :] = zero_block
        build_place(2)

    for k in range(rows):
        dest = order_a[k]
        at_rows, chosen, ends, _ = picker(dest)

        def move_resid(t, dest=dest, at_rows=at_rows, chosen=chosen, ends=ends):
            part = moved_rows(
                chosen, ends, resv[at_rows, tile_at(t)], end_resid[:, tile_at(t)]
            )
            zall[dest, block_at(z), tile_at(t)] = part.astype(bf16)

        repeat(tiles, move_resid)

    loads[1].wait()

    def project(e, t, count):
        wait = pl.ds(0, count * two)
        acc = jnp.dot(gath[0, e, wait, :], wall[0, :, tile_at(t)], preferred_element_type=f32)
        acc = acc + jnp.dot(
            gath[1, e, wait, :], wall[1, :, tile_at(t)], preferred_element_type=f32
        )
        for h in range(count):
            for d in range(2):
                low = h * two + d * pair
                term = acc[low : low + pair]
                where = (2 * e + d, block_at(homes[h]), tile_at(t))
                if h == 0:
                    term = term + zall[where].astype(f32)
                zall[where] = term.astype(bf16)

    def arrange(k, t):
        return jnp.dot(
            places[k], zall[order_a[k], :, tile_at(t)], preferred_element_type=f32
        )

    index = jnp.where(inner, zp - 1, 0)

    def xcopy(k, t):
        dest = [zo2, zq, zp][k]
        part = zall.at[dest, block_at(zo), tile_at(t)]
        return remote(part, part, xs.at[k, t], xr.at[k, t], {"dp": zp})

    def xwait(k, t):
        dest = [zo2, zq, zp][k]
        part = zall.at[dest, block_at(zo), tile_at(t)]
        remote(part, part, xs.at[k, t], xr.at[k, t], {"dp": zo}).wait_recv()

    def scopy(k, t):
        return remote(
            ssend.at[k, :, tile_at(t)],
            srecv.at[k, :, tile_at(t)],
            ss.at[k, t],
            sr.at[k, t],
            {"dp": zq},
        )

    def fcopy(t):
        return remote(
            fsend.at[:, tile_at(t)], srecv.at[0, :, tile_at(t)], fs.at[t], fr.at[t], {"dp": zo}
        )

    def ppeer(k):
        return lax.rem(z + k, rows)

    def ppcopy(k, t):
        part = ppall.at[index, :, :, tile_at(t)]
        return remote(part, part, pps.at[k, t], ppr.at[index, t], {"dp": ppeer(k)})

    def ppwait(which, t):
        part = ppall.at[which, :, :, tile_at(t)]
        remote(part, part, pps.at[1, t], ppr.at[which, t], {"dp": ppeer(1)}).wait_recv()

    def pocopy():
        return remote(poo, poorecv, pos.at[0], por.at[0], {"dp": zp})

    far_pair, near_pair = 1 - half_id, half_id

    def wait_own(ks):
        for k in ks:
            own_wait(0, k)

    @pl.when(outer)
    def _():
        wait_own((0, 1))

        def far_tile(t):
            forward_weight(t)
            wait_weight(t)
            project(far_pair, t, 1)
            xcopy(0, t).start()

        repeat(tiles, far_tile)
        repeat(tiles, lambda t: xcopy(1, t).start())
        wait_own((2, 3))

        def near_tile(t):
            project(near_pair, t, 1)
            xcopy(2, t).start()
            moved = arrange(2, t)
            tbuf[0, :, tile_at(t)] = moved[:tokens]
            poo[:, tile_at(t)] = moved[tokens : tokens + 8]

        repeat(tiles, near_tile)
        pocopy().start()

        def last_tile(t):
            fcopy(t).wait_recv()
            value = tbuf[0, :, tile_at(t)] + srecv[0, :, tile_at(t)].astype(f32)
            out_ref[:, tile_at(t)] = value.astype(bf16)

        repeat(tiles, last_tile)

    @pl.when(inner)
    def _():
        def arrive(k):
            for h in range(2):
                cross_wait(h, k, 0)
                cross_copy(h, k, 1).start()
                cross_copy(h, k, 0).start()

        def spread(k):
            for h in range(2):
                cross_wait(h, k, 2)
                cross_copy(h, k, 2).start()

        def settle(k):
            own_wait(0, k)
            for h in range(2):
                cross_wait(h, k, 1)
                cross_wait(h, k, 3)

        forward_weight(0)
        arrive(0)
        forward_weight(1)
        arrive(1)
        spread(0)
        forward_weight(2)
        arrive(2)
        spread(1)
        forward_weight(3)
        arrive(3)
        spread(2)
        for t in range(4, tiles):
            forward_weight(t)
        spread(3)
        settle(0)
        settle(1)

        def send_sum(k, t):
            xwait(k, t)
            moved = arrange(k, t)
            ssend[k, :, tile_at(t)] = moved[:tokens].astype(bf16)
            ppall[index, order_a[k], :, tile_at(t)] = moved[tokens : tokens + 8]
            scopy(k, t).start()

        def far_tile(t):
            wait_weight(t)
            project(far_pair, t, 3)
            send_sum(0, t)

        repeat(tiles, far_tile)
        repeat(tiles, lambda t: send_sum(1, t))
        settle(2)
        settle(3)

        def near_tile(t):
            project(near_pair, t, 3)
            moved = arrange(2, t)
            tbuf[0, :, tile_at(t)] = moved[:tokens]
            ppall[index, zo, :, tile_at(t)] = moved[tokens : tokens + 8]

        repeat(tiles, near_tile)

        def return_tile(t):
            scopy(0, t).wait_recv()
            value = tbuf[0, :, tile_at(t)] + srecv[0, :, tile_at(t)].astype(f32)
            fsend[:, tile_at(t)] = value.astype(bf16)
            fcopy(t).start()

        repeat(tiles, return_tile)
        pocopy().wait_recv()

        def pool_tile(t):
            xwait(2, t)
            moved = arrange(3, t)
            tbuf[1, :, tile_at(t)] = moved[:tokens]
            ppall[index, zp, :, tile_at(t)] = moved[tokens : tokens + 8]
            ppall[index, zo, :, tile_at(t)] += poorecv[:, tile_at(t)]
            for k in range(1, rows):
                ppcopy(k, t).start()

        repeat(tiles, pool_tile)

    loads[3].wait()
    group_rows = lgs.shape[1]
    lines = images * group_rows
    line = lax.broadcasted_iota(jnp.int32, (lines, 1), 0)
    wanted = jnp.full((lines, 1), -1, jnp.int32)
    divisor = jnp.ones((lines, 1), f32)
    for r in range(rows):
        for d in range(rows):
            count = 0
            for j in range(images):
                count = count + (plan[r, j] == d).astype(jnp.int32) * counts[r, j]
            divisor = jnp.where(line == d * group_rows + r, count.astype(f32), divisor)
        for j in range(images):
            wanted = jnp.where(line == j * group_rows + r, plan[r, j] * group_rows + r, wanted)
    order = (lax.broadcasted_iota(jnp.int32, (lines, lines), 1) == wanted).astype(bf16)
    classes = lwv.shape[1]
    lgs[...] = jnp.zeros(lgs.shape, f32)

    def label_tile(t):
        @pl.when(inner)
        def _():
            ppwait(1 - index, t)

        @pl.when(outer)
        def _():
            ppwait(0, t)
            ppwait(1, t)

        sums = (ppall[0, :, :, tile_at(t)] + ppall[1, :, :, tile_at(t)]).reshape(lines, TILE)
        pooled = (sums / divisor).astype(bf16)
        by_image = jnp.dot(order, pooled, preferred_element_type=f32).astype(bf16)
        part = jnp.dot(by_image, lwv[tile_at(t), :], preferred_element_type=f32)
        lgs[...] += part.reshape(lgs.shape)

    repeat(tiles, label_tile)

    def lcopy(k):
        peer = lax.rem(mp + k, 4)
        return remote(lgs.at[peer], lrecv.at[k], ls.at[k], lr.at[k], {"mp": peer})

    for k in range(1, 4):
        lcopy(k).start()
    for k in range(1, 4):
        lcopy(k).wait_recv()
    total = lgs[mp]
    for k in range(1, 4):
        total = total + lrecv[k]
    probs = jax.nn.sigmoid(total + bias_ref[...])
    for r in range(rows):
        for t in range(classes // LANES):
            pbuf[r, pl.ds(t, 1), :] = probs[r : r + 1, t * LANES : (t + 1) * LANES]

    def bcopy(k):
        peer = ppeer(k)
        return remote(pbuf.at[peer], precv.at[z], bs.at[k], br.at[k], {"dp": peer})

    for k in range(1, rows):
        bcopy(k).start()

    @pl.when(inner)
    def _():
        def last_tile(t):
            scopy(1, t).wait_recv()
            value = tbuf[1, :, tile_at(t)] + srecv[1, :, tile_at(t)].astype(f32)
            out_ref[:, tile_at(t)] = value.astype(bf16)

        repeat(tiles, last_tile)

    for k in range(1, rows):
        part = precv.at[lax.rem(z + rows - k, rows)]
        remote(part, part, bs.at[k], br.at[k], {"dp": ppeer(k)}).wait_recv()
    precv[z] = pbuf[z]
    lab_ref[...] = precv[...]

    for k in range(rows):
        own_near(k).wait_send()

        @pl.when(keeps)
        def _(k=k):
            own_side(k).wait_send()
            cross_high(k).wait_send()

        @pl.when(crosses)
        def _(k=k):
            cross_low(k).wait_send()
            cross_side(k).wait_send()

        @pl.when(inner)
        def _(k=k):
            for h in range(2):
                for kind in range(3):
                    cross_copy(h, k, kind).wait_send()

    def close_tile(t):
        wzcopy(t).wait_send()
        wycopy(t).wait_send()

        @pl.when(outer)
        def _():
            for k in range(3):
                xcopy(k, t).wait_send()

        @pl.when(inner)
        def _():
            for k in range(2):
                scopy(k, t).wait_send()
            fcopy(t).wait_send()
            for k in range(1, rows):
                ppcopy(k, t).wait_send()

    repeat(tiles, close_tile)

    @pl.when(outer)
    def _():
        pocopy().wait_send()

    for k in range(1, rows):
        bcopy(k).wait_send()
    for k in range(1, 4):
        lcopy(k).wait_send()


def round_up(value, step):
    return -(-value // step) * step


def fused(
    qkv_home,
    resid_home,
    out_weight,
    label_weight,
    label_bias,
    query_gain,
    key_gain,
    patch_counts,
    move_plan,
):
    rows = lax.axis_size("dp")
    slots, width = qkv_home.shape[1], qkv_home.shape[3]
    depth, cols = out_weight.shape
    classes = label_weight.shape[1]
    pair = round_up(slots // rows, 16)
    tiles = cols // TILE
    bf16, f32 = jnp.bfloat16, jnp.float32
    vmem = pl.BlockSpec(memory_space=pltpu.VMEM)
    smem = pl.BlockSpec(memory_space=pltpu.SMEM)
    hbm = pl.BlockSpec(memory_space=pl.ANY)
    dma = pltpu.SemaphoreType.DMA
    mixed, labels = pl.pallas_call(
        functools.partial(block_kernel, (rows, slots, pair)),
        out_shape=(
            jax.ShapeDtypeStruct((TOK, cols), bf16),
            jax.ShapeDtypeStruct((rows, classes // LANES, LANES), f32),
        ),
        in_specs=[smem, smem, vmem, vmem, vmem, hbm, hbm, hbm, hbm],
        out_specs=(vmem, vmem),
        scratch_shapes=[
            pltpu.VMEM((3, slots, width), bf16),
            pltpu.VMEM((3, pair, width), bf16),
            pltpu.VMEM((rows * pair, width), bf16),
            pltpu.VMEM((2, 2, 6 * pair, width), bf16),
            pltpu.VMEM((rows, pair, width // 2), bf16),
            pltpu.VMEM((2, depth, cols), bf16),
            pltpu.VMEM((slots, cols), bf16),
            pltpu.VMEM((3, 16, width), bf16),
            pltpu.VMEM((16, cols), bf16),
            pltpu.VMEM((rows, rows * pair, cols), bf16),
            pltpu.VMEM((rows, TOK + EXTRA, rows * pair), bf16),
            pltpu.VMEM((2, TOK, cols), bf16),
            pltpu.VMEM((2, TOK, cols), bf16),
            pltpu.VMEM((2, TOK, cols), f32),
            pltpu.VMEM((TOK, cols), bf16),
            pltpu.VMEM((2, rows, 8, cols), f32),
            pltpu.VMEM((8, cols), f32),
            pltpu.VMEM((8, cols), f32),
            pltpu.VMEM(label_weight.shape, bf16),
            pltpu.VMEM((rows, 8, classes), f32),
            pltpu.VMEM((4, 8, classes), f32),
            pltpu.VMEM((rows, classes // LANES, LANES), f32),
            pltpu.VMEM((rows, classes // LANES, LANES), f32),
            dma((4,)),
            dma((rows, 2)),
            dma((rows, 2)),
            dma((rows, 2)),
            dma((rows,)),
            dma((2, rows, 3)),
            dma((2, rows, 4)),
            dma((tiles,)),
            dma((tiles,)),
            dma((tiles,)),
            dma((tiles,)),
            dma((3, tiles)),
            dma((3, tiles)),
            dma((2, tiles)),
            dma((2, tiles)),
            dma((tiles,)),
            dma((tiles,)),
            dma((rows, tiles)),
            dma((2, tiles)),
            dma((1,)),
            dma((1,)),
            dma((4,)),
            dma((4,)),
            dma((rows,)),
            dma((rows,)),
        ],
        compiler_params=pltpu.CompilerParams(
            collective_id=0, has_side_effects=True, vmem_limit_bytes=63 * 1024 * 1024
        ),
    )(
        patch_counts,
        move_plan,
        label_bias[None],
        query_gain[None],
        key_gain[None],
        jnp.transpose(qkv_home[0], (1, 0, 2)),
        resid_home[0],
        out_weight,
        label_weight,
    )
    return (mixed[None], labels.reshape(1, 1, rows * classes))


def on_device(
    qkv_home,
    resid_home,
    out_weight,
    label_weight,
    label_bias,
    query_gain,
    key_gain,
    patch_counts,
    move_plan,
    segment_ids,
):
    row_count = lax.axis_size("dp")
    if row_count == lax.axis_size("mp") == 4 and lax.axis_size("groups") == 2:
        return fused(
            qkv_home,
            resid_home,
            out_weight,
            label_weight,
            label_bias,
            query_gain,
            key_gain,
            patch_counts,
            move_plan,
        )
    my_index = lax.axis_index("dp")
    home_slots = segment_ids.shape[1]
    pair_slots = home_slots // row_count
    image_ids = lax.broadcasted_iota(jnp.int32, (row_count, row_count, row_count), 2)
    image_ends = jnp.cumsum(patch_counts, axis=1)
    starts = image_ends - patch_counts
    matches = (move_plan[:, :, None] == image_ids).astype(jnp.int32)
    image_sizes = jnp.sum(patch_counts[:, :, None] * matches, axis=1)
    firsts = jnp.sum(starts[:, :, None] * matches, axis=1)
    send_sizes = lax.dynamic_index_in_dim(image_sizes, my_index, 0, keepdims=False)
    send_firsts = lax.dynamic_index_in_dim(firsts, my_index, 0, keepdims=False)
    within = lax.broadcasted_iota(jnp.int32, (row_count, pair_slots), 1)
    send_valid = within < send_sizes[:, None]
    send_index = jnp.minimum(send_firsts[:, None] + within, home_slots - 1).reshape(-1)
    arrive_sizes = lax.dynamic_index_in_dim(image_sizes, my_index, 1, keepdims=False)
    arrive_ends = jnp.cumsum(arrive_sizes)
    arrive_starts = arrive_ends - arrive_sizes
    slot_grid = lax.broadcasted_iota(jnp.int32, (TOK, row_count), 0)
    source = jnp.sum((slot_grid >= arrive_ends[None, :]).astype(jnp.int32), axis=1)
    chosen = (source[:, None] == lax.broadcasted_iota(jnp.int32, (TOK, row_count), 1)).astype(
        jnp.int32
    )
    arrive_index = (
        source * pair_slots + slot_grid[:, 0] - jnp.sum(chosen * arrive_starts[None, :], axis=1)
    )
    home_mixed = project(
        attend(qkv_home[0], segment_ids[0], query_gain, key_gain), resid_home[0], out_weight
    )
    count_row = lax.dynamic_index_in_dim(patch_counts, my_index, 0, keepdims=False)
    pooled = pool(home_mixed, segment_ids[0], count_row)
    partial_value = label_terms(pooled, label_weight)
    send_mixed = pick(home_mixed, send_index, send_valid)
    got_mixed = lax.all_to_all(send_mixed, "dp", split_axis=0, concat_axis=0, tiled=True)
    mixed = jnp.take(got_mixed.reshape(row_count * pair_slots, -1), arrive_index, axis=0)
    logit_sums = lax.psum_scatter(
        partial_value.astype(jnp.bfloat16), "mp", scatter_dimension=1, tiled=True
    ).astype(jnp.float32)
    class_probs = jax.nn.sigmoid(logit_sums + label_bias[None, None, :])
    labels = lax.all_to_all(
        class_probs.astype(jnp.bfloat16), "dp", split_axis=0, concat_axis=2, tiled=True
    ).astype(class_probs.dtype)
    return (mixed[None], labels)


def solution(mesh):
    return jax.shard_map(
        on_device,
        mesh=mesh,
        in_specs=(
            P(("groups", "dp"), None, None, "mp"),
            P(("groups", "dp"), None, "mp"),
            P("dp", "mp"),
            P("mp", "dp"),
            P("dp"),
            P(),
            P(),
            P("groups", None),
            P("groups", None),
            P(("groups", "dp"), None),
        ),
        out_specs=(P(("groups", "dp"), None, "mp"), P(("groups", "dp"), "mp", None)),
        check_vma=False,
    )
```

```python
import functools
import math

import jax
import jax.numpy as jnp
from jax import lax
from jax.experimental import pallas as pl
from jax.experimental.pallas import tpu as pltpu
from jax.sharding import PartitionSpec as P

TOK = 384


EPSILON = 1e-06


def head_norm(values, norm_gain):
    center = values - jnp.mean(values, axis=-1, keepdims=True)
    spread = jnp.mean(center * center, axis=-1, keepdims=True)
    return center * lax.rsqrt(spread + EPSILON) * norm_gain


def attend(qkv_rows, seg_rows, query_gain, key_gain):
    length = qkv_rows.shape[0]
    head_width = query_gain.shape[0]
    head_count = qkv_rows.shape[2] // head_width
    split_parts = qkv_rows.reshape(length, 3, head_count, head_width)
    queries = head_norm(split_parts[:, 0].astype(jnp.float32), query_gain).astype(jnp.bfloat16)
    key_rows = head_norm(split_parts[:, 1].astype(jnp.float32), key_gain).astype(jnp.bfloat16)
    scores = jnp.einsum(
        "qhd,khd->hqk", queries, key_rows, preferred_element_type=jnp.float32
    ) / math.sqrt(head_width)
    same_image = seg_rows[:, None] == seg_rows[None, :]
    raised = jnp.where(same_image[None], jnp.exp(scores), 0.0)
    weights = (raised / jnp.sum(raised, axis=-1, keepdims=True)).astype(jnp.bfloat16)
    head_out = jnp.einsum(
        "hqk,khd->qhd", weights, split_parts[:, 2], preferred_element_type=jnp.float32
    )
    return head_out.reshape(length, head_count * head_width).astype(jnp.bfloat16)


def project(heads_local, resid_rows, out_weight):
    gathered = lax.all_gather(heads_local, "mp", axis=1, tiled=True)
    running = resid_rows.astype(jnp.float32) + jnp.dot(
        gathered,
        lax.all_gather(out_weight, "dp", axis=0, tiled=True),
        preferred_element_type=jnp.float32,
    )
    return running.astype(jnp.bfloat16)


def pool(row_mixed, seg_rows, count_row):
    images = count_row.shape[0]
    member_ids = lax.broadcasted_iota(jnp.int32, (images, seg_rows.shape[0]), 0)
    member = (member_ids == seg_rows[None, :]).astype(jnp.bfloat16)
    image_sums = jnp.dot(member, row_mixed, preferred_element_type=jnp.float32)
    return (image_sums / count_row[:, None].astype(jnp.float32)).astype(jnp.bfloat16)


def label_terms(pooled, label_weight):
    return jnp.einsum(
        "abd,dc->abc",
        lax.all_gather(pooled[None], "dp", axis=0, tiled=True),
        label_weight,
        preferred_element_type=jnp.float32,
    )


def pick(values, row_index, is_valid):
    taken = jnp.take(values, row_index, axis=0)
    taken = taken.reshape(is_valid.shape + values.shape[1:])
    keep_mask = is_valid.reshape(is_valid.shape + (1,) * (values.ndim - 1))
    return jnp.where(keep_mask, taken, jnp.zeros_like(taken))


MESH = pl.DeviceIdType.MESH
LANES = 128
TILE = 256
WINDOW = 256


def remote(src, dst, send_sem, recv_sem, where):
    return pltpu.make_async_remote_copy(
        src_ref=src,
        dst_ref=dst,
        send_sem=send_sem,
        recv_sem=recv_sem,
        device_id=where,
        device_id_type=MESH,
    )


def normed(values, gain):
    values = values.astype(jnp.float32)
    center = values - jnp.mean(values, axis=-1, keepdims=True)
    spread = jnp.mean(center * center, axis=-1, keepdims=True)
    return (center * lax.rsqrt(spread + EPSILON) * gain).astype(jnp.bfloat16)


def block_kernel(
    sizes,
    counts,
    plan,
    bias_ref,
    qg_ref,
    kg_ref,
    qkv_hbm,
    resid_hbm,
    w_hbm,
    lw_hbm,
    out_ref,
    lab_ref,
    raw,
    blk,
    hx,
    gath,
    relay,
    wall,
    resv,
    end_qkv,
    end_resid,
    zall,
    places,
    ssend,
    srecv,
    fsend,
    hsum,
    hrecv,
    htot,
    lpart,
    lgot,
    lpool,
    lwv,
    lgs,
    lrecv,
    pbuf,
    precv,
    load_sem,
    os,
    orr,
    cs,
    rr,
    ins,
    cr,
    wzs,
    wzr,
    wys,
    wyr,
    xs,
    xr,
    ss,
    sr,
    fs,
    fr,
    hs,
    hr,
    ts,
    tr,
    gs,
    gr,
    ls,
    lr,
    bs,
    br,
):
    rows, slots, pair = sizes
    z = lax.axis_index("dp")
    mp = lax.axis_index("mp")
    group = lax.axis_index("groups")
    other = 1 - group
    core = lax.rem(mp, 2)
    xpos = mp // 2
    near = mp + 1 - 2 * core
    side = lax.rem(mp + 2, 4)
    half_id = z // 2
    member_id = z - 2 * half_id
    zo = 3 * half_id
    zp = 1 + half_id
    zq = 2 - half_id
    zo2 = 3 - 3 * half_id
    inner = z == zp
    outer = z == zo
    partner = zo + zp - z
    keeps = xpos == half_id
    crosses = xpos != half_id
    order_a = [zo2, zq, zo, zp]
    order_c = [zo, zp, zo2, zq]
    homes = [z, zq, zo2]
    width = raw.shape[2]
    split = width // 2
    depth, cols = w_hbm.shape
    tiles = cols // TILE
    images = rows
    tokens = out_ref.shape[0]
    bf16, f32 = jnp.bfloat16, jnp.float32

    loads = [
        pltpu.make_async_copy(qkv_hbm, raw, load_sem.at[0]),
        pltpu.make_async_copy(w_hbm, wall.at[member_id], load_sem.at[1]),
        pltpu.make_async_copy(resid_hbm, resv, load_sem.at[2]),
        pltpu.make_async_copy(lw_hbm, lwv, load_sem.at[3]),
    ]
    for load in loads:
        load.start()

    barrier = pltpu.get_barrier_semaphore()
    for k in range(1, 4):
        pl.semaphore_signal(
            barrier, inc=1, device_id={"mp": lax.rem(mp + k, 4)}, device_id_type=MESH
        )
    for k in range(1, rows):
        pl.semaphore_signal(
            barrier, inc=1, device_id={"dp": lax.rem(z + k, rows)}, device_id_type=MESH
        )
    pl.semaphore_signal(barrier, inc=1, device_id={"groups": other}, device_id_type=MESH)
    pl.semaphore_wait(barrier, 3 + rows - 1 + 1)

    def tile_at(t):
        return pl.ds(pl.multiple_of(t * TILE, TILE), TILE)

    def block_at(index):
        return pl.ds(pl.multiple_of(index * pair, pair), pair)

    def repeat(count, body):
        def step(t, carry):
            body(t)
            return carry

        lax.fori_loop(0, count, step, 0)

    def weight_part(which, part, t):
        size = depth // 2
        return wall.at[which, pl.ds(pl.multiple_of(part * size, size), size), tile_at(t)]

    def wzcopy(t):
        size = depth // 2
        own = w_hbm.at[pl.ds(pl.multiple_of(group * size, size), size), tile_at(t)]
        return remote(
            own, weight_part(member_id, group, t), wzs.at[t], wzr.at[t], {"dp": partner}
        )

    def wycopy(t):
        part = weight_part(1 - member_id, group, t)
        return remote(part, part, wys.at[t], wyr.at[t], {"groups": other})

    def forward_weight(t):
        part = weight_part(1 - member_id, group, t)
        remote(part, part, wys.at[t], wzr.at[t], {"groups": other}).wait_recv()
        wycopy(t).start()

    def wait_weight(t):
        part = weight_part(1 - member_id, other, t)
        remote(part, part, wys.at[t], wyr.at[t], {"groups": other}).wait_recv()

    early = 2

    def send_weight(t):
        @pl.when(outer)
        def _():
            wzcopy(t).start()

    for t in range(early):
        wzcopy(t).start()

    @pl.when(inner)
    def _():
        for t in range(early, tiles):
            wzcopy(t).start()

    def gathered(which, home, dest):
        return which, dest, pl.ds(pl.multiple_of(home * pair, pair), pair)

    def own_piece(which, k):
        kb, e, at = gathered(which, 0, order_a[k])
        return gath.at[kb, e, at, :]

    def own_near(k):
        part = own_piece(core, k)
        return remote(part, part, os.at[k, 0], orr.at[k, 0], {"mp": near})

    def own_side(k):
        part = own_piece(core, k)
        return remote(part, part, os.at[k, 1], orr.at[k, 1], {"mp": side})

    def own_wait(kind, k):
        part = own_piece(core if kind else 1 - core, k)
        remote(part, part, os.at[k, kind], orr.at[k, kind], {"mp": near}).wait_recv()

    def half_at(which):
        return pl.ds(pl.multiple_of(which * split, LANES), split)

    there = jnp.where(outer, 2, 1)

    def cross_low(k):
        dest = order_c[k]
        kb, e, at = gathered(core, there, dest)
        return remote(
            hx.at[block_at(dest), pl.ds(0, split)],
            gath.at[kb, e, at, pl.ds(0, split)],
            cs.at[k, 0],
            cr.at[there - 1, k, 0],
            {"dp": zq},
        )

    def cross_side(k):
        dest = order_c[k]
        return remote(
            hx.at[block_at(dest), pl.ds(split, split)],
            relay.at[k],
            cs.at[k, 1],
            rr.at[k],
            {"mp": side},
        )

    def cross_high(k):
        kb, e, at = gathered(core, there, order_c[k])
        return remote(
            relay.at[k],
            gath.at[kb, e, at, pl.ds(split, split)],
            cs.at[k, 0],
            cr.at[there - 1, k, 0],
            {"dp": zq},
        )

    mine = jnp.where(keeps, 0, 1)

    def cross_piece(h, k, which, part):
        kb, e, at = gathered(which, h + 1, order_a[k])
        return gath.at[kb, e, at, half_at(part)]

    def cross_copy(h, k, kind):
        part = cross_piece(h, k, core, 1 - mine if kind == 2 else mine)
        target = side if kind == 1 else near
        return remote(part, part, ins.at[h, k, kind], cr.at[h, k, kind + 1], {"mp": target})

    def cross_wait(h, k, kind):
        which = core if kind in (0, 2) else 1 - core
        part = cross_piece(h, k, which, mine if kind < 2 else 1 - mine)
        remote(part, part, ins.at[h, k, 0], cr.at[h, k, kind], {"mp": near}).wait_recv()

    def serve_keep(k):
        @pl.when(keeps)
        def _():
            remote(
                relay.at[k], relay.at[k], cs.at[k, 1], rr.at[k], {"mp": side}
            ).wait_recv()
            cross_high(k).start()

    def serve_cross(k):
        @pl.when(crosses)
        def _():
            own_wait(1, k)
            own_near(k).start()

    own_counts = [counts[z, j] for j in range(images)]
    own_plan = [plan[z, j] for j in range(images)]
    own_starts, running = [], 0
    for j in range(images):
        own_starts.append(running)
        running = running + own_counts[j]

    def span_of(dest):
        first, count = 0, 0
        for j in range(images):
            hit = (own_plan[j] == dest).astype(jnp.int32)
            first = first + hit * own_starts[j]
            count = count + hit * own_counts[j]
        return first, count

    pick_row = lax.broadcasted_iota(jnp.int32, (pair, 1), 0)
    pick_col = lax.broadcasted_iota(jnp.int32, (1, WINDOW), 1)
    base = slots // 16 * 16
    rest = slots - base

    def picker(dest):
        first, count = span_of(dest)
        low = lax.min(lax.div(first, 16), (base - WINDOW) // 16) * 16
        valid = pick_row < count
        chosen = jnp.logical_and(pick_col == pick_row + (first - low), valid).astype(bf16)
        ends = jnp.logical_and(pick_col[:, :16] == pick_row + (first - base), valid).astype(bf16)
        return pl.ds(low, WINDOW), chosen, ends, count

    def moved_rows(chosen, ends, body, end):
        part = jnp.dot(chosen, body, preferred_element_type=f32)
        return part + jnp.dot(ends, end, preferred_element_type=f32)

    heads = width // LANES
    q_gain = qg_ref[...]
    k_gain = kg_ref[...]
    scale = math.log2(math.e) / math.sqrt(LANES)
    key_at = lax.broadcasted_iota(jnp.int32, (1, pair), 1)

    loads[0].wait()
    end_qkv[...] = jnp.zeros(end_qkv.shape, bf16)
    if rest:
        end_qkv[:, pl.ds(0, rest), :] = raw[:, pl.ds(base, rest), :]

    def attend_block(dest):
        at_rows, chosen, ends, count = picker(dest)
        for part in range(3):
            blk[part] = moved_rows(
                chosen, ends, raw[part, at_rows, :], end_qkv[part]
            ).astype(bf16)
        seen = key_at < count
        real = pick_row < count
        line = sum_row == z * rows + dest

        for h in range(heads):
            at = pl.ds(h * LANES, LANES)
            scores = lax.dot_general(
                normed(blk[0, :, at], q_gain),
                normed(blk[1, :, at], k_gain),
                (((1,), (1,)), ((), ())),
                preferred_element_type=f32,
            )
            raised = jnp.where(seen, jnp.exp2(scores * scale), 0.0)
            total = jnp.sum(raised, axis=-1, keepdims=True)
            weights = (raised * (1.0 / total)).astype(bf16)
            result = jnp.dot(weights, blk[2, :, at], preferred_element_type=f32)
            result = result.astype(bf16)
            hx[block_at(dest), at] = result
            total = jnp.sum(jnp.where(real, result.astype(f32), 0.0), axis=0, keepdims=True)
            hsum[:, at] = jnp.where(line, total, hsum[:, at])

    group_lines = rows * rows
    sum_row = lax.broadcasted_iota(jnp.int32, (group_lines, 1), 0)
    hsum[...] = jnp.zeros(hsum.shape, f32)

    for k in range(rows):
        dest = jnp.where(keeps, order_a[k], order_c[k])
        attend_block(dest)

        @pl.when(keeps)
        def _(k=k):
            kb, e, at = gathered(core, 0, order_a[k])
            gath[kb, e, at, :] = hx[block_at(order_a[k]), :]
            if k < 2:
                own_side(k).start()
            else:

                @pl.when(outer)
                def _():
                    own_side(k).start()

            own_near(k).start()

        @pl.when(crosses)
        def _(k=k):
            cross_side(k).start()
            cross_low(k).start()

    def own_later(k):
        @pl.when(keeps)
        def _():
            own_side(k).start()

    collects = z == mp

    def hcopy():
        return remote(hsum, hrecv.at[z], hs.at[0], hr.at[z], {"dp": mp})

    def tcopy(k):
        peer = lax.rem(mp + k, 4)
        return remote(htot, htot, ts.at[k], tr.at[0], {"mp": peer})

    @pl.when(jnp.logical_not(collects))
    def _():
        hcopy().start()

    def collect_sums():
        @pl.when(collects)
        def _():
            total = hsum[...]
            for k in range(1, rows):
                source = lax.rem(z + k, rows)
                part = hrecv.at[source]
                remote(part, part, hs.at[0], hr.at[source], {"dp": source}).wait_recv()
                total = total + hrecv[source]
            htot[...] = total
            for k in range(1, 4):
                tcopy(k).start()

    def gcopy(kind):
        if kind == 0:
            return remote(lpart, lgot.at[0], gs.at[0], gr.at[0], {"dp": zp})
        if kind == 1:
            return remote(lpart, lgot.at[1], gs.at[0], gr.at[1], {"dp": zq})
        return remote(lpool, lgot.at[0], gs.at[1], gr.at[0], {"dp": zo})

    slot_at = lax.broadcasted_iota(jnp.int32, (1, slots), 1)

    def partial_sums():
        @pl.when(jnp.logical_not(collects))
        def _():
            remote(htot, htot, ts.at[1], tr.at[0], {"mp": near}).wait_recv()

        sums = htot[...]
        high = sums.astype(bf16)
        low = (sums - high.astype(f32)).astype(bf16)
        owner = jnp.full(slot_at.shape, -1, jnp.int32)
        for j in range(images):
            inside = jnp.logical_and(
                slot_at >= own_starts[j], slot_at < own_starts[j] + own_counts[j]
            )
            owner = jnp.where(inside, z * rows + own_plan[j], owner)
        member = (sum_row == owner).astype(bf16)

        def sum_tile(t):
            weights = wall[member_id, :, tile_at(t)]
            part = jnp.dot(high, weights, preferred_element_type=f32)
            part = part + jnp.dot(low, weights, preferred_element_type=f32)
            part = part + jnp.dot(member, resv[:, tile_at(t)], preferred_element_type=f32)
            lpart[:, tile_at(t)] = part

        repeat(tiles, sum_tile)

    loads[2].wait()
    end_resid[...] = jnp.zeros(end_resid.shape, bf16)
    if rest:
        end_resid[pl.ds(0, rest), :] = resv[pl.ds(base, rest), :]

    place_row = lax.broadcasted_iota(jnp.int32, (tokens, 1), 0)
    place_col = lax.broadcasted_iota(jnp.int32, (1, rows * pair), 1)

    def build_place(k):
        dest = order_a[k]
        begin = 0
        target = jnp.zeros(place_col.shape, jnp.int32)
        limit = jnp.zeros(place_col.shape, jnp.int32)
        for r in range(rows):
            count = 0
            for j in range(images):
                count = count + (plan[r, j] == dest).astype(jnp.int32) * counts[r, j]
            here = place_col >= r * pair
            target = jnp.where(here, place_col + (begin - r * pair), target)
            limit = jnp.where(here, r * pair + count, limit)
            begin = begin + count
        target = jnp.where(place_col < limit, target, -1)
        places[k] = (place_row == target).astype(bf16)

    zero_block = jnp.zeros((pair, cols), bf16)
    loads[1].wait()

    def project(k, t, count, chosen):
        at_rows, taken, ends, _ = chosen
        dest = order_a[k]
        used = pl.ds(0, count * pair)
        acc = jnp.dot(gath[0, dest, used, :], wall[0, :, tile_at(t)], preferred_element_type=f32)
        acc = acc + jnp.dot(
            gath[1, dest, used, :], wall[1, :, tile_at(t)], preferred_element_type=f32
        )
        for h in range(count):
            term = acc[h * pair : (h + 1) * pair]
            if h == 0:
                term = term + moved_rows(
                    taken, ends, resv[at_rows, tile_at(t)], end_resid[:, tile_at(t)]
                )
            zall[dest, block_at(homes[h]), tile_at(t)] = term.astype(bf16)

    def arrange(k, t):
        return jnp.dot(
            places[k], zall[order_a[k], :, tile_at(t)], preferred_element_type=f32
        )

    def xcopy(k, t):
        dest = order_a[k]
        part = zall.at[dest, block_at(zo), tile_at(t)]
        return remote(part, part, xs.at[k, t], xr.at[k, t], {"dp": zp})

    def xwait(k, t):
        dest = order_a[k]
        part = zall.at[dest, block_at(zo), tile_at(t)]
        remote(part, part, xs.at[k, t], xr.at[k, t], {"dp": zo}).wait_recv()

    def scopy(k, t):
        return remote(
            ssend.at[k, :, tile_at(t)],
            srecv.at[k, :, tile_at(t)],
            ss.at[k, t],
            sr.at[k, t],
            {"dp": zq},
        )

    def fcopy(t):
        return remote(
            fsend.at[:, tile_at(t)], srecv.at[0, :, tile_at(t)], fs.at[t], fr.at[t], {"dp": zo}
        )

    def ppeer(k):
        return lax.rem(z + k, rows)

    group_rows = lgs.shape[1]
    lines = images * group_rows
    classes = lwv.shape[1]

    def label_logits(source):
        loads[3].wait()
        line = lax.broadcasted_iota(jnp.int32, (lines, 1), 0)
        wanted = jnp.full((lines, 1), -1, jnp.int32)
        divisor = jnp.ones((group_lines, 1), f32)
        for r in range(rows):
            for j in range(images):
                row = r * rows + plan[r, j]
                wanted = jnp.where(line == j * group_rows + r, row, wanted)
                divisor = jnp.where(sum_row == row, counts[r, j].astype(f32), divisor)
        columns = lax.broadcasted_iota(jnp.int32, (lines, group_lines), 1)
        order = (columns == wanted).astype(bf16)
        pooled = (source[...] / divisor).astype(bf16)
        by_image = jnp.dot(order, pooled, preferred_element_type=f32).astype(bf16)

        def label_tile(t):
            part = jnp.dot(by_image, lwv[:, tile_at(t)], preferred_element_type=f32)
            for j in range(images):
                lgs[j, :, tile_at(t)] = part[j * group_rows : (j + 1) * group_rows]

        repeat(classes // TILE, label_tile)
        for k in range(1, 4):
            lcopy(k).start()

    def lcopy(k):
        peer = lax.rem(mp + k, 4)
        return remote(lgs.at[peer], lrecv.at[k], ls.at[k], lr.at[k], {"mp": peer})

    def bcopy(k):
        peer = ppeer(k)
        return remote(pbuf.at[peer], precv.at[z], bs.at[k], br.at[k], {"dp": peer})

    def label_probs():
        for k in range(1, 4):
            lcopy(k).wait_recv()
        total = lgs[mp]
        for k in range(1, 4):
            total = total + lrecv[k]
        probs = jax.nn.sigmoid(total + bias_ref[...])
        for r in range(rows):
            for t in range(classes // LANES):
                pbuf[r, pl.ds(t, 1), :] = probs[r : r + 1, t * LANES : (t + 1) * LANES]
        for k in range(1, rows):
            bcopy(k).start()

    @pl.when(outer)
    def _():
        forward_weight(0)
        serve_keep(0)
        serve_cross(0)
        forward_weight(1)
        for r in range(1, rows):
            zall[zo, block_at(lax.rem(z + r, rows)), :] = zero_block
        build_place(2)
        own_wait(0, 0)
        chosen = picker(order_a[0])
        for t in range(tiles):
            wait_weight(t)
            project(0, t, 1, chosen)
            xcopy(0, t).start()
            if t + 2 < tiles:
                send_weight(t + 2)
                forward_weight(t + 2)
            if t + 1 < rows:
                serve_keep(t + 1)
                serve_cross(t + 1)
            if t == 1:
                collect_sums()
        own_wait(0, 1)
        chosen = picker(order_a[1])

        def second_tile(t, chosen=chosen):
            project(1, t, 1, chosen)
            xcopy(1, t).start()

        repeat(tiles, second_tile)
        partial_sums()
        gcopy(0).start()
        own_wait(0, 3)
        chosen = picker(order_a[3])

        def third_tile(t, chosen=chosen):
            project(3, t, 1, chosen)
            xcopy(3, t).start()

        repeat(tiles, third_tile)
        own_wait(0, 2)
        chosen = picker(order_a[2])

        def last_tile(t, chosen=chosen):
            project(2, t, 1, chosen)
            moved = arrange(2, t)
            fcopy(t).wait_recv()
            value = moved + srecv[0, :, tile_at(t)].astype(f32)
            out_ref[:, tile_at(t)] = value.astype(bf16)

        repeat(tiles, last_tile)
        gcopy(2).wait_recv()
        label_logits(lgot.at[0])
        label_probs()

    @pl.when(inner)
    def _():
        def arrive(k):
            for h in range(2):
                cross_wait(h, k, 0)
                cross_copy(h, k, 1).start()
                cross_copy(h, k, 0).start()

        def spread(k):
            for h in range(2):
                cross_wait(h, k, 2)
                cross_copy(h, k, 2).start()

        def settle(k):
            own_wait(0, k)
            for h in range(2):
                cross_wait(h, k, 1)
                cross_wait(h, k, 3)

        def send_sum(k, t, chosen):
            project(k, t, 3, chosen)
            xwait(k, t)
            ssend[k, :, tile_at(t)] = arrange(k, t).astype(bf16)
            scopy(k, t).start()

        forward_weight(0)
        serve_keep(0)
        serve_cross(0)
        arrive(0)
        forward_weight(1)
        serve_keep(1)
        arrive(1)
        serve_cross(1)
        own_later(2)
        serve_keep(2)
        serve_keep(3)
        zall[zo, block_at(zo), :] = zero_block
        for k in range(rows):
            build_place(k)
        spread(0)
        collect_sums()
        arrive(2)
        own_later(3)
        settle(0)
        chosen = picker(order_a[0])
        after = {
            0: lambda: (forward_weight(2), spread(1), arrive(3)),
            1: lambda: (forward_weight(3), serve_cross(2)),
            2: lambda: (forward_weight(4), spread(2)),
            3: lambda: (forward_weight(5), serve_cross(3)),
            4: lambda: (spread(3), partial_sums()),
        }
        for t in range(tiles):
            wait_weight(t)
            send_sum(0, t, chosen)
            if t in after:
                after[t]()
        settle(1)
        settle(2)
        gcopy(0).wait_recv()
        lpart[...] += lgot[0]
        gcopy(1).start()
        chosen = picker(order_a[1])
        again = picker(order_a[2])

        def middle_tile(t, chosen=chosen, again=again):
            send_sum(1, t, chosen)
            project(2, t, 3, again)
            moved = arrange(2, t)
            scopy(0, t).wait_recv()
            value = moved + srecv[0, :, tile_at(t)].astype(f32)
            fsend[:, tile_at(t)] = value.astype(bf16)
            fcopy(t).start()

        repeat(tiles, middle_tile)
        gcopy(1).wait_recv()
        lpool[...] = lpart[...] + lgot[1]
        gcopy(2).start()
        label_logits(lpool)
        settle(3)
        chosen = picker(order_a[3])

        def last_tile(t, chosen=chosen):
            project(3, t, 3, chosen)
            xwait(3, t)
            moved = arrange(3, t)
            scopy(1, t).wait_recv()
            value = moved + srecv[1, :, tile_at(t)].astype(f32)
            out_ref[:, tile_at(t)] = value.astype(bf16)

        half = tiles // 2
        repeat(half, last_tile)
        label_probs()
        repeat(tiles - half, lambda t: last_tile(t + half))

    for k in range(1, rows):
        part = precv.at[lax.rem(z + rows - k, rows)]
        remote(part, part, bs.at[k], br.at[k], {"dp": ppeer(k)}).wait_recv()
    precv[z] = pbuf[z]
    lab_ref[...] = precv[...]

    for k in range(rows):
        own_near(k).wait_send()

        @pl.when(keeps)
        def _(k=k):
            own_side(k).wait_send()
            cross_high(k).wait_send()

        @pl.when(crosses)
        def _(k=k):
            cross_low(k).wait_send()
            cross_side(k).wait_send()

        @pl.when(inner)
        def _(k=k):
            for h in range(2):
                for kind in range(3):
                    cross_copy(h, k, kind).wait_send()

    def close_tile(t):
        wzcopy(t).wait_send()
        wycopy(t).wait_send()

        @pl.when(outer)
        def _():
            for k in (0, 1, 3):
                xcopy(k, t).wait_send()

        @pl.when(inner)
        def _():
            for k in range(2):
                scopy(k, t).wait_send()
            fcopy(t).wait_send()

    repeat(tiles, close_tile)

    @pl.when(outer)
    def _():
        gcopy(0).wait_send()

    @pl.when(inner)
    def _():
        gcopy(1).wait_send()
        gcopy(2).wait_send()

    @pl.when(collects)
    def _():
        for k in range(1, 4):
            tcopy(k).wait_send()

    @pl.when(jnp.logical_not(collects))
    def _():
        hcopy().wait_send()

    for k in range(1, rows):
        bcopy(k).wait_send()
    for k in range(1, 4):
        lcopy(k).wait_send()


def round_up(value, step):
    return -(-value // step) * step


def fused(
    qkv_home,
    resid_home,
    out_weight,
    label_weight,
    label_bias,
    query_gain,
    key_gain,
    patch_counts,
    move_plan,
):
    rows = lax.axis_size("dp")
    slots, width = qkv_home.shape[1], qkv_home.shape[3]
    depth, cols = out_weight.shape
    classes = label_weight.shape[1]
    pair = round_up(slots // rows, 16)
    tiles = cols // TILE
    bf16, f32 = jnp.bfloat16, jnp.float32
    vmem = pl.BlockSpec(memory_space=pltpu.VMEM)
    smem = pl.BlockSpec(memory_space=pltpu.SMEM)
    hbm = pl.BlockSpec(memory_space=pl.ANY)
    dma = pltpu.SemaphoreType.DMA
    mixed, labels = pl.pallas_call(
        functools.partial(block_kernel, (rows, slots, pair)),
        out_shape=(
            jax.ShapeDtypeStruct((TOK, cols), bf16),
            jax.ShapeDtypeStruct((rows, classes // LANES, LANES), f32),
        ),
        in_specs=[smem, smem, vmem, vmem, vmem, hbm, hbm, hbm, hbm],
        out_specs=(vmem, vmem),
        scratch_shapes=[
            pltpu.VMEM((3, slots, width), bf16),
            pltpu.VMEM((3, pair, width), bf16),
            pltpu.VMEM((rows * pair, width), bf16),
            pltpu.VMEM((2, rows, 3 * pair, width), bf16),
            pltpu.VMEM((rows, pair, width // 2), bf16),
            pltpu.VMEM((2, depth, cols), bf16),
            pltpu.VMEM((slots, cols), bf16),
            pltpu.VMEM((3, 16, width), bf16),
            pltpu.VMEM((16, cols), bf16),
            pltpu.VMEM((rows, rows * pair, cols), bf16),
            pltpu.VMEM((rows, TOK, rows * pair), bf16),
            pltpu.VMEM((2, TOK, cols), bf16),
            pltpu.VMEM((2, TOK, cols), bf16),
            pltpu.VMEM((TOK, cols), bf16),
            pltpu.VMEM((rows * rows, width), f32),
            pltpu.VMEM((rows, rows * rows, width), f32),
            pltpu.VMEM((rows * rows, width), f32),
            pltpu.VMEM((rows * rows, cols), f32),
            pltpu.VMEM((2, rows * rows, cols), f32),
            pltpu.VMEM((rows * rows, cols), f32),
            pltpu.VMEM(label_weight.shape, bf16),
            pltpu.VMEM((rows, 8, classes), f32),
            pltpu.VMEM((4, 8, classes), f32),
            pltpu.VMEM((rows, classes // LANES, LANES), f32),
            pltpu.VMEM((rows, classes // LANES, LANES), f32),
            dma((4,)),
            dma((rows, 2)),
            dma((rows, 2)),
            dma((rows, 2)),
            dma((rows,)),
            dma((2, rows, 3)),
            dma((2, rows, 4)),
            dma((tiles,)),
            dma((tiles,)),
            dma((tiles,)),
            dma((tiles,)),
            dma((rows, tiles)),
            dma((rows, tiles)),
            dma((2, tiles)),
            dma((2, tiles)),
            dma((tiles,)),
            dma((tiles,)),
            dma((1,)),
            dma((rows,)),
            dma((4,)),
            dma((1,)),
            dma((2,)),
            dma((2,)),
            dma((4,)),
            dma((4,)),
            dma((rows,)),
            dma((rows,)),
        ],
        compiler_params=pltpu.CompilerParams(
            collective_id=0, has_side_effects=True, vmem_limit_bytes=63 * 1024 * 1024
        ),
    )(
        patch_counts,
        move_plan,
        label_bias[None],
        query_gain[None],
        key_gain[None],
        jnp.transpose(qkv_home[0], (1, 0, 2)),
        resid_home[0],
        out_weight,
        label_weight,
    )
    return (mixed[None], labels.reshape(1, 1, rows * classes))


def on_device(
    qkv_home,
    resid_home,
    out_weight,
    label_weight,
    label_bias,
    query_gain,
    key_gain,
    patch_counts,
    move_plan,
    segment_ids,
):
    row_count = lax.axis_size("dp")
    if row_count == lax.axis_size("mp") == 4 and lax.axis_size("groups") == 2:
        return fused(
            qkv_home,
            resid_home,
            out_weight,
            label_weight,
            label_bias,
            query_gain,
            key_gain,
            patch_counts,
            move_plan,
        )
    my_index = lax.axis_index("dp")
    home_slots = segment_ids.shape[1]
    pair_slots = home_slots // row_count
    image_ids = lax.broadcasted_iota(jnp.int32, (row_count, row_count, row_count), 2)
    image_ends = jnp.cumsum(patch_counts, axis=1)
    starts = image_ends - patch_counts
    matches = (move_plan[:, :, None] == image_ids).astype(jnp.int32)
    image_sizes = jnp.sum(patch_counts[:, :, None] * matches, axis=1)
    firsts = jnp.sum(starts[:, :, None] * matches, axis=1)
    send_sizes = lax.dynamic_index_in_dim(image_sizes, my_index, 0, keepdims=False)
    send_firsts = lax.dynamic_index_in_dim(firsts, my_index, 0, keepdims=False)
    within = lax.broadcasted_iota(jnp.int32, (row_count, pair_slots), 1)
    send_valid = within < send_sizes[:, None]
    send_index = jnp.minimum(send_firsts[:, None] + within, home_slots - 1).reshape(-1)
    arrive_sizes = lax.dynamic_index_in_dim(image_sizes, my_index, 1, keepdims=False)
    arrive_ends = jnp.cumsum(arrive_sizes)
    arrive_starts = arrive_ends - arrive_sizes
    slot_grid = lax.broadcasted_iota(jnp.int32, (TOK, row_count), 0)
    source = jnp.sum((slot_grid >= arrive_ends[None, :]).astype(jnp.int32), axis=1)
    chosen = (source[:, None] == lax.broadcasted_iota(jnp.int32, (TOK, row_count), 1)).astype(
        jnp.int32
    )
    arrive_index = (
        source * pair_slots + slot_grid[:, 0] - jnp.sum(chosen * arrive_starts[None, :], axis=1)
    )
    home_mixed = project(
        attend(qkv_home[0], segment_ids[0], query_gain, key_gain), resid_home[0], out_weight
    )
    count_row = lax.dynamic_index_in_dim(patch_counts, my_index, 0, keepdims=False)
    pooled = pool(home_mixed, segment_ids[0], count_row)
    partial_value = label_terms(pooled, label_weight)
    send_mixed = pick(home_mixed, send_index, send_valid)
    got_mixed = lax.all_to_all(send_mixed, "dp", split_axis=0, concat_axis=0, tiled=True)
    mixed = jnp.take(got_mixed.reshape(row_count * pair_slots, -1), arrive_index, axis=0)
    logit_sums = lax.psum_scatter(
        partial_value.astype(jnp.bfloat16), "mp", scatter_dimension=1, tiled=True
    ).astype(jnp.float32)
    class_probs = jax.nn.sigmoid(logit_sums + label_bias[None, None, :])
    labels = lax.all_to_all(
        class_probs.astype(jnp.bfloat16), "dp", split_axis=0, concat_axis=2, tiled=True
    ).astype(class_probs.dtype)
    return (mixed[None], labels)


def solution(mesh):
    return jax.shard_map(
        on_device,
        mesh=mesh,
        in_specs=(
            P(("groups", "dp"), None, None, "mp"),
            P(("groups", "dp"), None, "mp"),
            P("dp", "mp"),
            P("mp", "dp"),
            P("dp"),
            P(),
            P(),
            P("groups", None),
            P("groups", None),
            P(("groups", "dp"), None),
        ),
        out_specs=(P(("groups", "dp"), None, "mp"), P(("groups", "dp"), "mp", None)),
        check_vma=False,
    )
```

```python
import functools
import math

import jax
import jax.numpy as jnp
from jax import lax
from jax.experimental import pallas as pl
from jax.experimental.pallas import tpu as pltpu
from jax.sharding import PartitionSpec as P

TOK = 384


EPSILON = 1e-06


def head_norm(values, norm_gain):
    center = values - jnp.mean(values, axis=-1, keepdims=True)
    spread = jnp.mean(center * center, axis=-1, keepdims=True)
    return center * lax.rsqrt(spread + EPSILON) * norm_gain


def attend(qkv_rows, seg_rows, query_gain, key_gain):
    length = qkv_rows.shape[0]
    head_width = query_gain.shape[0]
    head_count = qkv_rows.shape[2] // head_width
    split_parts = qkv_rows.reshape(length, 3, head_count, head_width)
    queries = head_norm(split_parts[:, 0].astype(jnp.float32), query_gain).astype(jnp.bfloat16)
    key_rows = head_norm(split_parts[:, 1].astype(jnp.float32), key_gain).astype(jnp.bfloat16)
    scores = jnp.einsum(
        "qhd,khd->hqk", queries, key_rows, preferred_element_type=jnp.float32
    ) / math.sqrt(head_width)
    same_image = seg_rows[:, None] == seg_rows[None, :]
    raised = jnp.where(same_image[None], jnp.exp(scores), 0.0)
    weights = (raised / jnp.sum(raised, axis=-1, keepdims=True)).astype(jnp.bfloat16)
    head_out = jnp.einsum(
        "hqk,khd->qhd", weights, split_parts[:, 2], preferred_element_type=jnp.float32
    )
    return head_out.reshape(length, head_count * head_width).astype(jnp.bfloat16)


def project(heads_local, resid_rows, out_weight):
    gathered = lax.all_gather(heads_local, "mp", axis=1, tiled=True)
    running = resid_rows.astype(jnp.float32) + jnp.dot(
        gathered,
        lax.all_gather(out_weight, "dp", axis=0, tiled=True),
        preferred_element_type=jnp.float32,
    )
    return running.astype(jnp.bfloat16)


def pool(row_mixed, seg_rows, count_row):
    images = count_row.shape[0]
    member_ids = lax.broadcasted_iota(jnp.int32, (images, seg_rows.shape[0]), 0)
    member = (member_ids == seg_rows[None, :]).astype(jnp.bfloat16)
    image_sums = jnp.dot(member, row_mixed, preferred_element_type=jnp.float32)
    return (image_sums / count_row[:, None].astype(jnp.float32)).astype(jnp.bfloat16)


def label_terms(pooled, label_weight):
    return jnp.einsum(
        "abd,dc->abc",
        lax.all_gather(pooled[None], "dp", axis=0, tiled=True),
        label_weight,
        preferred_element_type=jnp.float32,
    )


def pick(values, row_index, is_valid):
    taken = jnp.take(values, row_index, axis=0)
    taken = taken.reshape(is_valid.shape + values.shape[1:])
    keep_mask = is_valid.reshape(is_valid.shape + (1,) * (values.ndim - 1))
    return jnp.where(keep_mask, taken, jnp.zeros_like(taken))


MESH = pl.DeviceIdType.MESH
LANES = 128
TILE = 256
WINDOW = 256


def remote(src, dst, send_sem, recv_sem, where):
    return pltpu.make_async_remote_copy(
        src_ref=src,
        dst_ref=dst,
        send_sem=send_sem,
        recv_sem=recv_sem,
        device_id=where,
        device_id_type=MESH,
    )


def normed(values, gain):
    values = values.astype(jnp.float32)
    center = values - jnp.mean(values, axis=-1, keepdims=True)
    spread = jnp.mean(center * center, axis=-1, keepdims=True)
    return (center * lax.rsqrt(spread + EPSILON) * gain).astype(jnp.bfloat16)


def block_kernel(
    sizes,
    counts,
    plan,
    bias_ref,
    qg_ref,
    kg_ref,
    qkv_hbm,
    resid_hbm,
    w_hbm,
    lw_hbm,
    out_ref,
    lab_ref,
    raw,
    blk,
    hx,
    gath,
    relay,
    wall,
    resv,
    end_qkv,
    end_resid,
    zall,
    places,
    ssend,
    srecv,
    fsend,
    hsum,
    hrecv,
    htot,
    lpart,
    lgot,
    lpool,
    lwv,
    lgs,
    lrecv,
    pbuf,
    precv,
    load_sem,
    os,
    orr,
    cs,
    rr,
    ins,
    cr,
    wzs,
    wzr,
    wys,
    wyr,
    xs,
    xr,
    ss,
    sr,
    fs,
    fr,
    hs,
    hr,
    ts,
    tr,
    gs,
    gr,
    ls,
    lr,
    bs,
    br,
):
    rows, slots, pair = sizes
    z = lax.axis_index("dp")
    mp = lax.axis_index("mp")
    group = lax.axis_index("groups")
    other = 1 - group
    core = lax.rem(mp, 2)
    xpos = mp // 2
    near = mp + 1 - 2 * core
    side = lax.rem(mp + 2, 4)
    half_id = z // 2
    member_id = z - 2 * half_id
    zo = 3 * half_id
    zp = 1 + half_id
    zq = 2 - half_id
    zo2 = 3 - 3 * half_id
    inner = z == zp
    outer = z == zo
    partner = zo + zp - z
    keeps = xpos == half_id
    crosses = xpos != half_id
    order_a = [zo2, zq, zo, zp]
    order_c = [zo, zp, zo2, zq]
    homes = [z, zq, zo2]
    width = raw.shape[2]
    split = width // 2
    depth, cols = w_hbm.shape
    tiles = cols // TILE
    images = rows
    tokens = out_ref.shape[0]
    bf16, f32 = jnp.bfloat16, jnp.float32

    loads = [
        pltpu.make_async_copy(qkv_hbm, raw, load_sem.at[0]),
        pltpu.make_async_copy(w_hbm, wall.at[member_id], load_sem.at[1]),
        pltpu.make_async_copy(resid_hbm, resv, load_sem.at[2]),
        pltpu.make_async_copy(lw_hbm, lwv, load_sem.at[3]),
    ]
    loads[0].start()

    barrier = pltpu.get_barrier_semaphore()
    for k in range(1, 4):
        pl.semaphore_signal(
            barrier, inc=1, device_id={"mp": lax.rem(mp + k, 4)}, device_id_type=MESH
        )
    for k in range(1, rows):
        pl.semaphore_signal(
            barrier, inc=1, device_id={"dp": lax.rem(z + k, rows)}, device_id_type=MESH
        )
    pl.semaphore_signal(barrier, inc=1, device_id={"groups": other}, device_id_type=MESH)
    pl.semaphore_wait(barrier, 3 + rows - 1 + 1)

    def tile_at(t):
        return pl.ds(pl.multiple_of(t * TILE, TILE), TILE)

    def block_at(index):
        return pl.ds(pl.multiple_of(index * pair, pair), pair)

    def repeat(count, body):
        def step(t, carry):
            body(t)
            return carry

        lax.fori_loop(0, count, step, 0)

    def weight_part(which, part, t):
        size = depth // 2
        return wall.at[which, pl.ds(pl.multiple_of(part * size, size), size), tile_at(t)]

    def wzcopy(t):
        size = depth // 2
        own = w_hbm.at[pl.ds(pl.multiple_of(group * size, size), size), tile_at(t)]
        return remote(
            own, weight_part(member_id, group, t), wzs.at[t], wzr.at[t], {"dp": partner}
        )

    def wycopy(t):
        part = weight_part(1 - member_id, group, t)
        return remote(part, part, wys.at[t], wyr.at[t], {"groups": other})

    def forward_weight(t):
        part = weight_part(1 - member_id, group, t)
        remote(part, part, wys.at[t], wzr.at[t], {"groups": other}).wait_recv()
        wycopy(t).start()

    def wait_weight(t):
        part = weight_part(1 - member_id, other, t)
        remote(part, part, wys.at[t], wyr.at[t], {"groups": other}).wait_recv()

    early = tiles // 2
    wzcopy(0).start()

    @pl.when(inner)
    def _():
        for t in range(1, early):
            wzcopy(t).start()

    loads[1].start()
    loads[2].start()

    def gathered(which, home, dest):
        return which, dest, pl.ds(pl.multiple_of(home * pair, pair), pair)

    def own_piece(which, k):
        kb, e, at = gathered(which, 0, order_a[k])
        return gath.at[kb, e, at, :]

    def own_near(k):
        part = own_piece(core, k)
        return remote(part, part, os.at[k, 0], orr.at[k, 0], {"mp": near})

    def own_side(k):
        part = own_piece(core, k)
        return remote(part, part, os.at[k, 1], orr.at[k, 1], {"mp": side})

    def own_wait(kind, k):
        part = own_piece(core if kind else 1 - core, k)
        remote(part, part, os.at[k, kind], orr.at[k, kind], {"mp": near}).wait_recv()

    def half_at(which):
        return pl.ds(pl.multiple_of(which * split, LANES), split)

    there = jnp.where(outer, 2, 1)

    def cross_low(k):
        dest = order_c[k]
        kb, e, at = gathered(core, there, dest)
        return remote(
            hx.at[block_at(dest), pl.ds(0, split)],
            gath.at[kb, e, at, pl.ds(0, split)],
            cs.at[k, 0],
            cr.at[there - 1, k, 0],
            {"dp": zq},
        )

    def cross_side(k):
        dest = order_c[k]
        return remote(
            hx.at[block_at(dest), pl.ds(split, split)],
            relay.at[k],
            cs.at[k, 1],
            rr.at[k],
            {"mp": side},
        )

    def cross_high(k):
        kb, e, at = gathered(core, there, order_c[k])
        return remote(
            relay.at[k],
            gath.at[kb, e, at, pl.ds(split, split)],
            cs.at[k, 0],
            cr.at[there - 1, k, 0],
            {"dp": zq},
        )

    mine = jnp.where(keeps, 0, 1)

    def cross_piece(h, k, which, part):
        kb, e, at = gathered(which, h + 1, order_a[k])
        return gath.at[kb, e, at, half_at(part)]

    def cross_copy(h, k, kind):
        part = cross_piece(h, k, core, 1 - mine if kind == 2 else mine)
        target = side if kind == 1 else near
        return remote(part, part, ins.at[h, k, kind], cr.at[h, k, kind + 1], {"mp": target})

    def cross_wait(h, k, kind):
        which = core if kind in (0, 2) else 1 - core
        part = cross_piece(h, k, which, mine if kind < 2 else 1 - mine)
        remote(part, part, ins.at[h, k, 0], cr.at[h, k, kind], {"mp": near}).wait_recv()

    def serve_keep(k):
        @pl.when(keeps)
        def _():
            remote(
                relay.at[k], relay.at[k], cs.at[k, 1], rr.at[k], {"mp": side}
            ).wait_recv()
            cross_high(k).start()

    def serve_cross(k):
        @pl.when(crosses)
        def _():
            own_wait(1, k)
            own_near(k).start()

    own_counts = [counts[z, j] for j in range(images)]
    own_plan = [plan[z, j] for j in range(images)]
    own_starts, running = [], 0
    for j in range(images):
        own_starts.append(running)
        running = running + own_counts[j]

    def span_of(dest):
        first, count = 0, 0
        for j in range(images):
            hit = (own_plan[j] == dest).astype(jnp.int32)
            first = first + hit * own_starts[j]
            count = count + hit * own_counts[j]
        return first, count

    pick_row = lax.broadcasted_iota(jnp.int32, (pair, 1), 0)
    pick_col = lax.broadcasted_iota(jnp.int32, (1, WINDOW), 1)
    base = slots // 16 * 16
    rest = slots - base

    def picker(dest):
        first, count = span_of(dest)
        low = lax.min(lax.div(first, 16), (base - WINDOW) // 16) * 16
        valid = pick_row < count
        chosen = jnp.logical_and(pick_col == pick_row + (first - low), valid).astype(bf16)
        ends = jnp.logical_and(pick_col[:, :16] == pick_row + (first - base), valid).astype(bf16)
        return pl.ds(low, WINDOW), chosen, ends, count

    def moved_rows(chosen, ends, body, end):
        part = jnp.dot(chosen, body, preferred_element_type=f32)
        return part + jnp.dot(ends, end, preferred_element_type=f32)

    heads = width // LANES
    q_gain = qg_ref[...]
    k_gain = kg_ref[...]
    scale = math.log2(math.e) / math.sqrt(LANES)
    key_at = lax.broadcasted_iota(jnp.int32, (1, pair), 1)

    loads[0].wait()
    end_qkv[...] = jnp.zeros(end_qkv.shape, bf16)
    if rest:
        end_qkv[:, pl.ds(0, rest), :] = raw[:, pl.ds(base, rest), :]

    def attend_block(dest):
        at_rows, chosen, ends, count = picker(dest)
        for part in range(3):
            blk[part] = moved_rows(
                chosen, ends, raw[part, at_rows, :], end_qkv[part]
            ).astype(bf16)
        seen = key_at < count
        real = pick_row < count
        line = sum_row == z * rows + dest

        for h in range(heads):
            at = pl.ds(h * LANES, LANES)
            scores = lax.dot_general(
                normed(blk[0, :, at], q_gain),
                normed(blk[1, :, at], k_gain),
                (((1,), (1,)), ((), ())),
                preferred_element_type=f32,
            )
            raised = jnp.where(seen, jnp.exp2(scores * scale), 0.0)
            total = jnp.sum(raised, axis=-1, keepdims=True)
            weights = (raised * (1.0 / total)).astype(bf16)
            result = jnp.dot(weights, blk[2, :, at], preferred_element_type=f32)
            result = result.astype(bf16)
            hx[block_at(dest), at] = result
            total = jnp.sum(jnp.where(real, result.astype(f32), 0.0), axis=0, keepdims=True)
            hsum[:, at] = jnp.where(line, total, hsum[:, at])

    group_lines = rows * rows
    sum_row = lax.broadcasted_iota(jnp.int32, (group_lines, 1), 0)
    hsum[...] = jnp.zeros(hsum.shape, f32)

    for k in range(rows):
        dest = jnp.where(keeps, order_a[k], order_c[k])
        attend_block(dest)

        @pl.when(keeps)
        def _(k=k):
            kb, e, at = gathered(core, 0, order_a[k])
            gath[kb, e, at, :] = hx[block_at(order_a[k]), :]
            if k < 2:
                own_side(k).start()
            else:

                @pl.when(outer)
                def _():
                    own_side(k).start()

            own_near(k).start()

        @pl.when(crosses)
        def _(k=k):
            cross_side(k).start()
            cross_low(k).start()

    def own_later(k):
        @pl.when(keeps)
        def _():
            own_side(k).start()

    collects = z == mp

    def hcopy():
        return remote(hsum, hrecv.at[z], hs.at[0], hr.at[z], {"dp": mp})

    def tcopy(k):
        peer = lax.rem(mp + k, 4)
        return remote(htot, htot, ts.at[k], tr.at[0], {"mp": peer})

    @pl.when(jnp.logical_not(collects))
    def _():
        hcopy().start()

    @pl.when(outer)
    def _():
        wzcopy(1).start()

    @pl.when(inner)
    def _():
        for t in range(early, tiles):
            wzcopy(t).start()

    loads[3].start()

    def collect_sums():
        @pl.when(collects)
        def _():
            total = hsum[...]
            for k in range(1, rows):
                source = lax.rem(z + k, rows)
                part = hrecv.at[source]
                remote(part, part, hs.at[0], hr.at[source], {"dp": source}).wait_recv()
                total = total + hrecv[source]
            htot[...] = total
            for k in range(1, 4):
                tcopy(k).start()

    def gcopy(kind):
        if kind == 0:
            return remote(lpart, lgot.at[0], gs.at[0], gr.at[0], {"dp": zp})
        if kind == 1:
            return remote(lpart, lgot.at[1], gs.at[0], gr.at[1], {"dp": zq})
        return remote(lpool, lgot.at[0], gs.at[1], gr.at[0], {"dp": zo})

    slot_at = lax.broadcasted_iota(jnp.int32, (1, slots), 1)

    def partial_sums():
        @pl.when(jnp.logical_not(collects))
        def _():
            remote(htot, htot, ts.at[1], tr.at[0], {"mp": near}).wait_recv()

        sums = htot[...]
        high = sums.astype(bf16)
        low = (sums - high.astype(f32)).astype(bf16)
        owner = jnp.full(slot_at.shape, -1, jnp.int32)
        for j in range(images):
            inside = jnp.logical_and(
                slot_at >= own_starts[j], slot_at < own_starts[j] + own_counts[j]
            )
            owner = jnp.where(inside, z * rows + own_plan[j], owner)
        member = (sum_row == owner).astype(bf16)

        def sum_tile(t):
            weights = wall[member_id, :, tile_at(t)]
            part = jnp.dot(high, weights, preferred_element_type=f32)
            part = part + jnp.dot(low, weights, preferred_element_type=f32)
            part = part + jnp.dot(member, resv[:, tile_at(t)], preferred_element_type=f32)
            lpart[:, tile_at(t)] = part

        repeat(tiles, sum_tile)

    loads[2].wait()
    end_resid[...] = jnp.zeros(end_resid.shape, bf16)
    if rest:
        end_resid[pl.ds(0, rest), :] = resv[pl.ds(base, rest), :]

    place_row = lax.broadcasted_iota(jnp.int32, (tokens, 1), 0)
    place_col = lax.broadcasted_iota(jnp.int32, (1, rows * pair), 1)

    def build_place(k):
        dest = order_a[k]
        begin = 0
        target = jnp.zeros(place_col.shape, jnp.int32)
        limit = jnp.zeros(place_col.shape, jnp.int32)
        for r in range(rows):
            count = 0
            for j in range(images):
                count = count + (plan[r, j] == dest).astype(jnp.int32) * counts[r, j]
            here = place_col >= r * pair
            target = jnp.where(here, place_col + (begin - r * pair), target)
            limit = jnp.where(here, r * pair + count, limit)
            begin = begin + count
        target = jnp.where(place_col < limit, target, -1)
        places[k] = (place_row == target).astype(bf16)

    zero_block = jnp.zeros((pair, cols), bf16)
    loads[1].wait()

    def project(k, t, count, chosen):
        at_rows, taken, ends, _ = chosen
        dest = order_a[k]
        used = pl.ds(0, count * pair)
        acc = jnp.dot(gath[0, dest, used, :], wall[0, :, tile_at(t)], preferred_element_type=f32)
        acc = acc + jnp.dot(
            gath[1, dest, used, :], wall[1, :, tile_at(t)], preferred_element_type=f32
        )
        for h in range(count):
            term = acc[h * pair : (h + 1) * pair]
            if h == 0:
                term = term + moved_rows(
                    taken, ends, resv[at_rows, tile_at(t)], end_resid[:, tile_at(t)]
                )
            zall[dest, block_at(homes[h]), tile_at(t)] = term.astype(bf16)

    def arrange(k, t):
        return jnp.dot(
            places[k], zall[order_a[k], :, tile_at(t)], preferred_element_type=f32
        )

    def xcopy(k, t):
        dest = order_a[k]
        part = zall.at[dest, block_at(zo), tile_at(t)]
        return remote(part, part, xs.at[k, t], xr.at[k, t], {"dp": zp})

    def xwait(k, t):
        dest = order_a[k]
        part = zall.at[dest, block_at(zo), tile_at(t)]
        remote(part, part, xs.at[k, t], xr.at[k, t], {"dp": zo}).wait_recv()

    def scopy(k, t):
        return remote(
            ssend.at[k, :, tile_at(t)],
            srecv.at[k, :, tile_at(t)],
            ss.at[k, t],
            sr.at[k, t],
            {"dp": zq},
        )

    def fcopy(t):
        return remote(
            fsend.at[:, tile_at(t)], srecv.at[0, :, tile_at(t)], fs.at[t], fr.at[t], {"dp": zo}
        )

    def ppeer(k):
        return lax.rem(z + k, rows)

    group_rows = lgs.shape[1]
    lines = images * group_rows
    classes = lwv.shape[1]

    def label_logits(source):
        loads[3].wait()
        line = lax.broadcasted_iota(jnp.int32, (lines, 1), 0)
        wanted = jnp.full((lines, 1), -1, jnp.int32)
        divisor = jnp.ones((group_lines, 1), f32)
        for r in range(rows):
            for j in range(images):
                row = r * rows + plan[r, j]
                wanted = jnp.where(line == j * group_rows + r, row, wanted)
                divisor = jnp.where(sum_row == row, counts[r, j].astype(f32), divisor)
        columns = lax.broadcasted_iota(jnp.int32, (lines, group_lines), 1)
        order = (columns == wanted).astype(bf16)
        pooled = (source[...] / divisor).astype(bf16)
        by_image = jnp.dot(order, pooled, preferred_element_type=f32).astype(bf16)

        def label_tile(t):
            part = jnp.dot(by_image, lwv[:, tile_at(t)], preferred_element_type=f32)
            for j in range(images):
                lgs[j, :, tile_at(t)] = part[j * group_rows : (j + 1) * group_rows]

        repeat(classes // TILE, label_tile)
        for k in range(1, 4):
            lcopy(k).start()

    def lcopy(k):
        peer = lax.rem(mp + k, 4)
        return remote(lgs.at[peer], lrecv.at[k], ls.at[k], lr.at[k], {"mp": peer})

    def bcopy(k):
        peer = ppeer(k)
        return remote(pbuf.at[peer], precv.at[z], bs.at[k], br.at[k], {"dp": peer})

    def label_probs():
        for k in range(1, 4):
            lcopy(k).wait_recv()
        total = lgs[mp]
        for k in range(1, 4):
            total = total + lrecv[k]
        probs = jax.nn.sigmoid(total + bias_ref[...])
        for r in range(rows):
            for t in range(classes // LANES):
                pbuf[r, pl.ds(t, 1), :] = probs[r : r + 1, t * LANES : (t + 1) * LANES]
        for k in range(1, rows):
            bcopy(k).start()

    @pl.when(outer)
    def _():
        forward_weight(0)
        serve_keep(0)
        serve_cross(0)
        serve_keep(1)
        forward_weight(1)
        for r in range(1, rows):
            zall[zo, block_at(lax.rem(z + r, rows)), :] = zero_block
        build_place(2)
        own_wait(0, 0)
        chosen = picker(order_a[0])
        after = {
            0: lambda: (serve_keep(2), serve_cross(1)),
            1: lambda: (serve_keep(3), serve_cross(2)),
            2: lambda: (serve_cross(3), collect_sums()),
        }
        for t in range(tiles):
            wait_weight(t)
            project(0, t, 1, chosen)
            xcopy(0, t).start()
            if t + 2 < tiles:
                wzcopy(t + 2).start()
                forward_weight(t + 2)
            if t in after:
                after[t]()
        partial_sums()
        gcopy(0).start()
        own_wait(0, 1)
        chosen = picker(order_a[1])

        def second_tile(t, chosen=chosen):
            project(1, t, 1, chosen)
            xcopy(1, t).start()

        repeat(tiles, second_tile)
        own_wait(0, 3)
        chosen = picker(order_a[3])

        def third_tile(t, chosen=chosen):
            project(3, t, 1, chosen)
            xcopy(3, t).start()

        repeat(tiles, third_tile)
        own_wait(0, 2)
        chosen = picker(order_a[2])

        def last_tile(t, chosen=chosen):
            project(2, t, 1, chosen)
            moved = arrange(2, t)
            fcopy(t).wait_recv()
            value = moved + srecv[0, :, tile_at(t)].astype(f32)
            out_ref[:, tile_at(t)] = value.astype(bf16)

        repeat(tiles, last_tile)
        gcopy(2).wait_recv()
        label_logits(lgot.at[0])
        label_probs()

    @pl.when(inner)
    def _():
        def arrive(k):
            for h in range(2):
                cross_wait(h, k, 0)
                cross_copy(h, k, 1).start()
                cross_copy(h, k, 0).start()

        def spread(k):
            for h in range(2):
                cross_wait(h, k, 2)
                cross_copy(h, k, 2).start()

        def settle(k):
            own_wait(0, k)
            for h in range(2):
                cross_wait(h, k, 1)
                cross_wait(h, k, 3)

        def send_sum(k, t, chosen):
            project(k, t, 3, chosen)
            xwait(k, t)
            ssend[k, :, tile_at(t)] = arrange(k, t).astype(bf16)
            scopy(k, t).start()

        forward_weight(0)
        serve_keep(0)
        serve_cross(0)
        arrive(0)
        serve_keep(1)
        forward_weight(1)
        arrive(1)
        serve_cross(1)
        own_later(2)
        serve_keep(2)
        serve_keep(3)
        zall[zo, block_at(zo), :] = zero_block
        for k in range(rows):
            build_place(k)
        spread(0)
        arrive(2)
        own_later(3)
        settle(0)
        chosen = [picker(order_a[k]) for k in range(rows)]

        def return_sum(t):
            project(2, t, 3, chosen[2])
            moved = arrange(2, t)
            scopy(0, t).wait_recv()
            value = moved + srecv[0, :, tile_at(t)].astype(f32)
            fsend[:, tile_at(t)] = value.astype(bf16)
            fcopy(t).start()

        after = {
            0: lambda: (spread(1), collect_sums(), arrive(3), forward_weight(2)),
            1: lambda: (forward_weight(3), serve_cross(2)),
            2: lambda: (forward_weight(4), spread(2)),
            3: lambda: (forward_weight(5), serve_cross(3), settle(2)),
            4: lambda: (return_sum(0), return_sum(1), spread(3)),
            5: lambda: (return_sum(2), settle(1)),
        }
        for t in range(tiles):
            wait_weight(t)
            send_sum(0, t, chosen[0])
            if t in after:
                after[t]()
        send_sum(1, 0, chosen[1])
        return_sum(3)
        send_sum(1, 1, chosen[1])
        return_sum(4)
        send_sum(1, 2, chosen[1])
        return_sum(5)
        partial_sums()
        gcopy(0).wait_recv()
        lpart[...] += lgot[0]
        gcopy(1).start()
        repeat(tiles - 3, lambda t: send_sum(1, t + 3, chosen[1]))
        gcopy(1).wait_recv()
        lpool[...] = lpart[...] + lgot[1]
        gcopy(2).start()
        label_logits(lpool)
        settle(3)

        def last_tile(t):
            project(3, t, 3, chosen[3])
            xwait(3, t)
            moved = arrange(3, t)
            scopy(1, t).wait_recv()
            value = moved + srecv[1, :, tile_at(t)].astype(f32)
            out_ref[:, tile_at(t)] = value.astype(bf16)

        half = tiles // 2
        repeat(half, last_tile)
        label_probs()
        repeat(tiles - half, lambda t: last_tile(t + half))

    for k in range(1, rows):
        part = precv.at[lax.rem(z + rows - k, rows)]
        remote(part, part, bs.at[k], br.at[k], {"dp": ppeer(k)}).wait_recv()
    precv[z] = pbuf[z]
    lab_ref[...] = precv[...]

    for k in range(rows):
        own_near(k).wait_send()

        @pl.when(keeps)
        def _(k=k):
            own_side(k).wait_send()
            cross_high(k).wait_send()

        @pl.when(crosses)
        def _(k=k):
            cross_low(k).wait_send()
            cross_side(k).wait_send()

        @pl.when(inner)
        def _(k=k):
            for h in range(2):
                for kind in range(3):
                    cross_copy(h, k, kind).wait_send()

    def close_tile(t):
        wzcopy(t).wait_send()
        wycopy(t).wait_send()

        @pl.when(outer)
        def _():
            for k in (0, 1, 3):
                xcopy(k, t).wait_send()

        @pl.when(inner)
        def _():
            for k in range(2):
                scopy(k, t).wait_send()
            fcopy(t).wait_send()

    repeat(tiles, close_tile)

    @pl.when(outer)
    def _():
        gcopy(0).wait_send()

    @pl.when(inner)
    def _():
        gcopy(1).wait_send()
        gcopy(2).wait_send()

    @pl.when(collects)
    def _():
        for k in range(1, 4):
            tcopy(k).wait_send()

    @pl.when(jnp.logical_not(collects))
    def _():
        hcopy().wait_send()

    for k in range(1, rows):
        bcopy(k).wait_send()
    for k in range(1, 4):
        lcopy(k).wait_send()


def round_up(value, step):
    return -(-value // step) * step


def fused(
    qkv_home,
    resid_home,
    out_weight,
    label_weight,
    label_bias,
    query_gain,
    key_gain,
    patch_counts,
    move_plan,
):
    rows = lax.axis_size("dp")
    slots, width = qkv_home.shape[1], qkv_home.shape[3]
    depth, cols = out_weight.shape
    classes = label_weight.shape[1]
    pair = round_up(slots // rows, 16)
    tiles = cols // TILE
    bf16, f32 = jnp.bfloat16, jnp.float32
    vmem = pl.BlockSpec(memory_space=pltpu.VMEM)
    smem = pl.BlockSpec(memory_space=pltpu.SMEM)
    hbm = pl.BlockSpec(memory_space=pl.ANY)
    dma = pltpu.SemaphoreType.DMA
    mixed, labels = pl.pallas_call(
        functools.partial(block_kernel, (rows, slots, pair)),
        out_shape=(
            jax.ShapeDtypeStruct((TOK, cols), bf16),
            jax.ShapeDtypeStruct((rows, classes // LANES, LANES), f32),
        ),
        in_specs=[smem, smem, vmem, vmem, vmem, hbm, hbm, hbm, hbm],
        out_specs=(vmem, vmem),
        scratch_shapes=[
            pltpu.VMEM((3, slots, width), bf16),
            pltpu.VMEM((3, pair, width), bf16),
            pltpu.VMEM((rows * pair, width), bf16),
            pltpu.VMEM((2, rows, 3 * pair, width), bf16),
            pltpu.VMEM((rows, pair, width // 2), bf16),
            pltpu.VMEM((2, depth, cols), bf16),
            pltpu.VMEM((slots, cols), bf16),
            pltpu.VMEM((3, 16, width), bf16),
            pltpu.VMEM((16, cols), bf16),
            pltpu.VMEM((rows, rows * pair, cols), bf16),
            pltpu.VMEM((rows, TOK, rows * pair), bf16),
            pltpu.VMEM((2, TOK, cols), bf16),
            pltpu.VMEM((2, TOK, cols), bf16),
            pltpu.VMEM((TOK, cols), bf16),
            pltpu.VMEM((rows * rows, width), f32),
            pltpu.VMEM((rows, rows * rows, width), f32),
            pltpu.VMEM((rows * rows, width), f32),
            pltpu.VMEM((rows * rows, cols), f32),
            pltpu.VMEM((2, rows * rows, cols), f32),
            pltpu.VMEM((rows * rows, cols), f32),
            pltpu.VMEM(label_weight.shape, bf16),
            pltpu.VMEM((rows, 8, classes), f32),
            pltpu.VMEM((4, 8, classes), f32),
            pltpu.VMEM((rows, classes // LANES, LANES), f32),
            pltpu.VMEM((rows, classes // LANES, LANES), f32),
            dma((4,)),
            dma((rows, 2)),
            dma((rows, 2)),
            dma((rows, 2)),
            dma((rows,)),
            dma((2, rows, 3)),
            dma((2, rows, 4)),
            dma((tiles,)),
            dma((tiles,)),
            dma((tiles,)),
            dma((tiles,)),
            dma((rows, tiles)),
            dma((rows, tiles)),
            dma((2, tiles)),
            dma((2, tiles)),
            dma((tiles,)),
            dma((tiles,)),
            dma((1,)),
            dma((rows,)),
            dma((4,)),
            dma((1,)),
            dma((2,)),
            dma((2,)),
            dma((4,)),
            dma((4,)),
            dma((rows,)),
            dma((rows,)),
        ],
        compiler_params=pltpu.CompilerParams(
            collective_id=0, has_side_effects=True, vmem_limit_bytes=63 * 1024 * 1024
        ),
    )(
        patch_counts,
        move_plan,
        label_bias[None],
        query_gain[None],
        key_gain[None],
        jnp.transpose(qkv_home[0], (1, 0, 2)),
        resid_home[0],
        out_weight,
        label_weight,
    )
    return (mixed[None], labels.reshape(1, 1, rows * classes))


def on_device(
    qkv_home,
    resid_home,
    out_weight,
    label_weight,
    label_bias,
    query_gain,
    key_gain,
    patch_counts,
    move_plan,
    segment_ids,
):
    row_count = lax.axis_size("dp")
    if row_count == lax.axis_size("mp") == 4 and lax.axis_size("groups") == 2:
        return fused(
            qkv_home,
            resid_home,
            out_weight,
            label_weight,
            label_bias,
            query_gain,
            key_gain,
            patch_counts,
            move_plan,
        )
    my_index = lax.axis_index("dp")
    home_slots = segment_ids.shape[1]
    pair_slots = home_slots // row_count
    image_ids = lax.broadcasted_iota(jnp.int32, (row_count, row_count, row_count), 2)
    image_ends = jnp.cumsum(patch_counts, axis=1)
    starts = image_ends - patch_counts
    matches = (move_plan[:, :, None] == image_ids).astype(jnp.int32)
    image_sizes = jnp.sum(patch_counts[:, :, None] * matches, axis=1)
    firsts = jnp.sum(starts[:, :, None] * matches, axis=1)
    send_sizes = lax.dynamic_index_in_dim(image_sizes, my_index, 0, keepdims=False)
    send_firsts = lax.dynamic_index_in_dim(firsts, my_index, 0, keepdims=False)
    within = lax.broadcasted_iota(jnp.int32, (row_count, pair_slots), 1)
    send_valid = within < send_sizes[:, None]
    send_index = jnp.minimum(send_firsts[:, None] + within, home_slots - 1).reshape(-1)
    arrive_sizes = lax.dynamic_index_in_dim(image_sizes, my_index, 1, keepdims=False)
    arrive_ends = jnp.cumsum(arrive_sizes)
    arrive_starts = arrive_ends - arrive_sizes
    slot_grid = lax.broadcasted_iota(jnp.int32, (TOK, row_count), 0)
    source = jnp.sum((slot_grid >= arrive_ends[None, :]).astype(jnp.int32), axis=1)
    chosen = (source[:, None] == lax.broadcasted_iota(jnp.int32, (TOK, row_count), 1)).astype(
        jnp.int32
    )
    arrive_index = (
        source * pair_slots + slot_grid[:, 0] - jnp.sum(chosen * arrive_starts[None, :], axis=1)
    )
    home_mixed = project(
        attend(qkv_home[0], segment_ids[0], query_gain, key_gain), resid_home[0], out_weight
    )
    count_row = lax.dynamic_index_in_dim(patch_counts, my_index, 0, keepdims=False)
    pooled = pool(home_mixed, segment_ids[0], count_row)
    partial_value = label_terms(pooled, label_weight)
    send_mixed = pick(home_mixed, send_index, send_valid)
    got_mixed = lax.all_to_all(send_mixed, "dp", split_axis=0, concat_axis=0, tiled=True)
    mixed = jnp.take(got_mixed.reshape(row_count * pair_slots, -1), arrive_index, axis=0)
    logit_sums = lax.psum_scatter(
        partial_value.astype(jnp.bfloat16), "mp", scatter_dimension=1, tiled=True
    ).astype(jnp.float32)
    class_probs = jax.nn.sigmoid(logit_sums + label_bias[None, None, :])
    labels = lax.all_to_all(
        class_probs.astype(jnp.bfloat16), "dp", split_axis=0, concat_axis=2, tiled=True
    ).astype(class_probs.dtype)
    return (mixed[None], labels)


def solution(mesh):
    return jax.shard_map(
        on_device,
        mesh=mesh,
        in_specs=(
            P(("groups", "dp"), None, None, "mp"),
            P(("groups", "dp"), None, "mp"),
            P("dp", "mp"),
            P("mp", "dp"),
            P("dp"),
            P(),
            P(),
            P("groups", None),
            P("groups", None),
            P(("groups", "dp"), None),
        ),
        out_specs=(P(("groups", "dp"), None, "mp"), P(("groups", "dp"), "mp", None)),
        check_vma=False,
    )
```

```python
import functools
import math

import jax
import jax.numpy as jnp
from jax import lax
from jax.experimental import pallas as pl
from jax.experimental.pallas import tpu as pltpu
from jax.sharding import PartitionSpec as P

TOK = 384


EPSILON = 1e-06


def head_norm(values, norm_gain):
    center = values - jnp.mean(values, axis=-1, keepdims=True)
    spread = jnp.mean(center * center, axis=-1, keepdims=True)
    return center * lax.rsqrt(spread + EPSILON) * norm_gain


def attend(qkv_rows, seg_rows, query_gain, key_gain):
    length = qkv_rows.shape[0]
    head_width = query_gain.shape[0]
    head_count = qkv_rows.shape[2] // head_width
    split_parts = qkv_rows.reshape(length, 3, head_count, head_width)
    queries = head_norm(split_parts[:, 0].astype(jnp.float32), query_gain).astype(jnp.bfloat16)
    key_rows = head_norm(split_parts[:, 1].astype(jnp.float32), key_gain).astype(jnp.bfloat16)
    scores = jnp.einsum(
        "qhd,khd->hqk", queries, key_rows, preferred_element_type=jnp.float32
    ) / math.sqrt(head_width)
    same_image = seg_rows[:, None] == seg_rows[None, :]
    raised = jnp.where(same_image[None], jnp.exp(scores), 0.0)
    weights = (raised / jnp.sum(raised, axis=-1, keepdims=True)).astype(jnp.bfloat16)
    head_out = jnp.einsum(
        "hqk,khd->qhd", weights, split_parts[:, 2], preferred_element_type=jnp.float32
    )
    return head_out.reshape(length, head_count * head_width).astype(jnp.bfloat16)


def project(heads_local, resid_rows, out_weight):
    gathered = lax.all_gather(heads_local, "mp", axis=1, tiled=True)
    running = resid_rows.astype(jnp.float32) + jnp.dot(
        gathered,
        lax.all_gather(out_weight, "dp", axis=0, tiled=True),
        preferred_element_type=jnp.float32,
    )
    return running.astype(jnp.bfloat16)


def pool(row_mixed, seg_rows, count_row):
    images = count_row.shape[0]
    member_ids = lax.broadcasted_iota(jnp.int32, (images, seg_rows.shape[0]), 0)
    member = (member_ids == seg_rows[None, :]).astype(jnp.bfloat16)
    image_sums = jnp.dot(member, row_mixed, preferred_element_type=jnp.float32)
    return (image_sums / count_row[:, None].astype(jnp.float32)).astype(jnp.bfloat16)


def label_terms(pooled, label_weight):
    return jnp.einsum(
        "abd,dc->abc",
        lax.all_gather(pooled[None], "dp", axis=0, tiled=True),
        label_weight,
        preferred_element_type=jnp.float32,
    )


def pick(values, row_index, is_valid):
    taken = jnp.take(values, row_index, axis=0)
    taken = taken.reshape(is_valid.shape + values.shape[1:])
    keep_mask = is_valid.reshape(is_valid.shape + (1,) * (values.ndim - 1))
    return jnp.where(keep_mask, taken, jnp.zeros_like(taken))


MESH = pl.DeviceIdType.MESH
LANES = 128
TILE = 256
WINDOW = 256
VMEM_LIMIT = 52 * 1024 * 1024


def remote(src, dst, send_sem, recv_sem, where):
    return pltpu.make_async_remote_copy(
        src_ref=src,
        dst_ref=dst,
        send_sem=send_sem,
        recv_sem=recv_sem,
        device_id=where,
        device_id_type=MESH,
    )


def call_all(work):
    work()


def normed(values, gain):
    values = values.astype(jnp.float32)
    center = values - jnp.mean(values, axis=-1, keepdims=True)
    spread = jnp.mean(center * center, axis=-1, keepdims=True)
    return (center * lax.rsqrt(spread + EPSILON) * gain).astype(jnp.bfloat16)


def block_kernel(
    sizes,
    counts_hbm,
    plan_hbm,
    bias_hbm,
    qg_hbm,
    kg_hbm,
    qkv_hbm,
    resid_hbm,
    w_hbm,
    lw_hbm,
    out_ref,
    lab_ref,
    counts,
    plan,
    bias_ref,
    qg_ref,
    kg_ref,
    picks,
    pick_ends,
    moved_buf,
    raw,
    blk,
    hx,
    gath,
    relay,
    wall,
    resv,
    end_qkv,
    end_resid,
    zall,
    places,
    ssend,
    srecv,
    fsend,
    hsum,
    hrecv,
    htot,
    lpart,
    lgot,
    lpool,
    lwv,
    lgs,
    lrecv,
    pbuf,
    precv,
    load_sem,
    os,
    orr,
    cs,
    rr,
    ins,
    cr,
    wzs,
    wzr,
    wys,
    wyr,
    xs,
    xr,
    ss,
    sr,
    fs,
    fr,
    hs,
    hr,
    ts,
    tr,
    gs,
    gr,
    ls,
    lr,
    bs,
    br,
):
    rows, slots, pair = sizes
    z = lax.axis_index("dp")
    mp = lax.axis_index("mp")
    group = lax.axis_index("groups")
    other = 1 - group
    core = lax.rem(mp, 2)
    xpos = mp // 2
    near = mp + 1 - 2 * core
    side = lax.rem(mp + 2, 4)
    half_id = z // 2
    member_id = z - 2 * half_id
    zo = 3 * half_id
    zp = 1 + half_id
    zq = 2 - half_id
    zo2 = 3 - 3 * half_id
    inner = z == zp
    outer = z == zo
    partner = zo + zp - z
    keeps = xpos == half_id
    crosses = xpos != half_id
    order_a = [zo2, zq, zo, zp]
    order_c = [zo, zp, zo2, zq]
    homes = [z, zq, zo2]
    width = raw.shape[2]
    split = width // 2
    depth, cols = w_hbm.shape
    tiles = cols // TILE
    images = rows
    tokens = out_ref.shape[0]
    bf16, f32 = jnp.bfloat16, jnp.float32

    loads = [
        pltpu.make_async_copy(qkv_hbm, raw, load_sem.at[0]),
        pltpu.make_async_copy(w_hbm, wall.at[member_id], load_sem.at[1]),
        pltpu.make_async_copy(resid_hbm, resv, load_sem.at[2]),
        pltpu.make_async_copy(lw_hbm, lwv, load_sem.at[3]),
    ]
    small = [
        pltpu.make_async_copy(counts_hbm, counts, load_sem.at[4]),
        pltpu.make_async_copy(plan_hbm, plan, load_sem.at[5]),
        pltpu.make_async_copy(qg_hbm, qg_ref, load_sem.at[6]),
        pltpu.make_async_copy(kg_hbm, kg_ref, load_sem.at[7]),
        pltpu.make_async_copy(bias_hbm, bias_ref, load_sem.at[8]),
    ]
    for load in small:
        load.start()
    loads[0].start()

    barrier = pltpu.get_barrier_semaphore()
    for k in range(1, 4):
        pl.semaphore_signal(
            barrier, inc=1, device_id={"mp": lax.rem(mp + k, 4)}, device_id_type=MESH
        )
    for k in range(1, rows):
        pl.semaphore_signal(
            barrier, inc=1, device_id={"dp": lax.rem(z + k, rows)}, device_id_type=MESH
        )
    pl.semaphore_signal(barrier, inc=1, device_id={"groups": other}, device_id_type=MESH)
    pl.semaphore_wait(barrier, 3 + rows - 1 + 1)

    def tile_at(t):
        return pl.ds(pl.multiple_of(t * TILE, TILE), TILE)

    def block_at(index):
        return pl.ds(pl.multiple_of(index * pair, pair), pair)

    def repeat(count, body):
        def step(t, carry):
            body(t)
            return carry

        lax.fori_loop(0, count, step, 0)

    def weight_part(which, part, t):
        size = depth // 2
        return wall.at[which, pl.ds(pl.multiple_of(part * size, size), size), tile_at(t)]

    def wzcopy(t):
        size = depth // 2
        own = w_hbm.at[pl.ds(pl.multiple_of(group * size, size), size), tile_at(t)]
        return remote(
            own, weight_part(member_id, group, t), wzs.at[t], wzr.at[t], {"dp": partner}
        )

    def wycopy(t):
        part = weight_part(1 - member_id, group, t)
        return remote(part, part, wys.at[t], wyr.at[t], {"groups": other})

    def forward_weight(t):
        part = weight_part(1 - member_id, group, t)
        remote(part, part, wys.at[t], wzr.at[t], {"groups": other}).wait_recv()
        wycopy(t).start()

    def wait_weight(t):
        part = weight_part(1 - member_id, other, t)
        remote(part, part, wys.at[t], wyr.at[t], {"groups": other}).wait_recv()

    early = tiles // 2
    wzcopy(0).start()

    @pl.when(inner)
    def _():
        for t in range(1, early):
            wzcopy(t).start()

    loads[1].start()
    loads[2].start()

    def gathered(which, home, dest):
        return which, dest, pl.ds(pl.multiple_of(home * pair, pair), pair)

    def own_piece(which, k):
        kb, e, at = gathered(which, 0, order_a[k])
        return gath.at[kb, e, at, :]

    def own_near(k):
        part = own_piece(core, k)
        return remote(part, part, os.at[k, 0], orr.at[k, 0], {"mp": near})

    def own_side(k):
        part = own_piece(core, k)
        return remote(part, part, os.at[k, 1], orr.at[k, 1], {"mp": side})

    def own_wait(kind, k):
        part = own_piece(core if kind else 1 - core, k)
        remote(part, part, os.at[k, kind], orr.at[k, kind], {"mp": near}).wait_recv()

    def half_at(which):
        return pl.ds(pl.multiple_of(which * split, LANES), split)

    there = jnp.where(outer, 2, 1)

    def cross_low(k):
        dest = order_c[k]
        kb, e, at = gathered(core, there, dest)
        return remote(
            hx.at[block_at(dest), pl.ds(0, split)],
            gath.at[kb, e, at, pl.ds(0, split)],
            cs.at[k, 0],
            cr.at[there - 1, k, 0],
            {"dp": zq},
        )

    def cross_side(k):
        dest = order_c[k]
        return remote(
            hx.at[block_at(dest), pl.ds(split, split)],
            relay.at[k],
            cs.at[k, 1],
            rr.at[k],
            {"mp": side},
        )

    def cross_high(k):
        kb, e, at = gathered(core, there, order_c[k])
        return remote(
            relay.at[k],
            gath.at[kb, e, at, pl.ds(split, split)],
            cs.at[k, 0],
            cr.at[there - 1, k, 0],
            {"dp": zq},
        )

    mine = jnp.where(keeps, 0, 1)

    def cross_piece(h, k, which, part):
        kb, e, at = gathered(which, h + 1, order_a[k])
        return gath.at[kb, e, at, half_at(part)]

    def cross_copy(h, k, kind):
        part = cross_piece(h, k, core, 1 - mine if kind == 2 else mine)
        target = side if kind == 1 else near
        return remote(part, part, ins.at[h, k, kind], cr.at[h, k, kind + 1], {"mp": target})

    def cross_wait(h, k, kind):
        which = core if kind in (0, 2) else 1 - core
        part = cross_piece(h, k, which, mine if kind < 2 else 1 - mine)
        remote(part, part, ins.at[h, k, 0], cr.at[h, k, kind], {"mp": near}).wait_recv()

    def serve_keep(k):
        @pl.when(keeps)
        def _():
            remote(
                relay.at[k], relay.at[k], cs.at[k, 1], rr.at[k], {"mp": side}
            ).wait_recv()
            cross_high(k).start()

    def serve_cross(k):
        @pl.when(crosses)
        def _():
            own_wait(1, k)
            own_near(k).start()

    for load in small:
        load.wait()
    own_counts = [counts[z, j] for j in range(images)]
    own_plan = [plan[z, j] for j in range(images)]
    own_starts, running = [], 0
    for j in range(images):
        own_starts.append(running)
        running = running + own_counts[j]

    def span_of(dest):
        first, count = 0, 0
        for j in range(images):
            hit = (own_plan[j] == dest).astype(jnp.int32)
            first = first + hit * own_starts[j]
            count = count + hit * own_counts[j]
        return first, count

    pick_row = lax.broadcasted_iota(jnp.int32, (pair, 1), 0)
    pick_col = lax.broadcasted_iota(jnp.int32, (1, WINDOW), 1)
    base = slots // 16 * 16
    rest = slots - base

    def window(first):
        return lax.min(lax.div(first, 16), (base - WINDOW) // 16) * 16

    def picker(dest):
        first, count = span_of(dest)
        low = window(first)
        valid = pick_row < count
        chosen = jnp.logical_and(pick_col == pick_row + (first - low), valid).astype(bf16)
        ends = jnp.logical_and(pick_col[:, :16] == pick_row + (first - base), valid).astype(bf16)
        return pl.ds(low, WINDOW), chosen, ends, count

    def moved_rows(chosen, ends, body, end):
        part = jnp.dot(chosen, body, preferred_element_type=f32)
        return part + jnp.dot(ends, end, preferred_element_type=f32)

    heads = width // LANES
    q_gain = qg_ref[...]
    k_gain = kg_ref[...]
    scale = math.log2(math.e) / math.sqrt(LANES)
    key_at = lax.broadcasted_iota(jnp.int32, (1, pair), 1)

    loads[0].wait()
    end_qkv[...] = jnp.zeros(end_qkv.shape, bf16)
    if rest:
        end_qkv[:, pl.ds(0, rest), :] = raw[:, pl.ds(base, rest), :]

    def attend_block(dest):
        at_rows, chosen, ends, count = picker(dest)
        for part in range(3):
            blk[part] = moved_rows(
                chosen, ends, raw[part, at_rows, :], end_qkv[part]
            ).astype(bf16)
        picks[dest] = chosen
        pick_ends[dest] = ends
        seen = key_at < count
        real = pick_row < count
        line = sum_row == z * rows + dest

        for h in range(heads):
            at = pl.ds(h * LANES, LANES)
            scores = lax.dot_general(
                normed(blk[0, :, at], q_gain),
                normed(blk[1, :, at], k_gain),
                (((1,), (1,)), ((), ())),
                preferred_element_type=f32,
            )
            raised = jnp.where(seen, jnp.exp2(scores * scale), 0.0)
            total = jnp.sum(raised, axis=-1, keepdims=True)
            weights = (raised * (1.0 / total)).astype(bf16)
            result = jnp.dot(weights, blk[2, :, at], preferred_element_type=f32)
            result = result.astype(bf16)
            hx[block_at(dest), at] = result
            total = jnp.sum(jnp.where(real, result.astype(f32), 0.0), axis=0, keepdims=True)
            hsum[:, at] = jnp.where(line, total, hsum[:, at])

    group_lines = rows * rows
    sum_row = lax.broadcasted_iota(jnp.int32, (group_lines, 1), 0)
    hsum[...] = jnp.zeros(hsum.shape, f32)

    for k in range(rows):
        dest = jnp.where(keeps, order_a[k], order_c[k])
        attend_block(dest)

        @pl.when(keeps)
        def _(k=k):
            kb, e, at = gathered(core, 0, order_a[k])
            gath[kb, e, at, :] = hx[block_at(order_a[k]), :]
            if k < 1:
                own_side(k).start()
            else:

                @pl.when(outer)
                def _():
                    own_side(k).start()

            own_near(k).start()

        @pl.when(crosses)
        def _(k=k):
            cross_side(k).start()
            if k == 0:
                cross_low(k).start()
            if k == 1:

                @pl.when(inner)
                def _():
                    cross_low(k).start()

    def cross_later(k):
        serve_keep(k)

        @pl.when(crosses)
        def _():
            cross_low(k).start()

    def own_later(k):
        @pl.when(keeps)
        def _():
            own_side(k).start()

    collects = z == mp

    def hcopy():
        return remote(hsum, hrecv.at[z], hs.at[0], hr.at[z], {"dp": mp})

    def tcopy(k):
        peer = lax.rem(mp + k, 4)
        return remote(htot, htot, ts.at[k], tr.at[0], {"mp": peer})

    @pl.when(jnp.logical_not(collects))
    def _():
        hcopy().start()

    @pl.when(outer)
    def _():
        wzcopy(1).start()

    @pl.when(inner)
    def _():
        for t in range(early, tiles):
            wzcopy(t).start()

    loads[3].start()

    def collect_sums():
        @pl.when(collects)
        def _():
            total = hsum[...]
            for k in range(1, rows):
                source = lax.rem(z + k, rows)
                part = hrecv.at[source]
                remote(part, part, hs.at[0], hr.at[source], {"dp": source}).wait_recv()
                total = total + hrecv[source]
            htot[...] = total
            for k in range(1, 4):
                tcopy(k).start()

    def gcopy(kind):
        if kind == 0:
            return remote(lpart, lgot.at[0], gs.at[0], gr.at[0], {"dp": zp})
        if kind == 1:
            return remote(lpart, lgot.at[1], gs.at[0], gr.at[1], {"dp": zq})
        return remote(lpool, lgot.at[0], gs.at[1], gr.at[0], {"dp": zo})

    slot_at = lax.broadcasted_iota(jnp.int32, (1, slots), 1)

    def partial_sums():
        @pl.when(jnp.logical_not(collects))
        def _():
            remote(htot, htot, ts.at[1], tr.at[0], {"mp": near}).wait_recv()

        sums = htot[...]
        high = sums.astype(bf16)
        low = (sums - high.astype(f32)).astype(bf16)
        owner = jnp.full(slot_at.shape, -1, jnp.int32)
        for j in range(images):
            inside = jnp.logical_and(
                slot_at >= own_starts[j], slot_at < own_starts[j] + own_counts[j]
            )
            owner = jnp.where(inside, z * rows + own_plan[j], owner)
        member = (sum_row == owner).astype(bf16)

        def sum_tile(t):
            weights = wall[member_id, :, tile_at(t)]
            part = jnp.dot(high, weights, preferred_element_type=f32)
            part = part + jnp.dot(low, weights, preferred_element_type=f32)
            part = part + jnp.dot(member, resv[:, tile_at(t)], preferred_element_type=f32)
            lpart[:, tile_at(t)] = part

        repeat(tiles, sum_tile)

    loads[2].wait()
    end_resid[...] = jnp.zeros(end_resid.shape, bf16)
    if rest:
        end_resid[pl.ds(0, rest), :] = resv[pl.ds(base, rest), :]

    place_row = lax.broadcasted_iota(jnp.int32, (tokens, 1), 0)
    place_col = lax.broadcasted_iota(jnp.int32, (1, rows * pair), 1)

    def build_place(k):
        dest = order_a[k]
        begin = 0
        target = jnp.zeros(place_col.shape, jnp.int32)
        limit = jnp.zeros(place_col.shape, jnp.int32)
        for r in range(rows):
            count = 0
            for j in range(images):
                count = count + (plan[r, j] == dest).astype(jnp.int32) * counts[r, j]
            here = place_col >= r * pair
            target = jnp.where(here, place_col + (begin - r * pair), target)
            limit = jnp.where(here, r * pair + count, limit)
            begin = begin + count
        target = jnp.where(place_col < limit, target, -1)
        places[k] = (place_row == target).astype(bf16)

    zero_block = jnp.zeros((pair, cols), bf16)
    loads[1].wait()

    def project(dest, t, count):
        at_rows = pl.ds(window(span_of(dest)[0]), WINDOW)
        used = pl.ds(0, count * pair)
        acc = jnp.dot(gath[0, dest, used, :], wall[0, :, tile_at(t)], preferred_element_type=f32)
        acc = acc + jnp.dot(
            gath[1, dest, used, :], wall[1, :, tile_at(t)], preferred_element_type=f32
        )
        for h in range(count):
            term = acc[h * pair : (h + 1) * pair]
            if h == 0:
                term = term + moved_rows(
                    picks[dest],
                    pick_ends[dest],
                    resv[at_rows, tile_at(t)],
                    end_resid[:, tile_at(t)],
                )
            zall[dest, block_at(homes[h]), tile_at(t)] = term.astype(bf16)

    def dest_of(k):
        if isinstance(k, int):
            return order_a[k]
        low = jnp.where(k == 0, order_a[0], order_a[1])
        return jnp.where(k < 2, low, jnp.where(k == 2, order_a[2], order_a[3]))

    def arrange(k, t):
        return jnp.dot(
            places[k], zall[dest_of(k), :, tile_at(t)], preferred_element_type=f32
        )

    def xcopy(k, t):
        dest = dest_of(k)
        part = zall.at[dest, block_at(zo), tile_at(t)]
        return remote(part, part, xs.at[k, t], xr.at[k, t], {"dp": zp})

    def xwait(k, t):
        dest = dest_of(k)
        part = zall.at[dest, block_at(zo), tile_at(t)]
        remote(part, part, xs.at[k, t], xr.at[k, t], {"dp": zo}).wait_recv()

    def scopy(k, t):
        return remote(
            ssend.at[k, :, tile_at(t)],
            srecv.at[k, :, tile_at(t)],
            ss.at[k, t],
            sr.at[k, t],
            {"dp": zq},
        )

    def fcopy(t):
        return remote(
            fsend.at[:, tile_at(t)], srecv.at[0, :, tile_at(t)], fs.at[t], fr.at[t], {"dp": zo}
        )

    def ppeer(k):
        return lax.rem(z + k, rows)

    group_rows = lgs.shape[1]
    lines = images * group_rows
    classes = lwv.shape[1]

    def label_logits(source):
        loads[3].wait()
        line = lax.broadcasted_iota(jnp.int32, (lines, 1), 0)
        wanted = jnp.full((lines, 1), -1, jnp.int32)
        divisor = jnp.ones((group_lines, 1), f32)
        for r in range(rows):
            for j in range(images):
                row = r * rows + plan[r, j]
                wanted = jnp.where(line == j * group_rows + r, row, wanted)
                divisor = jnp.where(sum_row == row, counts[r, j].astype(f32), divisor)
        columns = lax.broadcasted_iota(jnp.int32, (lines, group_lines), 1)
        order = (columns == wanted).astype(bf16)
        pooled = (source[...] / divisor).astype(bf16)
        by_image = jnp.dot(order, pooled, preferred_element_type=f32).astype(bf16)

        def label_tile(t):
            part = jnp.dot(by_image, lwv[:, tile_at(t)], preferred_element_type=f32)
            for j in range(images):
                lgs[j, :, tile_at(t)] = part[j * group_rows : (j + 1) * group_rows]

        repeat(classes // TILE, label_tile)
        for k in range(1, 4):
            lcopy(k).start()

    def lcopy(k):
        peer = lax.rem(mp + k, 4)
        return remote(lgs.at[peer], lrecv.at[k], ls.at[k], lr.at[k], {"mp": peer})

    def bcopy(k):
        peer = ppeer(k)
        return remote(pbuf.at[peer], precv.at[z], bs.at[k], br.at[k], {"dp": peer})

    def label_probs():
        for k in range(1, 4):
            lcopy(k).wait_recv()
        total = lgs[mp]
        for k in range(1, 4):
            total = total + lrecv[k]
        probs = jax.nn.sigmoid(total + bias_ref[...])
        for r in range(rows):
            for t in range(classes // LANES):
                pbuf[r, pl.ds(t, 1), :] = probs[r : r + 1, t * LANES : (t + 1) * LANES]
        for k in range(1, rows):
            bcopy(k).start()

    @pl.when(outer)
    def _():
        forward_weight(0)
        serve_keep(0)
        serve_cross(0)
        forward_weight(1)
        for r in range(1, rows):
            zall[zo, block_at(lax.rem(z + r, rows)), :] = zero_block
        build_place(2)
        own_wait(0, 0)
        after = {
            0: lambda: serve_cross(1),
            1: lambda: (cross_later(1), serve_cross(2)),
            2: lambda: serve_cross(3),
            3: lambda: (cross_later(2), collect_sums()),
        }

        def first_tile(t):
            wait_weight(t)
            project(order_a[0], t, 1)
            xcopy(0, t).start()

            @pl.when(t + 2 < tiles)
            def _():
                wzcopy(t + 2).start()
                forward_weight(t + 2)

            for step, work in after.items():
                pl.when(t == step)(functools.partial(call_all, work))

        repeat(tiles, first_tile)
        partial_sums()
        gcopy(0).start()
        own_wait(0, 1)
        half = tiles // 2

        def second_tile(t):
            project(order_a[1], t, 1)
            xcopy(1, t).start()

            @pl.when(t == half)
            def _():
                cross_later(3)

        repeat(tiles, second_tile)
        own_wait(0, 3)

        def third_tile(t):
            project(order_a[3], t, 1)
            xcopy(3, t).start()

        repeat(tiles, third_tile)
        own_wait(0, 2)

        def labels_ready():
            gcopy(2).wait_recv()
            label_logits(lgot.at[0])

        after_last = {half: labels_ready, tiles - 2: label_probs}

        def last_tile(t):
            project(order_a[2], t, 1)
            moved = arrange(2, t)
            fcopy(t).wait_recv()
            value = moved + srecv[0, :, tile_at(t)].astype(f32)
            out_ref[:, tile_at(t)] = value.astype(bf16)
            for step, work in after_last.items():
                pl.when(t == step)(functools.partial(call_all, work))

        repeat(tiles, last_tile)

    @pl.when(inner)
    def _():
        def arrive(k):
            for h in range(2):
                cross_wait(h, k, 0)
                cross_copy(h, k, 1).start()
                cross_copy(h, k, 0).start()

        def spread(k):
            for h in range(2):
                cross_wait(h, k, 2)
                cross_copy(h, k, 2).start()

        def settle(k):
            own_wait(0, k)
            for h in range(2):
                cross_wait(h, k, 1)
                cross_wait(h, k, 3)

        forward_weight(0)
        serve_keep(0)
        serve_cross(0)
        serve_keep(1)
        arrive(0)
        own_later(1)
        cross_later(2)
        cross_later(3)
        zall[zo, block_at(zo), :] = zero_block
        for k in range(rows):
            build_place(k)
        forward_weight(1)
        spread(0)
        settle(0)

        def add_sums():
            gcopy(0).wait_recv()
            lpart[...] += lgot[0]
            gcopy(1).start()

        def labels_ready():
            gcopy(1).wait_recv()
            lpool[...] = lpart[...] + lgot[1]
            gcopy(2).start()
            label_logits(lpool)

        ones = [(1, t) for t in range(tiles)]
        twos = [(2, t) for t in range(tiles)]
        plan_of = [(0, t) for t in range(tiles - 1)] + twos[:2] + [(0, tiles - 1)]
        for t in range(tiles - 2):
            plan_of += [ones[t], twos[t + 2]]
        plan_of += ones[tiles - 2 :]
        ends_at = len(plan_of) - 1
        plan_of += [(3, t) for t in range(tiles)]

        after = {
            0: lambda: forward_weight(2),
            1: lambda: (forward_weight(3), collect_sums(), serve_cross(1)),
            2: lambda: (own_later(2), arrive(1), forward_weight(4)),
            3: lambda: (spread(1), partial_sums(), forward_weight(5), arrive(2)),
            4: lambda: (own_later(3), spread(2), serve_cross(2), settle(2)),
            6: lambda: settle(1),
            11: lambda: (add_sums(), serve_cross(3)),
            14: lambda: arrive(3),
            ends_at: lambda: (labels_ready(), spread(3), settle(3)),
            ends_at + 3: label_probs,
        }

        def step_tile(u):
            k, t = 0, 0
            for i, (k_i, t_i) in enumerate(plan_of):
                here = (u == i).astype(jnp.int32)
                k = k + k_i * here
                t = t + t_i * here

            @pl.when(k == 0)
            def _():
                wait_weight(t)

            project(dest_of(k), t, 3)

            @pl.when(k != 2)
            def _():
                xwait(k, t)

            moved_buf[...] = arrange(k, t)

            @pl.when(k < 2)
            def _():
                ssend[k, :, tile_at(t)] = moved_buf[...].astype(bf16)
                scopy(k, t).start()

            @pl.when(k == 2)
            def _():
                scopy(0, t).wait_recv()
                value = moved_buf[...] + srecv[0, :, tile_at(t)].astype(f32)
                fsend[:, tile_at(t)] = value.astype(bf16)
                fcopy(t).start()

            @pl.when(k == 3)
            def _():
                scopy(1, t).wait_recv()
                value = moved_buf[...] + srecv[1, :, tile_at(t)].astype(f32)
                out_ref[:, tile_at(t)] = value.astype(bf16)

            for step, work in after.items():
                pl.when(u == step)(functools.partial(call_all, work))

        repeat(len(plan_of), step_tile)

    for k in range(1, rows):
        part = precv.at[lax.rem(z + rows - k, rows)]
        remote(part, part, bs.at[k], br.at[k], {"dp": ppeer(k)}).wait_recv()
    precv[z] = pbuf[z]
    lab_ref[...] = precv[...]

    for k in range(rows):
        own_near(k).wait_send()

        @pl.when(keeps)
        def _(k=k):
            own_side(k).wait_send()
            cross_high(k).wait_send()

        @pl.when(crosses)
        def _(k=k):
            cross_low(k).wait_send()
            cross_side(k).wait_send()

        @pl.when(inner)
        def _(k=k):
            for h in range(2):
                for kind in range(3):
                    cross_copy(h, k, kind).wait_send()

    def close_tile(t):
        wzcopy(t).wait_send()
        wycopy(t).wait_send()

        @pl.when(outer)
        def _():
            for k in (0, 1, 3):
                xcopy(k, t).wait_send()

        @pl.when(inner)
        def _():
            for k in range(2):
                scopy(k, t).wait_send()
            fcopy(t).wait_send()

    repeat(tiles, close_tile)

    @pl.when(outer)
    def _():
        gcopy(0).wait_send()

    @pl.when(inner)
    def _():
        gcopy(1).wait_send()
        gcopy(2).wait_send()

    @pl.when(collects)
    def _():
        for k in range(1, 4):
            tcopy(k).wait_send()

    @pl.when(jnp.logical_not(collects))
    def _():
        hcopy().wait_send()

    for k in range(1, rows):
        bcopy(k).wait_send()
    for k in range(1, 4):
        lcopy(k).wait_send()


def round_up(value, step):
    return -(-value // step) * step


def fused(
    qkv_home,
    resid_home,
    out_weight,
    label_weight,
    label_bias,
    query_gain,
    key_gain,
    patch_counts,
    move_plan,
):
    rows = lax.axis_size("dp")
    slots, width = qkv_home.shape[1], qkv_home.shape[3]
    depth, cols = out_weight.shape
    classes = label_weight.shape[1]
    pair = round_up(slots // rows, 16)
    tiles = cols // TILE
    bf16, f32 = jnp.bfloat16, jnp.float32
    vmem = pl.BlockSpec(memory_space=pltpu.VMEM)
    hbm = pl.BlockSpec(memory_space=pltpu.HBM)
    dma = pltpu.SemaphoreType.DMA

    def keep(value):
        return pltpu.with_memory_space_constraint(value, pltpu.HBM)

    mixed, labels = pl.pallas_call(
        functools.partial(block_kernel, (rows, slots, pair)),
        out_shape=(
            jax.ShapeDtypeStruct((TOK, cols), bf16),
            jax.ShapeDtypeStruct((rows, classes // LANES, LANES), f32),
        ),
        in_specs=[hbm] * 9,
        out_specs=(vmem, vmem),
        scratch_shapes=[
            pltpu.SMEM(patch_counts.shape, jnp.int32),
            pltpu.SMEM(move_plan.shape, jnp.int32),
            pltpu.VMEM((1, classes), f32),
            pltpu.VMEM((1, LANES), f32),
            pltpu.VMEM((1, LANES), f32),
            pltpu.VMEM((rows, pair, WINDOW), bf16),
            pltpu.VMEM((rows, pair, 16), bf16),
            pltpu.VMEM((TOK, TILE), f32),
            pltpu.VMEM((3, slots, width), bf16),
            pltpu.VMEM((3, pair, width), bf16),
            pltpu.VMEM((rows * pair, width), bf16),
            pltpu.VMEM((2, rows, 3 * pair, width), bf16),
            pltpu.VMEM((rows, pair, width // 2), bf16),
            pltpu.VMEM((2, depth, cols), bf16),
            pltpu.VMEM((slots, cols), bf16),
            pltpu.VMEM((3, 16, width), bf16),
            pltpu.VMEM((16, cols), bf16),
            pltpu.VMEM((rows, rows * pair, cols), bf16),
            pltpu.VMEM((rows, TOK, rows * pair), bf16),
            pltpu.VMEM((2, TOK, cols), bf16),
            pltpu.VMEM((2, TOK, cols), bf16),
            pltpu.VMEM((TOK, cols), bf16),
            pltpu.VMEM((rows * rows, width), f32),
            pltpu.VMEM((rows, rows * rows, width), f32),
            pltpu.VMEM((rows * rows, width), f32),
            pltpu.VMEM((rows * rows, cols), f32),
            pltpu.VMEM((2, rows * rows, cols), f32),
            pltpu.VMEM((rows * rows, cols), f32),
            pltpu.VMEM(label_weight.shape, bf16),
            pltpu.VMEM((rows, 8, classes), f32),
            pltpu.VMEM((4, 8, classes), f32),
            pltpu.VMEM((rows, classes // LANES, LANES), f32),
            pltpu.VMEM((rows, classes // LANES, LANES), f32),
            dma((9,)),
            dma((rows, 2)),
            dma((rows, 2)),
            dma((rows, 2)),
            dma((rows,)),
            dma((2, rows, 3)),
            dma((2, rows, 4)),
            dma((tiles,)),
            dma((tiles,)),
            dma((tiles,)),
            dma((tiles,)),
            dma((rows, tiles)),
            dma((rows, tiles)),
            dma((2, tiles)),
            dma((2, tiles)),
            dma((tiles,)),
            dma((tiles,)),
            dma((1,)),
            dma((rows,)),
            dma((4,)),
            dma((1,)),
            dma((2,)),
            dma((2,)),
            dma((4,)),
            dma((4,)),
            dma((rows,)),
            dma((rows,)),
        ],
        compiler_params=pltpu.CompilerParams(
            collective_id=0, has_side_effects=True, vmem_limit_bytes=VMEM_LIMIT
        ),
    )(
        keep(patch_counts),
        keep(move_plan),
        keep(label_bias[None]),
        keep(query_gain[None]),
        keep(key_gain[None]),
        jnp.transpose(qkv_home[0], (1, 0, 2)),
        resid_home[0],
        out_weight,
        label_weight,
    )
    return (mixed[None], labels.reshape(1, 1, rows * classes))


def on_device(
    qkv_home,
    resid_home,
    out_weight,
    label_weight,
    label_bias,
    query_gain,
    key_gain,
    patch_counts,
    move_plan,
    segment_ids,
):
    row_count = lax.axis_size("dp")
    if row_count == lax.axis_size("mp") == 4 and lax.axis_size("groups") == 2:
        return fused(
            qkv_home,
            resid_home,
            out_weight,
            label_weight,
            label_bias,
            query_gain,
            key_gain,
            patch_counts,
            move_plan,
        )
    my_index = lax.axis_index("dp")
    home_slots = segment_ids.shape[1]
    pair_slots = home_slots // row_count
    image_ids = lax.broadcasted_iota(jnp.int32, (row_count, row_count, row_count), 2)
    image_ends = jnp.cumsum(patch_counts, axis=1)
    starts = image_ends - patch_counts
    matches = (move_plan[:, :, None] == image_ids).astype(jnp.int32)
    image_sizes = jnp.sum(patch_counts[:, :, None] * matches, axis=1)
    firsts = jnp.sum(starts[:, :, None] * matches, axis=1)
    send_sizes = lax.dynamic_index_in_dim(image_sizes, my_index, 0, keepdims=False)
    send_firsts = lax.dynamic_index_in_dim(firsts, my_index, 0, keepdims=False)
    within = lax.broadcasted_iota(jnp.int32, (row_count, pair_slots), 1)
    send_valid = within < send_sizes[:, None]
    send_index = jnp.minimum(send_firsts[:, None] + within, home_slots - 1).reshape(-1)
    arrive_sizes = lax.dynamic_index_in_dim(image_sizes, my_index, 1, keepdims=False)
    arrive_ends = jnp.cumsum(arrive_sizes)
    arrive_starts = arrive_ends - arrive_sizes
    slot_grid = lax.broadcasted_iota(jnp.int32, (TOK, row_count), 0)
    source = jnp.sum((slot_grid >= arrive_ends[None, :]).astype(jnp.int32), axis=1)
    chosen = (source[:, None] == lax.broadcasted_iota(jnp.int32, (TOK, row_count), 1)).astype(
        jnp.int32
    )
    arrive_index = (
        source * pair_slots + slot_grid[:, 0] - jnp.sum(chosen * arrive_starts[None, :], axis=1)
    )
    home_mixed = project(
        attend(qkv_home[0], segment_ids[0], query_gain, key_gain), resid_home[0], out_weight
    )
    count_row = lax.dynamic_index_in_dim(patch_counts, my_index, 0, keepdims=False)
    pooled = pool(home_mixed, segment_ids[0], count_row)
    partial_value = label_terms(pooled, label_weight)
    send_mixed = pick(home_mixed, send_index, send_valid)
    got_mixed = lax.all_to_all(send_mixed, "dp", split_axis=0, concat_axis=0, tiled=True)
    mixed = jnp.take(got_mixed.reshape(row_count * pair_slots, -1), arrive_index, axis=0)
    logit_sums = lax.psum_scatter(
        partial_value.astype(jnp.bfloat16), "mp", scatter_dimension=1, tiled=True
    ).astype(jnp.float32)
    class_probs = jax.nn.sigmoid(logit_sums + label_bias[None, None, :])
    labels = lax.all_to_all(
        class_probs.astype(jnp.bfloat16), "dp", split_axis=0, concat_axis=2, tiled=True
    ).astype(class_probs.dtype)
    return (mixed[None], labels)


def solution(mesh):
    return jax.shard_map(
        on_device,
        mesh=mesh,
        in_specs=(
            P(("groups", "dp"), None, None, "mp"),
            P(("groups", "dp"), None, "mp"),
            P("dp", "mp"),
            P("mp", "dp"),
            P("dp"),
            P(),
            P(),
            P("groups", None),
            P("groups", None),
            P(("groups", "dp"), None),
        ),
        out_specs=(P(("groups", "dp"), None, "mp"), P(("groups", "dp"), "mp", None)),
        check_vma=False,
    )
```

```python
import functools
import math

import jax
import jax.numpy as jnp
from jax import lax
from jax.experimental import pallas as pl
from jax.experimental.pallas import tpu as pltpu
from jax.sharding import PartitionSpec as P

TOK = 384


EPSILON = 1e-06


def head_norm(values, norm_gain):
    center = values - jnp.mean(values, axis=-1, keepdims=True)
    spread = jnp.mean(center * center, axis=-1, keepdims=True)
    return center * lax.rsqrt(spread + EPSILON) * norm_gain


def attend(qkv_rows, seg_rows, query_gain, key_gain):
    length = qkv_rows.shape[0]
    head_width = query_gain.shape[0]
    head_count = qkv_rows.shape[2] // head_width
    split_parts = qkv_rows.reshape(length, 3, head_count, head_width)
    queries = head_norm(split_parts[:, 0].astype(jnp.float32), query_gain).astype(jnp.bfloat16)
    key_rows = head_norm(split_parts[:, 1].astype(jnp.float32), key_gain).astype(jnp.bfloat16)
    scores = jnp.einsum(
        "qhd,khd->hqk", queries, key_rows, preferred_element_type=jnp.float32
    ) / math.sqrt(head_width)
    same_image = seg_rows[:, None] == seg_rows[None, :]
    raised = jnp.where(same_image[None], jnp.exp(scores), 0.0)
    weights = (raised / jnp.sum(raised, axis=-1, keepdims=True)).astype(jnp.bfloat16)
    head_out = jnp.einsum(
        "hqk,khd->qhd", weights, split_parts[:, 2], preferred_element_type=jnp.float32
    )
    return head_out.reshape(length, head_count * head_width).astype(jnp.bfloat16)


def project(heads_local, resid_rows, out_weight):
    gathered = lax.all_gather(heads_local, "mp", axis=1, tiled=True)
    running = resid_rows.astype(jnp.float32) + jnp.dot(
        gathered,
        lax.all_gather(out_weight, "dp", axis=0, tiled=True),
        preferred_element_type=jnp.float32,
    )
    return running.astype(jnp.bfloat16)


def pool(row_mixed, seg_rows, count_row):
    images = count_row.shape[0]
    member_ids = lax.broadcasted_iota(jnp.int32, (images, seg_rows.shape[0]), 0)
    member = (member_ids == seg_rows[None, :]).astype(jnp.bfloat16)
    image_sums = jnp.dot(member, row_mixed, preferred_element_type=jnp.float32)
    return (image_sums / count_row[:, None].astype(jnp.float32)).astype(jnp.bfloat16)


def label_terms(pooled, label_weight):
    return jnp.einsum(
        "abd,dc->abc",
        lax.all_gather(pooled[None], "dp", axis=0, tiled=True),
        label_weight,
        preferred_element_type=jnp.float32,
    )


def pick(values, row_index, is_valid):
    taken = jnp.take(values, row_index, axis=0)
    taken = taken.reshape(is_valid.shape + values.shape[1:])
    keep_mask = is_valid.reshape(is_valid.shape + (1,) * (values.ndim - 1))
    return jnp.where(keep_mask, taken, jnp.zeros_like(taken))


MESH = pl.DeviceIdType.MESH
LANES = 128
TILE = 256
WINDOW = 256
VMEM_LIMIT = 52 * 1024 * 1024


def remote(src, dst, send_sem, recv_sem, where):
    return pltpu.make_async_remote_copy(
        src_ref=src,
        dst_ref=dst,
        send_sem=send_sem,
        recv_sem=recv_sem,
        device_id=where,
        device_id_type=MESH,
    )


def call_all(work):
    work()


def normed(values, gain):
    values = values.astype(jnp.float32)
    center = values - jnp.mean(values, axis=-1, keepdims=True)
    spread = jnp.mean(center * center, axis=-1, keepdims=True)
    return (center * lax.rsqrt(spread + EPSILON) * gain).astype(jnp.bfloat16)


def block_kernel(
    sizes,
    counts_hbm,
    plan_hbm,
    bias_hbm,
    qg_hbm,
    kg_hbm,
    qkv_hbm,
    resid_hbm,
    w_hbm,
    lw_hbm,
    out_ref,
    lab_ref,
    counts,
    plan,
    bias_ref,
    qg_ref,
    kg_ref,
    picks,
    pick_ends,
    rest_picks,
    rest_ends,
    xplaces,
    packed,
    raw,
    blk,
    hx,
    gath,
    relay,
    wall,
    resv,
    end_qkv,
    end_resid,
    xall,
    places,
    obuf,
    srecv,
    hsum,
    hrecv,
    htot,
    lpart,
    lgot,
    lpool,
    lwv,
    lgs,
    lrecv,
    pbuf,
    precv,
    load_sem,
    os,
    orr,
    cs,
    rr,
    ins,
    cr,
    wzs,
    wzr,
    wys,
    wyr,
    xs,
    xr,
    ss,
    sr,
    fs,
    fr,
    hs,
    hr,
    ts,
    tr,
    gs,
    gr,
    ls,
    lr,
    bs,
    br,
):
    rows, slots, pair = sizes
    z = lax.axis_index("dp")
    mp = lax.axis_index("mp")
    group = lax.axis_index("groups")
    other = 1 - group
    core = lax.rem(mp, 2)
    xpos = mp // 2
    near = mp + 1 - 2 * core
    side = lax.rem(mp + 2, 4)
    half_id = z // 2
    member_id = z - 2 * half_id
    zo = 3 * half_id
    zp = 1 + half_id
    zq = 2 - half_id
    zo2 = 3 - 3 * half_id
    inner = z == zp
    outer = z == zo
    partner = zo + zp - z
    keeps = xpos == half_id
    crosses = xpos != half_id
    order_a = [zo2, zq, zo, zp]
    order_c = [zo, zp, zo2, zq]
    homes = [z, zq, zo2]
    width = raw.shape[2]
    split = width // 2
    depth, cols = w_hbm.shape
    tiles = cols // TILE
    images = rows
    tokens = out_ref.shape[0]
    bf16, f32 = jnp.bfloat16, jnp.float32

    loads = [
        pltpu.make_async_copy(qkv_hbm, raw, load_sem.at[0]),
        pltpu.make_async_copy(w_hbm, wall.at[member_id], load_sem.at[1]),
        pltpu.make_async_copy(resid_hbm, resv, load_sem.at[2]),
        pltpu.make_async_copy(lw_hbm, lwv, load_sem.at[3]),
    ]
    small = [
        pltpu.make_async_copy(counts_hbm, counts, load_sem.at[4]),
        pltpu.make_async_copy(plan_hbm, plan, load_sem.at[5]),
        pltpu.make_async_copy(qg_hbm, qg_ref, load_sem.at[6]),
        pltpu.make_async_copy(kg_hbm, kg_ref, load_sem.at[7]),
        pltpu.make_async_copy(bias_hbm, bias_ref, load_sem.at[8]),
    ]
    for load in small:
        load.start()
    loads[0].start()

    barrier = pltpu.get_barrier_semaphore()
    for k in range(1, 4):
        pl.semaphore_signal(
            barrier, inc=1, device_id={"mp": lax.rem(mp + k, 4)}, device_id_type=MESH
        )
    for k in range(1, rows):
        pl.semaphore_signal(
            barrier, inc=1, device_id={"dp": lax.rem(z + k, rows)}, device_id_type=MESH
        )
    pl.semaphore_signal(barrier, inc=1, device_id={"groups": other}, device_id_type=MESH)
    pl.semaphore_wait(barrier, 3 + rows - 1 + 1)

    def tile_at(t):
        return pl.ds(pl.multiple_of(t * TILE, TILE), TILE)

    def block_at(index):
        return pl.ds(pl.multiple_of(index * pair, pair), pair)

    def repeat(count, body):
        def step(t, carry):
            body(t)
            return carry

        lax.fori_loop(0, count, step, 0)

    def weight_part(which, part, t):
        size = depth // 2
        return wall.at[which, pl.ds(pl.multiple_of(part * size, size), size), tile_at(t)]

    def wzcopy(t):
        size = depth // 2
        own = w_hbm.at[pl.ds(pl.multiple_of(group * size, size), size), tile_at(t)]
        return remote(
            own, weight_part(member_id, group, t), wzs.at[t], wzr.at[t], {"dp": partner}
        )

    def wycopy(t):
        part = weight_part(1 - member_id, group, t)
        return remote(part, part, wys.at[t], wyr.at[t], {"groups": other})

    def forward_weight(t):
        part = weight_part(1 - member_id, group, t)
        remote(part, part, wys.at[t], wzr.at[t], {"groups": other}).wait_recv()
        wycopy(t).start()

    def wait_weight(t):
        part = weight_part(1 - member_id, other, t)
        remote(part, part, wys.at[t], wyr.at[t], {"groups": other}).wait_recv()

    early = tiles // 2
    wzcopy(0).start()

    @pl.when(inner)
    def _():
        for t in range(1, early):
            wzcopy(t).start()

    loads[1].start()
    loads[2].start()

    def gathered(which, home, dest):
        return which, dest, pl.ds(pl.multiple_of(home * pair, pair), pair)

    def own_piece(which, k):
        kb, e, at = gathered(which, 0, order_a[k])
        return gath.at[kb, e, at, :]

    def own_near(k):
        part = own_piece(core, k)
        return remote(part, part, os.at[k, 0], orr.at[k, 0], {"mp": near})

    def own_side(k):
        part = own_piece(core, k)
        return remote(part, part, os.at[k, 1], orr.at[k, 1], {"mp": side})

    def own_wait(kind, k):
        part = own_piece(core if kind else 1 - core, k)
        remote(part, part, os.at[k, kind], orr.at[k, kind], {"mp": near}).wait_recv()

    def half_at(which):
        return pl.ds(pl.multiple_of(which * split, LANES), split)

    there = jnp.where(outer, 2, 1)

    def cross_low(k):
        dest = order_c[k]
        kb, e, at = gathered(core, there, dest)
        return remote(
            hx.at[block_at(dest), pl.ds(0, split)],
            gath.at[kb, e, at, pl.ds(0, split)],
            cs.at[k, 0],
            cr.at[there - 1, k, 0],
            {"dp": zq},
        )

    def cross_side(k):
        dest = order_c[k]
        return remote(
            hx.at[block_at(dest), pl.ds(split, split)],
            relay.at[k],
            cs.at[k, 1],
            rr.at[k],
            {"mp": side},
        )

    def cross_high(k):
        kb, e, at = gathered(core, there, order_c[k])
        return remote(
            relay.at[k],
            gath.at[kb, e, at, pl.ds(split, split)],
            cs.at[k, 0],
            cr.at[there - 1, k, 0],
            {"dp": zq},
        )

    mine = jnp.where(keeps, 0, 1)

    def cross_piece(h, k, which, part):
        kb, e, at = gathered(which, h + 1, order_a[k])
        return gath.at[kb, e, at, half_at(part)]

    def cross_copy(h, k, kind):
        part = cross_piece(h, k, core, 1 - mine if kind == 2 else mine)
        target = side if kind == 1 else near
        return remote(part, part, ins.at[h, k, kind], cr.at[h, k, kind + 1], {"mp": target})

    def cross_wait(h, k, kind):
        which = core if kind in (0, 2) else 1 - core
        part = cross_piece(h, k, which, mine if kind < 2 else 1 - mine)
        remote(part, part, ins.at[h, k, 0], cr.at[h, k, kind], {"mp": near}).wait_recv()

    def serve_keep(k):
        @pl.when(keeps)
        def _():
            remote(
                relay.at[k], relay.at[k], cs.at[k, 1], rr.at[k], {"mp": side}
            ).wait_recv()
            cross_high(k).start()

    def serve_cross(k):
        @pl.when(crosses)
        def _():
            own_wait(1, k)
            own_near(k).start()

    for load in small:
        load.wait()
    own_counts = [counts[z, j] for j in range(images)]
    own_plan = [plan[z, j] for j in range(images)]
    own_starts, running = [], 0
    for j in range(images):
        own_starts.append(running)
        running = running + own_counts[j]

    def span_of(dest):
        first, count = 0, 0
        for j in range(images):
            hit = (own_plan[j] == dest).astype(jnp.int32)
            first = first + hit * own_starts[j]
            count = count + hit * own_counts[j]
        return first, count

    pick_row = lax.broadcasted_iota(jnp.int32, (pair, 1), 0)
    pick_col = lax.broadcasted_iota(jnp.int32, (1, WINDOW), 1)
    base = slots // 16 * 16
    rest = slots - base

    def window(first):
        return lax.min(lax.div(first, 16), (base - WINDOW) // 16) * 16

    def picker(dest):
        first, count = span_of(dest)
        low = window(first)
        valid = pick_row < count
        chosen = jnp.logical_and(pick_col == pick_row + (first - low), valid).astype(bf16)
        ends = jnp.logical_and(pick_col[:, :16] == pick_row + (first - base), valid).astype(bf16)
        return pl.ds(low, WINDOW), chosen, ends, count

    def moved_rows(chosen, ends, body, end):
        part = jnp.dot(chosen, body, preferred_element_type=f32)
        return part + jnp.dot(ends, end, preferred_element_type=f32)

    heads = width // LANES
    q_gain = qg_ref[...]
    k_gain = kg_ref[...]
    scale = math.log2(math.e) / math.sqrt(LANES)
    key_at = lax.broadcasted_iota(jnp.int32, (1, pair), 1)

    loads[0].wait()
    end_qkv[...] = jnp.zeros(end_qkv.shape, bf16)
    if rest:
        end_qkv[:, pl.ds(0, rest), :] = raw[:, pl.ds(base, rest), :]

    def attend_block(dest):
        at_rows, chosen, ends, count = picker(dest)
        for part in range(3):
            blk[part] = moved_rows(
                chosen, ends, raw[part, at_rows, :], end_qkv[part]
            ).astype(bf16)
        picks[dest] = chosen
        pick_ends[dest] = ends
        seen = key_at < count
        real = pick_row < count
        line = own_row == dest

        for h in range(heads):
            at = pl.ds(h * LANES, LANES)
            scores = lax.dot_general(
                normed(blk[0, :, at], q_gain),
                normed(blk[1, :, at], k_gain),
                (((1,), (1,)), ((), ())),
                preferred_element_type=f32,
            )
            raised = jnp.where(seen, jnp.exp2(scores * scale), 0.0)
            total = jnp.sum(raised, axis=-1, keepdims=True)
            weights = (raised * (1.0 / total)).astype(bf16)
            result = jnp.dot(weights, blk[2, :, at], preferred_element_type=f32)
            result = result.astype(bf16)
            hx[block_at(dest), at] = result
            total = jnp.sum(jnp.where(real, result.astype(f32), 0.0), axis=0, keepdims=True)
            hsum[:, at] = jnp.where(line, total, hsum[:, at])

    group_lines = rows * rows
    sum_row = lax.broadcasted_iota(jnp.int32, (group_lines, 1), 0)
    own_row = lax.broadcasted_iota(jnp.int32, (8, 1), 0)
    wide_col = lax.broadcasted_iota(jnp.int32, (1, 8 * rows), 1)
    hsum[...] = jnp.zeros(hsum.shape, f32)

    for k in range(rows):
        dest = jnp.where(keeps, order_a[k], order_c[k])
        attend_block(dest)

        @pl.when(keeps)
        def _(k=k):
            kb, e, at = gathered(core, 0, order_a[k])
            gath[kb, e, at, :] = hx[block_at(order_a[k]), :]
            if k < 1:
                own_side(k).start()
            else:

                @pl.when(outer)
                def _():
                    own_side(k).start()

            own_near(k).start()

        @pl.when(crosses)
        def _(k=k):
            cross_side(k).start()
            if k == 0:
                cross_low(k).start()
            if k == 1:

                @pl.when(outer)
                def _():
                    cross_low(k).start()

    def cross_later(k):
        serve_keep(k)

        @pl.when(crosses)
        def _():
            cross_low(k).start()

    def own_later(k):
        @pl.when(keeps)
        def _():
            own_side(k).start()

    collects = z == mp

    def hcopy():
        return remote(hsum, hrecv.at[z], hs.at[0], hr.at[z], {"dp": mp})

    def tcopy(k):
        peer = lax.rem(mp + k, 4)
        return remote(htot, htot, ts.at[k], tr.at[0], {"mp": peer})

    @pl.when(jnp.logical_not(collects))
    def _():
        hcopy().start()

    @pl.when(inner)
    def _():
        for t in range(early, tiles):
            wzcopy(t).start()

    loads[3].start()

    def collect_sums():
        @pl.when(collects)
        def _():
            htot[z] = hsum[...]
            for k in range(1, rows):
                source = lax.rem(z + k, rows)
                part = hrecv.at[source]
                remote(part, part, hs.at[0], hr.at[source], {"dp": source}).wait_recv()
                htot[source] = hrecv[source]
            for k in range(1, 4):
                tcopy(k).start()

    def gcopy(kind):
        if kind == 0:
            return remote(lpart, lgot.at[0], gs.at[0], gr.at[0], {"dp": zp})
        if kind == 1:
            return remote(lpart, lgot.at[1], gs.at[0], gr.at[1], {"dp": zq})
        return remote(lpool, lgot.at[0], gs.at[1], gr.at[0], {"dp": zo})

    slot_at = lax.broadcasted_iota(jnp.int32, (1, slots), 1)

    def partial_sums():
        @pl.when(jnp.logical_not(collects))
        def _():
            remote(htot, htot, ts.at[1], tr.at[0], {"mp": near}).wait_recv()

        sums = htot[...].reshape(8 * rows, width)
        high = sums.astype(bf16)
        low = (sums - high.astype(f32)).astype(bf16)
        squeeze = (wide_col == sum_row // rows * 8 + lax.rem(sum_row, rows)).astype(bf16)
        high = jnp.dot(squeeze, high, preferred_element_type=f32).astype(bf16)
        low = jnp.dot(squeeze, low, preferred_element_type=f32).astype(bf16)
        owner = jnp.full(slot_at.shape, -1, jnp.int32)
        for j in range(images):
            inside = jnp.logical_and(
                slot_at >= own_starts[j], slot_at < own_starts[j] + own_counts[j]
            )
            owner = jnp.where(inside, z * rows + own_plan[j], owner)
        member = (sum_row == owner).astype(bf16)

        def sum_tile(t):
            weights = wall[member_id, :, tile_at(t)]
            part = jnp.dot(high, weights, preferred_element_type=f32)
            part = part + jnp.dot(low, weights, preferred_element_type=f32)
            part = part + jnp.dot(member, resv[:, tile_at(t)], preferred_element_type=f32)
            lpart[:, tile_at(t)] = part

        repeat(tiles, sum_tile)

    loads[2].wait()
    end_resid[...] = jnp.zeros(end_resid.shape, bf16)
    if rest:
        end_resid[pl.ds(0, rest), :] = resv[pl.ds(base, rest), :]

    place_row = lax.broadcasted_iota(jnp.int32, (tokens, 1), 0)
    place_col = lax.broadcasted_iota(jnp.int32, (1, 3 * pair), 1)

    def choose(values, index):
        total = 0
        for i, value in enumerate(values):
            total = total + (index == i).astype(jnp.int32) * value
        return total

    def spans_to(dest):
        begins, sizes, begin = [], [], 0
        for r in range(rows):
            count = 0
            for j in range(images):
                count = count + (plan[r, j] == dest).astype(jnp.int32) * counts[r, j]
            begins.append(begin)
            sizes.append(count)
            begin = begin + count
        return begins, sizes

    def build_cross(k):
        begins, sizes = spans_to(order_a[k])
        at = place_col[:, :pair]
        target = jnp.where(at < choose(sizes, zo), at + choose(begins, zo), -1)
        xplaces[k] = (place_row == target).astype(bf16)

    def build_place(k):
        dest = order_a[k]
        begins, sizes = spans_to(dest)
        target = jnp.full(place_col.shape, -1, jnp.int32)
        for h in range(3):
            at = place_col - h * pair
            inside = jnp.logical_and(at >= 0, at < choose(sizes, homes[h]))
            target = jnp.where(inside, at + choose(begins, homes[h]), target)
        places[k] = (place_row == target).astype(bf16)
        first, count = span_of(dest)
        begin = choose(begins, z)
        for ref, low, columns in (
            (rest_picks, window(first), pick_col),
            (rest_ends, base, pick_col[:, :16]),
        ):
            at = columns + (low - first)
            inside = jnp.logical_and(at >= 0, at < count)
            ref[k] = (place_row == jnp.where(inside, at + begin, -1)).astype(bf16)

    loads[1].wait()

    def project(dest, t):
        at_rows = pl.ds(window(span_of(dest)[0]), WINDOW)
        used = pl.ds(0, pair)
        term = jnp.dot(gath[0, dest, used, :], wall[0, :, tile_at(t)], preferred_element_type=f32)
        term = term + jnp.dot(
            gath[1, dest, used, :], wall[1, :, tile_at(t)], preferred_element_type=f32
        )
        term = term + moved_rows(
            picks[dest], pick_ends[dest], resv[at_rows, tile_at(t)], end_resid[:, tile_at(t)]
        )
        xall[dest, :, tile_at(t)] = term.astype(bf16)

    def dest_of(k):
        if isinstance(k, int):
            return order_a[k]
        low = jnp.where(k == 0, order_a[0], order_a[1])
        return jnp.where(k < 2, low, jnp.where(k == 2, order_a[2], order_a[3]))

    def compact(k):
        dest = order_a[k]
        for which in range(2):

            def pack_tile(t, which=which):
                part = jnp.dot(
                    places[k], gath[which, dest, :, tile_at(t)], preferred_element_type=f32
                )
                packed[k, which, :, tile_at(t)] = part.astype(bf16)

            repeat(width // TILE, pack_tile)

    def xcopy(k, t):
        dest = dest_of(k)
        part = xall.at[dest, :, tile_at(t)]
        return remote(part, part, xs.at[k, t], xr.at[k, t], {"dp": zp})

    def xwait(k, t):
        dest = dest_of(k)
        part = xall.at[dest, :, tile_at(t)]
        remote(part, part, xs.at[k, t], xr.at[k, t], {"dp": zo}).wait_recv()

    def scopy(k, t):
        return remote(
            obuf.at[k, :, tile_at(t)],
            srecv.at[k, :, tile_at(t)],
            ss.at[k, t],
            sr.at[k, t],
            {"dp": zq},
        )

    def fcopy(t):
        return remote(
            obuf.at[2, :, tile_at(t)], srecv.at[0, :, tile_at(t)], fs.at[t], fr.at[t], {"dp": zo}
        )

    def ppeer(k):
        return lax.rem(z + k, rows)

    group_rows = lgs.shape[1]
    lines = images * group_rows
    classes = lwv.shape[1]

    def label_logits(source):
        loads[3].wait()
        line = lax.broadcasted_iota(jnp.int32, (lines, 1), 0)
        wanted = jnp.full((lines, 1), -1, jnp.int32)
        divisor = jnp.ones((group_lines, 1), f32)
        for r in range(rows):
            for j in range(images):
                row = r * rows + plan[r, j]
                wanted = jnp.where(line == j * group_rows + r, row, wanted)
                divisor = jnp.where(sum_row == row, counts[r, j].astype(f32), divisor)
        columns = lax.broadcasted_iota(jnp.int32, (lines, group_lines), 1)
        order = (columns == wanted).astype(bf16)
        pooled = (source[...] / divisor).astype(bf16)
        by_image = jnp.dot(order, pooled, preferred_element_type=f32).astype(bf16)

        def label_tile(t):
            part = jnp.dot(by_image, lwv[:, tile_at(t)], preferred_element_type=f32)
            for j in range(images):
                lgs[j, :, tile_at(t)] = part[j * group_rows : (j + 1) * group_rows]

        repeat(classes // TILE, label_tile)
        for k in range(1, 4):
            lcopy(k).start()

    def lcopy(k):
        peer = lax.rem(mp + k, 4)
        return remote(lgs.at[peer], lrecv.at[k], ls.at[k], lr.at[k], {"mp": peer})

    def bcopy(k):
        peer = ppeer(k)
        return remote(pbuf.at[peer], precv.at[z], bs.at[k], br.at[k], {"dp": peer})

    def label_probs():
        for k in range(1, 4):
            lcopy(k).wait_recv()
        total = lgs[mp]
        for k in range(1, 4):
            total = total + lrecv[k]
        probs = jax.nn.sigmoid(total + bias_ref[...])
        for r in range(rows):
            for t in range(classes // LANES):
                pbuf[r, pl.ds(t, 1), :] = probs[r : r + 1, t * LANES : (t + 1) * LANES]
        for k in range(1, rows):
            bcopy(k).start()

    @pl.when(outer)
    def _():
        serve_keep(0)
        wzcopy(1).start()
        forward_weight(0)
        serve_cross(0)
        serve_keep(1)
        forward_weight(1)
        build_cross(2)
        own_wait(0, 0)

        def send_sums():
            partial_sums()
            gcopy(0).start()

        after = {
            0: lambda: serve_cross(1),
            1: lambda: (cross_later(2), serve_cross(2), collect_sums()),
            2: send_sums,
            3: lambda: serve_cross(3),
        }

        def first_tile(t):
            wait_weight(t)
            project(order_a[0], t)
            xcopy(0, t).start()

            @pl.when(t + 2 < tiles)
            def _():
                wzcopy(t + 2).start()
                forward_weight(t + 2)

            for step, work in after.items():
                pl.when(t == step)(functools.partial(call_all, work))

        repeat(tiles, first_tile)
        own_wait(0, 1)
        half = tiles // 2

        def second_tile(t):
            project(order_a[1], t)
            xcopy(1, t).start()

            @pl.when(t == half)
            def _():
                cross_later(3)

        repeat(tiles, second_tile)
        own_wait(0, 3)

        def third_tile(t):
            project(order_a[3], t)
            xcopy(3, t).start()

        repeat(tiles, third_tile)
        own_wait(0, 2)

        gcopy(2).wait_recv()
        label_logits(lgot.at[0])
        label_probs()

        def last_tile(t):
            project(order_a[2], t)
            moved = jnp.dot(xplaces[2], xall[zo, :, tile_at(t)], preferred_element_type=f32)
            fcopy(t).wait_recv()
            value = moved + srecv[0, :, tile_at(t)].astype(f32)
            out_ref[:, tile_at(t)] = value.astype(bf16)

        repeat(tiles, last_tile)

    @pl.when(inner)
    def _():
        def arrive(k):
            for h in range(2):
                cross_wait(h, k, 0)
                cross_copy(h, k, 1).start()
                cross_copy(h, k, 0).start()

        def spread(k):
            for h in range(2):
                cross_wait(h, k, 2)
                cross_copy(h, k, 2).start()

        def settle(k):
            own_wait(0, k)
            for h in range(2):
                cross_wait(h, k, 1)
                cross_wait(h, k, 3)

        forward_weight(0)
        serve_keep(0)
        serve_cross(0)
        arrive(0)
        own_later(1)
        cross_later(1)
        cross_later(2)
        cross_later(3)
        xall[zo] = jnp.zeros((pair, cols), bf16)
        srecv[2] = jnp.zeros((tokens, cols), bf16)
        for k in range(rows):
            build_place(k)
            build_cross(k)
        forward_weight(1)
        spread(0)
        settle(0)
        compact(0)

        def add_sums():
            gcopy(0).wait_recv()
            lpart[...] += lgot[0]
            gcopy(1).start()

        def total_sums():
            gcopy(1).wait_recv()
            lpool[...] = lpart[...] + lgot[1]
            gcopy(2).start()

        plan_of = [(0, t) for t in range(tiles)]
        for t in range(tiles):
            plan_of += [(1, t), (2, t)]
        ends_at = len(plan_of) - 1
        plan_of += [(3, t) for t in range(tiles)]

        after = {
            0: lambda: (forward_weight(2), collect_sums()),
            1: lambda: (arrive(1), own_later(2), partial_sums(), serve_cross(1), forward_weight(3)),
            2: lambda: (spread(1), forward_weight(4)),
            3: lambda: (arrive(2), own_later(3), settle(1), compact(1), forward_weight(5)),
            4: lambda: (add_sums(), serve_cross(2), spread(2)),
            6: lambda: (settle(2), compact(2)),
            8: total_sums,
            10: lambda: label_logits(lpool),
            12: lambda: serve_cross(3),
            14: lambda: (label_probs(), arrive(3)),
            ends_at: lambda: (spread(3), settle(3), compact(3)),
        }

        def step_tile(u):
            k, t = 0, 0
            for i, (k_i, t_i) in enumerate(plan_of):
                here = (u == i).astype(jnp.int32)
                k = k + k_i * here
                t = t + t_i * here

            @pl.when(k == 0)
            def _():
                wait_weight(t)

            @pl.when(k != 2)
            def _():
                xwait(k, t)

            @pl.when(k >= 2)
            def _():
                scopy(k - 2, t).wait_recv()

            dest = dest_of(k)
            at_rows = pl.ds(window(span_of(dest)[0]), WINDOW)
            value = jnp.dot(packed[k, 0], wall[0, :, tile_at(t)], preferred_element_type=f32)
            value = value + jnp.dot(
                packed[k, 1], wall[1, :, tile_at(t)], preferred_element_type=f32
            )
            value = value + jnp.dot(
                rest_picks[k], resv[at_rows, tile_at(t)], preferred_element_type=f32
            )
            value = value + jnp.dot(
                rest_ends[k], end_resid[:, tile_at(t)], preferred_element_type=f32
            )
            value = value + jnp.dot(
                xplaces[k], xall[dest, :, tile_at(t)], preferred_element_type=f32
            )
            got = jnp.where(k < 2, 2, k - 2)
            value = value + srecv[got, :, tile_at(t)].astype(f32)
            obuf[k, :, tile_at(t)] = value.astype(bf16)

            @pl.when(k < 2)
            def _():
                scopy(k, t).start()

            @pl.when(k == 2)
            def _():
                fcopy(t).start()

            @pl.when(k == 3)
            def _():
                out_ref[:, tile_at(t)] = obuf[3, :, tile_at(t)]

            for step, work in after.items():
                pl.when(u == step)(functools.partial(call_all, work))

        repeat(len(plan_of), step_tile)

    for k in range(1, rows):
        part = precv.at[lax.rem(z + rows - k, rows)]
        remote(part, part, bs.at[k], br.at[k], {"dp": ppeer(k)}).wait_recv()
    precv[z] = pbuf[z]
    lab_ref[...] = precv[...]

    for k in range(rows):
        own_near(k).wait_send()

        @pl.when(keeps)
        def _(k=k):
            own_side(k).wait_send()
            cross_high(k).wait_send()

        @pl.when(crosses)
        def _(k=k):
            cross_low(k).wait_send()
            cross_side(k).wait_send()

        @pl.when(inner)
        def _(k=k):
            for h in range(2):
                for kind in range(3):
                    cross_copy(h, k, kind).wait_send()

    def close_tile(t):
        wzcopy(t).wait_send()
        wycopy(t).wait_send()

        @pl.when(outer)
        def _():
            for k in (0, 1, 3):
                xcopy(k, t).wait_send()

        @pl.when(inner)
        def _():
            for k in range(2):
                scopy(k, t).wait_send()
            fcopy(t).wait_send()

    repeat(tiles, close_tile)

    @pl.when(outer)
    def _():
        gcopy(0).wait_send()

    @pl.when(inner)
    def _():
        gcopy(1).wait_send()
        gcopy(2).wait_send()

    @pl.when(collects)
    def _():
        for k in range(1, 4):
            tcopy(k).wait_send()

    @pl.when(jnp.logical_not(collects))
    def _():
        hcopy().wait_send()

    for k in range(1, rows):
        bcopy(k).wait_send()
    for k in range(1, 4):
        lcopy(k).wait_send()


def round_up(value, step):
    return -(-value // step) * step


def fused(
    qkv_home,
    resid_home,
    out_weight,
    label_weight,
    label_bias,
    query_gain,
    key_gain,
    patch_counts,
    move_plan,
):
    rows = lax.axis_size("dp")
    slots, width = qkv_home.shape[1], qkv_home.shape[3]
    depth, cols = out_weight.shape
    classes = label_weight.shape[1]
    pair = round_up(slots // rows, 16)
    tiles = cols // TILE
    bf16, f32 = jnp.bfloat16, jnp.float32
    vmem = pl.BlockSpec(memory_space=pltpu.VMEM)
    hbm = pl.BlockSpec(memory_space=pltpu.HBM)
    dma = pltpu.SemaphoreType.DMA

    def keep(value):
        return pltpu.with_memory_space_constraint(value, pltpu.HBM)

    mixed, labels = pl.pallas_call(
        functools.partial(block_kernel, (rows, slots, pair)),
        out_shape=(
            jax.ShapeDtypeStruct((TOK, cols), bf16),
            jax.ShapeDtypeStruct((rows, classes // LANES, LANES), f32),
        ),
        in_specs=[hbm] * 9,
        out_specs=(vmem, vmem),
        scratch_shapes=[
            pltpu.SMEM(patch_counts.shape, jnp.int32),
            pltpu.SMEM(move_plan.shape, jnp.int32),
            pltpu.VMEM((1, classes), f32),
            pltpu.VMEM((1, LANES), f32),
            pltpu.VMEM((1, LANES), f32),
            pltpu.VMEM((rows, pair, WINDOW), bf16),
            pltpu.VMEM((rows, pair, 16), bf16),
            pltpu.VMEM((rows, TOK, WINDOW), bf16),
            pltpu.VMEM((rows, TOK, 16), bf16),
            pltpu.VMEM((rows, TOK, pair), bf16),
            pltpu.VMEM((rows, 2, TOK, width), bf16),
            pltpu.VMEM((3, slots, width), bf16),
            pltpu.VMEM((3, pair, width), bf16),
            pltpu.VMEM((rows * pair, width), bf16),
            pltpu.VMEM((2, rows, 3 * pair, width), bf16),
            pltpu.VMEM((rows, pair, width // 2), bf16),
            pltpu.VMEM((2, depth, cols), bf16),
            pltpu.VMEM((slots, cols), bf16),
            pltpu.VMEM((3, 16, width), bf16),
            pltpu.VMEM((16, cols), bf16),
            pltpu.VMEM((rows, pair, cols), bf16),
            pltpu.VMEM((rows, TOK, 3 * pair), bf16),
            pltpu.VMEM((rows, TOK, cols), bf16),
            pltpu.VMEM((3, TOK, cols), bf16),
            pltpu.VMEM((8, width), f32),
            pltpu.VMEM((rows, 8, width), f32),
            pltpu.VMEM((rows, 8, width), f32),
            pltpu.VMEM((rows * rows, cols), f32),
            pltpu.VMEM((2, rows * rows, cols), f32),
            pltpu.VMEM((rows * rows, cols), f32),
            pltpu.VMEM(label_weight.shape, bf16),
            pltpu.VMEM((rows, 8, classes), f32),
            pltpu.VMEM((4, 8, classes), f32),
            pltpu.VMEM((rows, classes // LANES, LANES), f32),
            pltpu.VMEM((rows, classes // LANES, LANES), f32),
            dma((9,)),
            dma((rows, 2)),
            dma((rows, 2)),
            dma((rows, 2)),
            dma((rows,)),
            dma((2, rows, 3)),
            dma((2, rows, 4)),
            dma((tiles,)),
            dma((tiles,)),
            dma((tiles,)),
            dma((tiles,)),
            dma((rows, tiles)),
            dma((rows, tiles)),
            dma((2, tiles)),
            dma((2, tiles)),
            dma((tiles,)),
            dma((tiles,)),
            dma((1,)),
            dma((rows,)),
            dma((4,)),
            dma((1,)),
            dma((2,)),
            dma((2,)),
            dma((4,)),
            dma((4,)),
            dma((rows,)),
            dma((rows,)),
        ],
        compiler_params=pltpu.CompilerParams(
            collective_id=0, has_side_effects=True, vmem_limit_bytes=VMEM_LIMIT
        ),
    )(
        keep(patch_counts),
        keep(move_plan),
        keep(label_bias[None]),
        keep(query_gain[None]),
        keep(key_gain[None]),
        jnp.transpose(qkv_home[0], (1, 0, 2)),
        resid_home[0],
        out_weight,
        label_weight,
    )
    return (mixed[None], labels.reshape(1, 1, rows * classes))


def on_device(
    qkv_home,
    resid_home,
    out_weight,
    label_weight,
    label_bias,
    query_gain,
    key_gain,
    patch_counts,
    move_plan,
    segment_ids,
):
    row_count = lax.axis_size("dp")
    if row_count == lax.axis_size("mp") == 4 and lax.axis_size("groups") == 2:
        return fused(
            qkv_home,
            resid_home,
            out_weight,
            label_weight,
            label_bias,
            query_gain,
            key_gain,
            patch_counts,
            move_plan,
        )
    my_index = lax.axis_index("dp")
    home_slots = segment_ids.shape[1]
    pair_slots = home_slots // row_count
    image_ids = lax.broadcasted_iota(jnp.int32, (row_count, row_count, row_count), 2)
    image_ends = jnp.cumsum(patch_counts, axis=1)
    starts = image_ends - patch_counts
    matches = (move_plan[:, :, None] == image_ids).astype(jnp.int32)
    image_sizes = jnp.sum(patch_counts[:, :, None] * matches, axis=1)
    firsts = jnp.sum(starts[:, :, None] * matches, axis=1)
    send_sizes = lax.dynamic_index_in_dim(image_sizes, my_index, 0, keepdims=False)
    send_firsts = lax.dynamic_index_in_dim(firsts, my_index, 0, keepdims=False)
    within = lax.broadcasted_iota(jnp.int32, (row_count, pair_slots), 1)
    send_valid = within < send_sizes[:, None]
    send_index = jnp.minimum(send_firsts[:, None] + within, home_slots - 1).reshape(-1)
    arrive_sizes = lax.dynamic_index_in_dim(image_sizes, my_index, 1, keepdims=False)
    arrive_ends = jnp.cumsum(arrive_sizes)
    arrive_starts = arrive_ends - arrive_sizes
    slot_grid = lax.broadcasted_iota(jnp.int32, (TOK, row_count), 0)
    source = jnp.sum((slot_grid >= arrive_ends[None, :]).astype(jnp.int32), axis=1)
    chosen = (source[:, None] == lax.broadcasted_iota(jnp.int32, (TOK, row_count), 1)).astype(
        jnp.int32
    )
    arrive_index = (
        source * pair_slots + slot_grid[:, 0] - jnp.sum(chosen * arrive_starts[None, :], axis=1)
    )
    home_mixed = project(
        attend(qkv_home[0], segment_ids[0], query_gain, key_gain), resid_home[0], out_weight
    )
    count_row = lax.dynamic_index_in_dim(patch_counts, my_index, 0, keepdims=False)
    pooled = pool(home_mixed, segment_ids[0], count_row)
    partial_value = label_terms(pooled, label_weight)
    send_mixed = pick(home_mixed, send_index, send_valid)
    got_mixed = lax.all_to_all(send_mixed, "dp", split_axis=0, concat_axis=0, tiled=True)
    mixed = jnp.take(got_mixed.reshape(row_count * pair_slots, -1), arrive_index, axis=0)
    logit_sums = lax.psum_scatter(
        partial_value.astype(jnp.bfloat16), "mp", scatter_dimension=1, tiled=True
    ).astype(jnp.float32)
    class_probs = jax.nn.sigmoid(logit_sums + label_bias[None, None, :])
    labels = lax.all_to_all(
        class_probs.astype(jnp.bfloat16), "dp", split_axis=0, concat_axis=2, tiled=True
    ).astype(class_probs.dtype)
    return (mixed[None], labels)


def solution(mesh):
    return jax.shard_map(
        on_device,
        mesh=mesh,
        in_specs=(
            P(("groups", "dp"), None, None, "mp"),
            P(("groups", "dp"), None, "mp"),
            P("dp", "mp"),
            P("mp", "dp"),
            P("dp"),
            P(),
            P(),
            P("groups", None),
            P("groups", None),
            P(("groups", "dp"), None),
        ),
        out_specs=(P(("groups", "dp"), None, "mp"), P(("groups", "dp"), "mp", None)),
        check_vma=False,
    )
```

```python
import functools
import math

import jax
import jax.numpy as jnp
from jax import lax
from jax.experimental import pallas as pl
from jax.experimental.pallas import tpu as pltpu
from jax.sharding import PartitionSpec as P

TOK = 384


EPSILON = 1e-06


def head_norm(values, norm_gain):
    center = values - jnp.mean(values, axis=-1, keepdims=True)
    spread = jnp.mean(center * center, axis=-1, keepdims=True)
    return center * lax.rsqrt(spread + EPSILON) * norm_gain


def attend(qkv_rows, seg_rows, query_gain, key_gain):
    length = qkv_rows.shape[0]
    head_width = query_gain.shape[0]
    head_count = qkv_rows.shape[2] // head_width
    split_parts = qkv_rows.reshape(length, 3, head_count, head_width)
    queries = head_norm(split_parts[:, 0].astype(jnp.float32), query_gain).astype(jnp.bfloat16)
    key_rows = head_norm(split_parts[:, 1].astype(jnp.float32), key_gain).astype(jnp.bfloat16)
    scores = jnp.einsum(
        "qhd,khd->hqk", queries, key_rows, preferred_element_type=jnp.float32
    ) / math.sqrt(head_width)
    same_image = seg_rows[:, None] == seg_rows[None, :]
    raised = jnp.where(same_image[None], jnp.exp(scores), 0.0)
    weights = (raised / jnp.sum(raised, axis=-1, keepdims=True)).astype(jnp.bfloat16)
    head_out = jnp.einsum(
        "hqk,khd->qhd", weights, split_parts[:, 2], preferred_element_type=jnp.float32
    )
    return head_out.reshape(length, head_count * head_width).astype(jnp.bfloat16)


def project(heads_local, resid_rows, out_weight):
    gathered = lax.all_gather(heads_local, "mp", axis=1, tiled=True)
    running = resid_rows.astype(jnp.float32) + jnp.dot(
        gathered,
        lax.all_gather(out_weight, "dp", axis=0, tiled=True),
        preferred_element_type=jnp.float32,
    )
    return running.astype(jnp.bfloat16)


def pool(row_mixed, seg_rows, count_row):
    images = count_row.shape[0]
    member_ids = lax.broadcasted_iota(jnp.int32, (images, seg_rows.shape[0]), 0)
    member = (member_ids == seg_rows[None, :]).astype(jnp.bfloat16)
    image_sums = jnp.dot(member, row_mixed, preferred_element_type=jnp.float32)
    return (image_sums / count_row[:, None].astype(jnp.float32)).astype(jnp.bfloat16)


def label_terms(pooled, label_weight):
    return jnp.einsum(
        "abd,dc->abc",
        lax.all_gather(pooled[None], "dp", axis=0, tiled=True),
        label_weight,
        preferred_element_type=jnp.float32,
    )


def pick(values, row_index, is_valid):
    taken = jnp.take(values, row_index, axis=0)
    taken = taken.reshape(is_valid.shape + values.shape[1:])
    keep_mask = is_valid.reshape(is_valid.shape + (1,) * (values.ndim - 1))
    return jnp.where(keep_mask, taken, jnp.zeros_like(taken))


MESH = pl.DeviceIdType.MESH
LANES = 128
TILE = 256
WINDOW = 256
VMEM_LIMIT = 52 * 1024 * 1024


def remote(src, dst, send_sem, recv_sem, where):
    return pltpu.make_async_remote_copy(
        src_ref=src,
        dst_ref=dst,
        send_sem=send_sem,
        recv_sem=recv_sem,
        device_id=where,
        device_id_type=MESH,
    )


def call_all(work):
    work()


def normed(values, gain):
    values = values.astype(jnp.float32)
    center = values - jnp.mean(values, axis=-1, keepdims=True)
    spread = jnp.mean(center * center, axis=-1, keepdims=True)
    return (center * lax.rsqrt(spread + EPSILON) * gain).astype(jnp.bfloat16)


def block_kernel(
    sizes,
    counts_hbm,
    plan_hbm,
    bias_hbm,
    qg_hbm,
    kg_hbm,
    qkv_hbm,
    resid_hbm,
    w_hbm,
    lw_hbm,
    out_ref,
    lab_ref,
    counts,
    plan,
    bias_ref,
    qg_ref,
    kg_ref,
    picks,
    pick_ends,
    rest_picks,
    rest_ends,
    xplaces,
    packed,
    raw,
    blk,
    hx,
    gath,
    relay,
    wall,
    resv,
    end_qkv,
    end_resid,
    xall,
    places,
    obuf,
    srecv,
    hsum,
    hrecv,
    htot,
    lpart,
    lgot,
    lpool,
    lwv,
    lgs,
    lrecv,
    pbuf,
    precv,
    load_sem,
    os,
    orr,
    cs,
    rr,
    ins,
    cr,
    wzs,
    wzr,
    wys,
    wyr,
    xs,
    xr,
    ss,
    sr,
    fs,
    fr,
    hs,
    hr,
    ts,
    tr,
    gs,
    gr,
    ls,
    lr,
    bs,
    br,
):
    rows, slots, pair = sizes
    z = lax.axis_index("dp")
    mp = lax.axis_index("mp")
    group = lax.axis_index("groups")
    other = 1 - group
    core = lax.rem(mp, 2)
    xpos = mp // 2
    near = mp + 1 - 2 * core
    side = lax.rem(mp + 2, 4)
    half_id = z // 2
    member_id = z - 2 * half_id
    zo = 3 * half_id
    zp = 1 + half_id
    zq = 2 - half_id
    zo2 = 3 - 3 * half_id
    inner = z == zp
    outer = z == zo
    partner = zo + zp - z
    keeps = xpos == half_id
    crosses = xpos != half_id
    order_a = [zo2, zq, zo, zp]
    order_c = [zo, zp, zo2, zq]
    homes = [z, zq, zo2]
    width = raw.shape[2]
    split = width // 2
    depth, cols = w_hbm.shape
    tiles = cols // TILE
    images = rows
    tokens = out_ref.shape[0]
    bf16, f32 = jnp.bfloat16, jnp.float32

    loads = [
        pltpu.make_async_copy(qkv_hbm, raw, load_sem.at[0]),
        pltpu.make_async_copy(w_hbm, wall.at[member_id], load_sem.at[1]),
        pltpu.make_async_copy(resid_hbm, resv, load_sem.at[2]),
        pltpu.make_async_copy(lw_hbm, lwv, load_sem.at[3]),
    ]
    small = [
        pltpu.make_async_copy(counts_hbm, counts, load_sem.at[4]),
        pltpu.make_async_copy(plan_hbm, plan, load_sem.at[5]),
        pltpu.make_async_copy(qg_hbm, qg_ref, load_sem.at[6]),
        pltpu.make_async_copy(kg_hbm, kg_ref, load_sem.at[7]),
        pltpu.make_async_copy(bias_hbm, bias_ref, load_sem.at[8]),
    ]
    for load in small:
        load.start()
    loads[0].start()

    barrier = pltpu.get_barrier_semaphore()
    for k in range(1, 4):
        pl.semaphore_signal(
            barrier, inc=1, device_id={"mp": lax.rem(mp + k, 4)}, device_id_type=MESH
        )
    for k in range(1, rows):
        pl.semaphore_signal(
            barrier, inc=1, device_id={"dp": lax.rem(z + k, rows)}, device_id_type=MESH
        )
    pl.semaphore_signal(barrier, inc=1, device_id={"groups": other}, device_id_type=MESH)
    pl.semaphore_wait(barrier, 3 + rows - 1 + 1)

    def tile_at(t):
        return pl.ds(pl.multiple_of(t * TILE, TILE), TILE)

    def block_at(index):
        return pl.ds(pl.multiple_of(index * pair, pair), pair)

    def repeat(count, body):
        def step(t, carry):
            body(t)
            return carry

        lax.fori_loop(0, count, step, 0)

    def weight_part(which, part, t):
        size = depth // 2
        return wall.at[which, pl.ds(pl.multiple_of(part * size, size), size), tile_at(t)]

    def wzcopy(t):
        size = depth // 2
        own = w_hbm.at[pl.ds(pl.multiple_of(group * size, size), size), tile_at(t)]
        return remote(
            own, weight_part(member_id, group, t), wzs.at[t], wzr.at[t], {"dp": partner}
        )

    def wycopy(t):
        part = weight_part(1 - member_id, group, t)
        return remote(part, part, wys.at[t], wyr.at[t], {"groups": other})

    def forward_weight(t):
        part = weight_part(1 - member_id, group, t)
        remote(part, part, wys.at[t], wzr.at[t], {"groups": other}).wait_recv()
        wycopy(t).start()

    def wait_weight(t):
        part = weight_part(1 - member_id, other, t)
        remote(part, part, wys.at[t], wyr.at[t], {"groups": other}).wait_recv()

    early = tiles // 2
    wzcopy(0).start()

    @pl.when(inner)
    def _():
        for t in range(1, early):
            wzcopy(t).start()

    loads[1].start()
    loads[2].start()

    def gathered(which, home, dest):
        return which, dest, pl.ds(pl.multiple_of(home * pair, pair), pair)

    def own_piece(which, k):
        kb, e, at = gathered(which, 0, order_a[k])
        return gath.at[kb, e, at, :]

    def own_near(k):
        part = own_piece(core, k)
        return remote(part, part, os.at[k, 0], orr.at[k, 0], {"mp": near})

    def own_side(k):
        part = own_piece(core, k)
        return remote(part, part, os.at[k, 1], orr.at[k, 1], {"mp": side})

    def own_wait(kind, k):
        part = own_piece(core if kind else 1 - core, k)
        remote(part, part, os.at[k, kind], orr.at[k, kind], {"mp": near}).wait_recv()

    def half_at(which):
        return pl.ds(pl.multiple_of(which * split, LANES), split)

    there = jnp.where(outer, 2, 1)

    def cross_low(k):
        dest = order_c[k]
        kb, e, at = gathered(core, there, dest)
        return remote(
            hx.at[block_at(dest), pl.ds(0, split)],
            gath.at[kb, e, at, pl.ds(0, split)],
            cs.at[k, 0],
            cr.at[there - 1, k, 0],
            {"dp": zq},
        )

    def cross_side(k):
        dest = order_c[k]
        return remote(
            hx.at[block_at(dest), pl.ds(split, split)],
            relay.at[k],
            cs.at[k, 1],
            rr.at[k],
            {"mp": side},
        )

    def cross_high(k):
        kb, e, at = gathered(core, there, order_c[k])
        return remote(
            relay.at[k],
            gath.at[kb, e, at, pl.ds(split, split)],
            cs.at[k, 0],
            cr.at[there - 1, k, 0],
            {"dp": zq},
        )

    mine = jnp.where(keeps, 0, 1)

    def cross_piece(h, k, which, part):
        kb, e, at = gathered(which, h + 1, order_a[k])
        return gath.at[kb, e, at, half_at(part)]

    def cross_copy(h, k, kind):
        part = cross_piece(h, k, core, 1 - mine if kind == 2 else mine)
        target = side if kind == 1 else near
        return remote(part, part, ins.at[h, k, kind], cr.at[h, k, kind + 1], {"mp": target})

    def cross_wait(h, k, kind):
        which = core if kind in (0, 2) else 1 - core
        part = cross_piece(h, k, which, mine if kind < 2 else 1 - mine)
        remote(part, part, ins.at[h, k, 0], cr.at[h, k, kind], {"mp": near}).wait_recv()

    def serve_keep(k):
        @pl.when(keeps)
        def _():
            remote(
                relay.at[k], relay.at[k], cs.at[k, 1], rr.at[k], {"mp": side}
            ).wait_recv()
            cross_high(k).start()

    def serve_cross(k):
        @pl.when(crosses)
        def _():
            own_wait(1, k)
            own_near(k).start()

    for load in small:
        load.wait()
    own_counts = [counts[z, j] for j in range(images)]
    own_plan = [plan[z, j] for j in range(images)]
    own_starts, running = [], 0
    for j in range(images):
        own_starts.append(running)
        running = running + own_counts[j]

    def span_of(dest):
        first, count = 0, 0
        for j in range(images):
            hit = (own_plan[j] == dest).astype(jnp.int32)
            first = first + hit * own_starts[j]
            count = count + hit * own_counts[j]
        return first, count

    pick_row = lax.broadcasted_iota(jnp.int32, (pair, 1), 0)
    pick_col = lax.broadcasted_iota(jnp.int32, (1, WINDOW), 1)
    base = slots // 16 * 16
    rest = slots - base

    def window(first):
        return lax.min(lax.div(first, 16), (base - WINDOW) // 16) * 16

    def picker(dest):
        first, count = span_of(dest)
        low = window(first)
        valid = pick_row < count
        chosen = jnp.logical_and(pick_col == pick_row + (first - low), valid).astype(bf16)
        ends = jnp.logical_and(pick_col[:, :16] == pick_row + (first - base), valid).astype(bf16)
        return pl.ds(low, WINDOW), chosen, ends, count

    def moved_rows(chosen, ends, body, end):
        part = jnp.dot(chosen, body, preferred_element_type=f32)
        return part + jnp.dot(ends, end, preferred_element_type=f32)

    heads = width // LANES
    q_gain = qg_ref[...]
    k_gain = kg_ref[...]
    scale = math.log2(math.e) / math.sqrt(LANES)
    key_at = lax.broadcasted_iota(jnp.int32, (1, pair), 1)

    loads[0].wait()
    end_qkv[...] = jnp.zeros(end_qkv.shape, bf16)
    if rest:
        end_qkv[:, pl.ds(0, rest), :] = raw[:, pl.ds(base, rest), :]

    def attend_block(dest):
        at_rows, chosen, ends, count = picker(dest)
        for part in range(3):
            blk[part] = moved_rows(
                chosen, ends, raw[part, at_rows, :], end_qkv[part]
            ).astype(bf16)
        picks[dest] = chosen
        pick_ends[dest] = ends
        seen = key_at < count
        real = pick_row < count
        line = own_row == dest

        for h in range(heads):
            at = pl.ds(h * LANES, LANES)
            scores = lax.dot_general(
                normed(blk[0, :, at], q_gain),
                normed(blk[1, :, at], k_gain),
                (((1,), (1,)), ((), ())),
                preferred_element_type=f32,
            )
            raised = jnp.where(seen, jnp.exp2(scores * scale), 0.0)
            total = jnp.sum(raised, axis=-1, keepdims=True)
            weights = (raised * (1.0 / total)).astype(bf16)
            result = jnp.dot(weights, blk[2, :, at], preferred_element_type=f32)
            result = result.astype(bf16)
            hx[block_at(dest), at] = result
            total = jnp.sum(jnp.where(real, result.astype(f32), 0.0), axis=0, keepdims=True)
            hsum[:, at] = jnp.where(line, total, hsum[:, at])

    group_lines = rows * rows
    sum_row = lax.broadcasted_iota(jnp.int32, (group_lines, 1), 0)
    own_row = lax.broadcasted_iota(jnp.int32, (8, 1), 0)
    wide_col = lax.broadcasted_iota(jnp.int32, (1, 8 * rows), 1)
    hsum[...] = jnp.zeros(hsum.shape, f32)

    for k in range(rows):
        dest = jnp.where(keeps, order_a[k], order_c[k])
        attend_block(dest)

        @pl.when(keeps)
        def _(k=k):
            kb, e, at = gathered(core, 0, order_a[k])
            gath[kb, e, at, :] = hx[block_at(order_a[k]), :]
            if k < 1:
                own_side(k).start()
            else:

                @pl.when(outer)
                def _():
                    own_side(k).start()

            own_near(k).start()

        @pl.when(crosses)
        def _(k=k):
            cross_side(k).start()
            if k == 0:
                cross_low(k).start()
            if k == 1:

                @pl.when(outer)
                def _():
                    cross_low(k).start()

    def cross_later(k):
        serve_keep(k)

        @pl.when(crosses)
        def _():
            cross_low(k).start()

    def own_later(k):
        @pl.when(keeps)
        def _():
            own_side(k).start()

    collects = z == mp

    def hcopy():
        return remote(hsum, hrecv.at[z], hs.at[0], hr.at[z], {"dp": mp})

    def tcopy(k):
        peer = lax.rem(mp + k, 4)
        return remote(htot, htot, ts.at[k], tr.at[0], {"mp": peer})

    @pl.when(jnp.logical_not(collects))
    def _():
        hcopy().start()

    @pl.when(inner)
    def _():
        for t in range(early, tiles):
            wzcopy(t).start()

    loads[3].start()

    def collect_sums():
        @pl.when(collects)
        def _():
            htot[z] = hsum[...]
            for k in range(1, rows):
                source = lax.rem(z + k, rows)
                part = hrecv.at[source]
                remote(part, part, hs.at[0], hr.at[source], {"dp": source}).wait_recv()
                htot[source] = hrecv[source]
            for k in range(1, 4):
                tcopy(k).start()

    def gcopy(kind):
        if kind == 0:
            return remote(lpart, lgot.at[0], gs.at[0], gr.at[0], {"dp": zp})
        if kind == 1:
            return remote(lpart, lgot.at[1], gs.at[0], gr.at[1], {"dp": zq})
        return remote(lpool, lgot.at[0], gs.at[1], gr.at[0], {"dp": zo})

    slot_at = lax.broadcasted_iota(jnp.int32, (1, slots), 1)

    def partial_sums():
        @pl.when(jnp.logical_not(collects))
        def _():
            remote(htot, htot, ts.at[1], tr.at[0], {"mp": near}).wait_recv()

        sums = htot[...].reshape(8 * rows, width)
        high = sums.astype(bf16)
        low = (sums - high.astype(f32)).astype(bf16)
        squeeze = (wide_col == sum_row // rows * 8 + lax.rem(sum_row, rows)).astype(bf16)
        high = jnp.dot(squeeze, high, preferred_element_type=f32).astype(bf16)
        low = jnp.dot(squeeze, low, preferred_element_type=f32).astype(bf16)
        owner = jnp.full(slot_at.shape, -1, jnp.int32)
        for j in range(images):
            inside = jnp.logical_and(
                slot_at >= own_starts[j], slot_at < own_starts[j] + own_counts[j]
            )
            owner = jnp.where(inside, z * rows + own_plan[j], owner)
        member = (sum_row == owner).astype(bf16)

        def sum_tile(t):
            weights = wall[member_id, :, tile_at(t)]
            part = jnp.dot(high, weights, preferred_element_type=f32)
            part = part + jnp.dot(low, weights, preferred_element_type=f32)
            part = part + jnp.dot(member, resv[:, tile_at(t)], preferred_element_type=f32)
            lpart[:, tile_at(t)] = part

        repeat(tiles, sum_tile)

    loads[2].wait()
    end_resid[...] = jnp.zeros(end_resid.shape, bf16)
    if rest:
        end_resid[pl.ds(0, rest), :] = resv[pl.ds(base, rest), :]

    place_row = lax.broadcasted_iota(jnp.int32, (tokens, 1), 0)
    place_col = lax.broadcasted_iota(jnp.int32, (1, 3 * pair), 1)

    def choose(values, index):
        total = 0
        for i, value in enumerate(values):
            total = total + (index == i).astype(jnp.int32) * value
        return total

    def spans_to(dest):
        begins, sizes, begin = [], [], 0
        for r in range(rows):
            count = 0
            for j in range(images):
                count = count + (plan[r, j] == dest).astype(jnp.int32) * counts[r, j]
            begins.append(begin)
            sizes.append(count)
            begin = begin + count
        return begins, sizes

    def build_cross(k):
        begins, sizes = spans_to(order_a[k])
        at = place_col[:, :pair]
        target = jnp.where(at < choose(sizes, zo), at + choose(begins, zo), -1)
        xplaces[k] = (place_row == target).astype(bf16)

    def build_place(k):
        dest = order_a[k]
        begins, sizes = spans_to(dest)
        target = jnp.full(place_col.shape, -1, jnp.int32)
        for h in range(3):
            at = place_col - h * pair
            inside = jnp.logical_and(at >= 0, at < choose(sizes, homes[h]))
            target = jnp.where(inside, at + choose(begins, homes[h]), target)
        places[k] = (place_row == target).astype(bf16)
        first, count = span_of(dest)
        begin = choose(begins, z)
        for ref, low, columns in (
            (rest_picks, window(first), pick_col),
            (rest_ends, base, pick_col[:, :16]),
        ):
            at = columns + (low - first)
            inside = jnp.logical_and(at >= 0, at < count)
            ref[k] = (place_row == jnp.where(inside, at + begin, -1)).astype(bf16)

    loads[1].wait()

    def project(dest, t):
        at_rows = pl.ds(window(span_of(dest)[0]), WINDOW)
        used = pl.ds(0, pair)
        term = jnp.dot(gath[0, dest, used, :], wall[0, :, tile_at(t)], preferred_element_type=f32)
        term = term + jnp.dot(
            gath[1, dest, used, :], wall[1, :, tile_at(t)], preferred_element_type=f32
        )
        term = term + moved_rows(
            picks[dest], pick_ends[dest], resv[at_rows, tile_at(t)], end_resid[:, tile_at(t)]
        )
        xall[dest, :, tile_at(t)] = term.astype(bf16)

    def dest_of(k):
        if isinstance(k, int):
            return order_a[k]
        low = jnp.where(k == 0, order_a[0], order_a[1])
        return jnp.where(k < 2, low, jnp.where(k == 2, order_a[2], order_a[3]))

    def compact(k):
        dest = order_a[k]
        for which in range(2):

            def pack_tile(t, which=which):
                part = jnp.dot(
                    places[k], gath[which, dest, :, tile_at(t)], preferred_element_type=f32
                )
                packed[k, which, :, tile_at(t)] = part.astype(bf16)

            repeat(width // TILE, pack_tile)

    def xcopy(k, t):
        dest = dest_of(k)
        part = xall.at[dest, :, tile_at(t)]
        return remote(part, part, xs.at[k, t], xr.at[k, t], {"dp": zp})

    def xwait(k, t):
        dest = dest_of(k)
        part = xall.at[dest, :, tile_at(t)]
        remote(part, part, xs.at[k, t], xr.at[k, t], {"dp": zo}).wait_recv()

    def scopy(k, t):
        return remote(
            obuf.at[k, :, tile_at(t)],
            srecv.at[k, :, tile_at(t)],
            ss.at[k, t],
            sr.at[k, t],
            {"dp": zq},
        )

    def fcopy(t):
        return remote(
            obuf.at[2, :, tile_at(t)], srecv.at[0, :, tile_at(t)], fs.at[t], fr.at[t], {"dp": zo}
        )

    def ppeer(k):
        return lax.rem(z + k, rows)

    group_rows = lgs.shape[1]
    lines = images * group_rows
    classes = lwv.shape[1]

    def label_logits(source):
        loads[3].wait()
        line = lax.broadcasted_iota(jnp.int32, (lines, 1), 0)
        wanted = jnp.full((lines, 1), -1, jnp.int32)
        divisor = jnp.ones((group_lines, 1), f32)
        for r in range(rows):
            for j in range(images):
                row = r * rows + plan[r, j]
                wanted = jnp.where(line == j * group_rows + r, row, wanted)
                divisor = jnp.where(sum_row == row, counts[r, j].astype(f32), divisor)
        columns = lax.broadcasted_iota(jnp.int32, (lines, group_lines), 1)
        order = (columns == wanted).astype(bf16)
        pooled = (source[...] / divisor).astype(bf16)
        by_image = jnp.dot(order, pooled, preferred_element_type=f32).astype(bf16)

        def label_tile(t):
            part = jnp.dot(by_image, lwv[:, tile_at(t)], preferred_element_type=f32)
            for j in range(images):
                lgs[j, :, tile_at(t)] = part[j * group_rows : (j + 1) * group_rows]

        repeat(classes // TILE, label_tile)
        for k in range(1, 4):
            lcopy(k).start()

    def lcopy(k):
        peer = lax.rem(mp + k, 4)
        return remote(lgs.at[peer], lrecv.at[k], ls.at[k], lr.at[k], {"mp": peer})

    def bcopy(k):
        peer = ppeer(k)
        return remote(pbuf.at[peer], precv.at[z], bs.at[k], br.at[k], {"dp": peer})

    def label_probs():
        for k in range(1, 4):
            lcopy(k).wait_recv()
        total = lgs[mp]
        for k in range(1, 4):
            total = total + lrecv[k]
        probs = jax.nn.sigmoid(total + bias_ref[...])
        for r in range(rows):
            for t in range(classes // LANES):
                pbuf[r, pl.ds(t, 1), :] = probs[r : r + 1, t * LANES : (t + 1) * LANES]
        for k in range(1, rows):
            bcopy(k).start()

    @pl.when(outer)
    def _():
        serve_keep(0)
        wzcopy(1).start()
        forward_weight(0)
        serve_cross(0)
        serve_keep(1)
        forward_weight(1)
        build_cross(2)
        own_wait(0, 0)
        lag = 2

        def send_sums():
            partial_sums()
            gcopy(0).start()

        after = {
            0: lambda: (serve_cross(1), own_wait(0, 1)),
            1: lambda: (cross_later(2), serve_cross(2), collect_sums()),
            2: lambda: (send_sums(), serve_cross(3)),
            4: lambda: cross_later(3),
        }

        def near_piece(t):
            project(order_a[1], t)
            xcopy(1, t).start()

        def first_tile(t):
            wait_weight(t)
            project(order_a[0], t)
            xcopy(0, t).start()

            @pl.when(t + 2 < tiles)
            def _():
                wzcopy(t + 2).start()

            @pl.when(t >= lag)
            def _():
                near_piece(t - lag)

            @pl.when(t + 2 < tiles)
            def _():
                forward_weight(t + 2)

            for step, work in after.items():
                pl.when(t == step)(functools.partial(call_all, work))

        repeat(tiles, first_tile)
        repeat(lag, lambda t: near_piece(t + tiles - lag))
        own_wait(0, 3)

        def third_tile(t):
            project(order_a[3], t)
            xcopy(3, t).start()

        repeat(tiles, third_tile)
        own_wait(0, 2)

        gcopy(2).wait_recv()
        label_logits(lgot.at[0])
        label_probs()

        def last_tile(t):
            project(order_a[2], t)
            moved = jnp.dot(xplaces[2], xall[zo, :, tile_at(t)], preferred_element_type=f32)
            fcopy(t).wait_recv()
            value = moved + srecv[0, :, tile_at(t)].astype(f32)
            out_ref[:, tile_at(t)] = value.astype(bf16)

        repeat(tiles, last_tile)

    @pl.when(inner)
    def _():
        def arrive(k):
            for h in range(2):
                cross_wait(h, k, 0)
                cross_copy(h, k, 1).start()
                cross_copy(h, k, 0).start()

        def spread(k):
            for h in range(2):
                cross_wait(h, k, 2)
                cross_copy(h, k, 2).start()

        def settle(k):
            own_wait(0, k)
            for h in range(2):
                cross_wait(h, k, 1)
                cross_wait(h, k, 3)

        forward_weight(0)
        serve_keep(0)
        serve_cross(0)
        arrive(0)
        own_later(1)
        cross_later(1)
        cross_later(2)
        cross_later(3)
        xall[zo] = jnp.zeros((pair, cols), bf16)
        srecv[2] = jnp.zeros((tokens, cols), bf16)
        for k in range(rows):
            build_place(k)
            build_cross(k)
        forward_weight(1)
        spread(0)
        settle(0)
        compact(0)

        def add_sums():
            gcopy(0).wait_recv()
            lpart[...] += lgot[0]
            gcopy(1).start()

        def total_sums():
            gcopy(1).wait_recv()
            lpool[...] = lpart[...] + lgot[1]
            gcopy(2).start()

        plan_of = [(0, 0), (0, 1), (0, 2), (1, 0), (0, 3), (1, 1), (2, 0), (0, 4), (1, 2)]
        plan_of += [(2, 1), (0, 5), (1, 3), (2, 2), (1, 4), (2, 3), (1, 5), (2, 4), (2, 5)]
        plan_of += [(3, t) for t in range(tiles)]

        after = {
            0: lambda: (arrive(1), serve_cross(1), forward_weight(2), collect_sums()),
            1: lambda: (own_later(2), spread(1), forward_weight(3)),
            2: lambda: (settle(1), compact(1), arrive(2), own_later(3), partial_sums(), forward_weight(4)),
            3: lambda: (serve_cross(2), add_sums()),
            4: lambda: (spread(2), forward_weight(5)),
            5: lambda: (settle(2), compact(2)),
            8: lambda: (total_sums(), label_logits(lpool)),
            11: label_probs,
            13: lambda: (arrive(3), serve_cross(3)),
            17: lambda: (spread(3), settle(3), compact(3)),
        }

        def step_tile(u):
            k, t = 0, 0
            for i, (k_i, t_i) in enumerate(plan_of):
                here = (u == i).astype(jnp.int32)
                k = k + k_i * here
                t = t + t_i * here

            @pl.when(k == 0)
            def _():
                wait_weight(t)

            @pl.when(k != 2)
            def _():
                xwait(k, t)

            @pl.when(k >= 2)
            def _():
                scopy(k - 2, t).wait_recv()

            dest = dest_of(k)
            at_rows = pl.ds(window(span_of(dest)[0]), WINDOW)
            value = jnp.dot(packed[k, 0], wall[0, :, tile_at(t)], preferred_element_type=f32)
            value = value + jnp.dot(
                packed[k, 1], wall[1, :, tile_at(t)], preferred_element_type=f32
            )
            value = value + jnp.dot(
                rest_picks[k], resv[at_rows, tile_at(t)], preferred_element_type=f32
            )
            value = value + jnp.dot(
                rest_ends[k], end_resid[:, tile_at(t)], preferred_element_type=f32
            )
            value = value + jnp.dot(
                xplaces[k], xall[dest, :, tile_at(t)], preferred_element_type=f32
            )
            got = jnp.where(k < 2, 2, k - 2)
            value = value + srecv[got, :, tile_at(t)].astype(f32)
            obuf[k, :, tile_at(t)] = value.astype(bf16)

            @pl.when(k < 2)
            def _():
                scopy(k, t).start()

            @pl.when(k == 2)
            def _():
                fcopy(t).start()

            @pl.when(k == 3)
            def _():
                out_ref[:, tile_at(t)] = obuf[3, :, tile_at(t)]

            for step, work in after.items():
                pl.when(u == step)(functools.partial(call_all, work))

        repeat(len(plan_of), step_tile)

    for k in range(1, rows):
        part = precv.at[lax.rem(z + rows - k, rows)]
        remote(part, part, bs.at[k], br.at[k], {"dp": ppeer(k)}).wait_recv()
    precv[z] = pbuf[z]
    lab_ref[...] = precv[...]

    for k in range(rows):
        own_near(k).wait_send()

        @pl.when(keeps)
        def _(k=k):
            own_side(k).wait_send()
            cross_high(k).wait_send()

        @pl.when(crosses)
        def _(k=k):
            cross_low(k).wait_send()
            cross_side(k).wait_send()

        @pl.when(inner)
        def _(k=k):
            for h in range(2):
                for kind in range(3):
                    cross_copy(h, k, kind).wait_send()

    def close_tile(t):
        wzcopy(t).wait_send()
        wycopy(t).wait_send()

        @pl.when(outer)
        def _():
            for k in (0, 1, 3):
                xcopy(k, t).wait_send()

        @pl.when(inner)
        def _():
            for k in range(2):
                scopy(k, t).wait_send()
            fcopy(t).wait_send()

    repeat(tiles, close_tile)

    @pl.when(outer)
    def _():
        gcopy(0).wait_send()

    @pl.when(inner)
    def _():
        gcopy(1).wait_send()
        gcopy(2).wait_send()

    @pl.when(collects)
    def _():
        for k in range(1, 4):
            tcopy(k).wait_send()

    @pl.when(jnp.logical_not(collects))
    def _():
        hcopy().wait_send()

    for k in range(1, rows):
        bcopy(k).wait_send()
    for k in range(1, 4):
        lcopy(k).wait_send()


def round_up(value, step):
    return -(-value // step) * step


def fused(
    qkv_home,
    resid_home,
    out_weight,
    label_weight,
    label_bias,
    query_gain,
    key_gain,
    patch_counts,
    move_plan,
):
    rows = lax.axis_size("dp")
    slots, width = qkv_home.shape[1], qkv_home.shape[3]
    depth, cols = out_weight.shape
    classes = label_weight.shape[1]
    pair = round_up(slots // rows, 16)
    tiles = cols // TILE
    bf16, f32 = jnp.bfloat16, jnp.float32
    vmem = pl.BlockSpec(memory_space=pltpu.VMEM)
    hbm = pl.BlockSpec(memory_space=pltpu.HBM)
    dma = pltpu.SemaphoreType.DMA

    def keep(value):
        return pltpu.with_memory_space_constraint(value, pltpu.HBM)

    mixed, labels = pl.pallas_call(
        functools.partial(block_kernel, (rows, slots, pair)),
        out_shape=(
            jax.ShapeDtypeStruct((TOK, cols), bf16),
            jax.ShapeDtypeStruct((rows, classes // LANES, LANES), f32),
        ),
        in_specs=[hbm] * 9,
        out_specs=(vmem, vmem),
        scratch_shapes=[
            pltpu.SMEM(patch_counts.shape, jnp.int32),
            pltpu.SMEM(move_plan.shape, jnp.int32),
            pltpu.VMEM((1, classes), f32),
            pltpu.VMEM((1, LANES), f32),
            pltpu.VMEM((1, LANES), f32),
            pltpu.VMEM((rows, pair, WINDOW), bf16),
            pltpu.VMEM((rows, pair, 16), bf16),
            pltpu.VMEM((rows, TOK, WINDOW), bf16),
            pltpu.VMEM((rows, TOK, 16), bf16),
            pltpu.VMEM((rows, TOK, pair), bf16),
            pltpu.VMEM((rows, 2, TOK, width), bf16),
            pltpu.VMEM((3, slots, width), bf16),
            pltpu.VMEM((3, pair, width), bf16),
            pltpu.VMEM((rows * pair, width), bf16),
            pltpu.VMEM((2, rows, 3 * pair, width), bf16),
            pltpu.VMEM((rows, pair, width // 2), bf16),
            pltpu.VMEM((2, depth, cols), bf16),
            pltpu.VMEM((slots, cols), bf16),
            pltpu.VMEM((3, 16, width), bf16),
            pltpu.VMEM((16, cols), bf16),
            pltpu.VMEM((rows, pair, cols), bf16),
            pltpu.VMEM((rows, TOK, 3 * pair), bf16),
            pltpu.VMEM((rows, TOK, cols), bf16),
            pltpu.VMEM((3, TOK, cols), bf16),
            pltpu.VMEM((8, width), f32),
            pltpu.VMEM((rows, 8, width), f32),
            pltpu.VMEM((rows, 8, width), f32),
            pltpu.VMEM((rows * rows, cols), f32),
            pltpu.VMEM((2, rows * rows, cols), f32),
            pltpu.VMEM((rows * rows, cols), f32),
            pltpu.VMEM(label_weight.shape, bf16),
            pltpu.VMEM((rows, 8, classes), f32),
            pltpu.VMEM((4, 8, classes), f32),
            pltpu.VMEM((rows, classes // LANES, LANES), f32),
            pltpu.VMEM((rows, classes // LANES, LANES), f32),
            dma((9,)),
            dma((rows, 2)),
            dma((rows, 2)),
            dma((rows, 2)),
            dma((rows,)),
            dma((2, rows, 3)),
            dma((2, rows, 4)),
            dma((tiles,)),
            dma((tiles,)),
            dma((tiles,)),
            dma((tiles,)),
            dma((rows, tiles)),
            dma((rows, tiles)),
            dma((2, tiles)),
            dma((2, tiles)),
            dma((tiles,)),
            dma((tiles,)),
            dma((1,)),
            dma((rows,)),
            dma((4,)),
            dma((1,)),
            dma((2,)),
            dma((2,)),
            dma((4,)),
            dma((4,)),
            dma((rows,)),
            dma((rows,)),
        ],
        compiler_params=pltpu.CompilerParams(
            collective_id=0, has_side_effects=True, vmem_limit_bytes=VMEM_LIMIT
        ),
    )(
        keep(patch_counts),
        keep(move_plan),
        keep(label_bias[None]),
        keep(query_gain[None]),
        keep(key_gain[None]),
        jnp.transpose(qkv_home[0], (1, 0, 2)),
        resid_home[0],
        out_weight,
        label_weight,
    )
    return (mixed[None], labels.reshape(1, 1, rows * classes))


def on_device(
    qkv_home,
    resid_home,
    out_weight,
    label_weight,
    label_bias,
    query_gain,
    key_gain,
    patch_counts,
    move_plan,
    segment_ids,
):
    row_count = lax.axis_size("dp")
    if row_count == lax.axis_size("mp") == 4 and lax.axis_size("groups") == 2:
        return fused(
            qkv_home,
            resid_home,
            out_weight,
            label_weight,
            label_bias,
            query_gain,
            key_gain,
            patch_counts,
            move_plan,
        )
    my_index = lax.axis_index("dp")
    home_slots = segment_ids.shape[1]
    pair_slots = home_slots // row_count
    image_ids = lax.broadcasted_iota(jnp.int32, (row_count, row_count, row_count), 2)
    image_ends = jnp.cumsum(patch_counts, axis=1)
    starts = image_ends - patch_counts
    matches = (move_plan[:, :, None] == image_ids).astype(jnp.int32)
    image_sizes = jnp.sum(patch_counts[:, :, None] * matches, axis=1)
    firsts = jnp.sum(starts[:, :, None] * matches, axis=1)
    send_sizes = lax.dynamic_index_in_dim(image_sizes, my_index, 0, keepdims=False)
    send_firsts = lax.dynamic_index_in_dim(firsts, my_index, 0, keepdims=False)
    within = lax.broadcasted_iota(jnp.int32, (row_count, pair_slots), 1)
    send_valid = within < send_sizes[:, None]
    send_index = jnp.minimum(send_firsts[:, None] + within, home_slots - 1).reshape(-1)
    arrive_sizes = lax.dynamic_index_in_dim(image_sizes, my_index, 1, keepdims=False)
    arrive_ends = jnp.cumsum(arrive_sizes)
    arrive_starts = arrive_ends - arrive_sizes
    slot_grid = lax.broadcasted_iota(jnp.int32, (TOK, row_count), 0)
    source = jnp.sum((slot_grid >= arrive_ends[None, :]).astype(jnp.int32), axis=1)
    chosen = (source[:, None] == lax.broadcasted_iota(jnp.int32, (TOK, row_count), 1)).astype(
        jnp.int32
    )
    arrive_index = (
        source * pair_slots + slot_grid[:, 0] - jnp.sum(chosen * arrive_starts[None, :], axis=1)
    )
    home_mixed = project(
        attend(qkv_home[0], segment_ids[0], query_gain, key_gain), resid_home[0], out_weight
    )
    count_row = lax.dynamic_index_in_dim(patch_counts, my_index, 0, keepdims=False)
    pooled = pool(home_mixed, segment_ids[0], count_row)
    partial_value = label_terms(pooled, label_weight)
    send_mixed = pick(home_mixed, send_index, send_valid)
    got_mixed = lax.all_to_all(send_mixed, "dp", split_axis=0, concat_axis=0, tiled=True)
    mixed = jnp.take(got_mixed.reshape(row_count * pair_slots, -1), arrive_index, axis=0)
    logit_sums = lax.psum_scatter(
        partial_value.astype(jnp.bfloat16), "mp", scatter_dimension=1, tiled=True
    ).astype(jnp.float32)
    class_probs = jax.nn.sigmoid(logit_sums + label_bias[None, None, :])
    labels = lax.all_to_all(
        class_probs.astype(jnp.bfloat16), "dp", split_axis=0, concat_axis=2, tiled=True
    ).astype(class_probs.dtype)
    return (mixed[None], labels)


def solution(mesh):
    return jax.shard_map(
        on_device,
        mesh=mesh,
        in_specs=(
            P(("groups", "dp"), None, None, "mp"),
            P(("groups", "dp"), None, "mp"),
            P("dp", "mp"),
            P("mp", "dp"),
            P("dp"),
            P(),
            P(),
            P("groups", None),
            P("groups", None),
            P(("groups", "dp"), None),
        ),
        out_specs=(P(("groups", "dp"), None, "mp"), P(("groups", "dp"), "mp", None)),
        check_vma=False,
    )
```
